32 devices in a mesh: section: 2 (over core), dp: 4 (over z), tensor: 4 (over y, x).
Axes of the slice: x: 2, y: 2, z: 4, core: 2. Of those that a mesh axis runs over, the one named last changes fastest.
Arguments:
- boundary: bfloat16 [2, 8, 1024, 1024], P('section', 'dp', 'tensor'), may hold values from -6 to 6
- seg_ids: int32 [8, 1024], P('dp'), may hold values from 0 to 3, never falling along the last dimension, each value on 1 to 512 neighbouring positions
- ln1_gain: bfloat16 [2, 1024], P('section'), may hold values from 0.5 to 1.5
- ln1_bias: bfloat16 [2, 1024], P('section'), may hold values from -3 to 3
- w_qkv: bfloat16 [2, 1024, 16, 192], P('section', None, 'tensor'), may hold values from -0.1875 to 0.1875
- b_qkv: bfloat16 [2, 16, 192], P('section', 'tensor'), may hold values from -4 to 4
- w_out: bfloat16 [2, 16, 64, 1024], P('section', 'tensor'), may hold values from -1.5 to 1.5
- b_out: bfloat16 [2, 1024], P('section'), may hold values from -4 to 4
- ln2_gain: bfloat16 [2, 1024], P('section'), may hold values from 0.5 to 1.5
- ln2_bias: bfloat16 [2, 1024], P('section'), may hold values from -3 to 3
- w_up: bfloat16 [2, 1024, 4096], P('section', None, 'tensor'), may hold values from -0.1875 to 0.1875
- b_up: bfloat16 [2, 4096], P('section', 'tensor'), may hold values from -4 to 4
- w_down: bfloat16 [2, 4096, 1024], P('section', 'tensor'), may hold values from -0.09375 to 0.09375
- b_down: bfloat16 [2, 1024], P('section'), may hold values from -4 to 4
- prefix_embed: bfloat16 [10, 1024], replicated, may hold values from -6 to 6
- reparam_w1: bfloat16 [1024, 512], replicated, may hold values from -0.1875 to 0.1875
- reparam_b1: bfloat16 [512], replicated, may hold values from -4 to 4
- reparam_w2: bfloat16 [512, 2, 16, 128], P(None, 'section', 'tensor'), may hold values from -0.375 to 0.375
- reparam_b2: bfloat16 [2, 16, 128], P('section', 'tensor'), may hold values from -4 to 4
Outputs:
- boundary_out: bfloat16 [2, 8, 1024, 1024], P('section', 'dp', 'tensor')
- embed_grad: float32 [10, 1024], replicated
- w1_grad: float32 [1024, 512], replicated
- b1_grad: float32 [512], replicated
- w2_grad: float32 [512, 2, 16, 128], P(None, 'section', 'tensor')
- b2_grad: float32 [2, 16, 128], P('section', 'tensor')
The draws below stay inside these ranges and needn't reach their ends.
All inputs are finite; a program needn't handle non-finite values.
Results may differ from the reference program's by a relative error of at most 0.02.
Values may be sent and summed in bfloat16 or wider, within the bound.
No kernel may reach another device: no remote copies, remote signals or barrier semaphores. Data moves between devices by JAX's collectives and lax.ppermute only.
A program may use at most 192 MiB of HBM per device.

```python
import math
import jax
import jax.numpy as jnp
import numpy as np
from jax import lax

D = 1024
HEADS = 16
HEAD_DIM = 64
FF = 4096
PREFIX = 10
RHID = 512
LAYERS = 2
SEQ = 1024
ROWS = 8


def raised(entries, own_key, source, target, parts, factor):
    owner, partner = [(jnp.arange(entries.shape[position]) // (entries.shape[position] // parts)).reshape([-1 if axis == position else 1 for axis in range(entries.ndim)]) for position in (source, target)]
    chosen = jax.random.permutation(own_key, parts)[partner]
    strong = (owner == chosen) | (owner == (partner + parts // 2) % parts)
    return jnp.where(strong, factor * entries, entries)


def level_of(stream_key, extent, split, smallest, top_value):
    def one(axis_at, blocks):
        steps = jax.random.uniform(jax.random.fold_in(jax.random.fold_in(stream_key, 6), axis_at), (blocks,), jnp.float32, smallest / len(split), top_value / len(split))
        return jnp.repeat(jnp.exp(steps), extent[axis_at] // blocks).reshape((-1,) + (1,) * (len(extent) - axis_at - 1))

    gain = one(*split[0])
    for cut in split[1:]:
        gain = gain * one(*cut)
    return gain


def split_up(count, total, limit, lean):
    weights = [(1 << 20) // math.isqrt(rank ** lean) + 1 for rank in range(2, count + 1)]
    surplus, counts = total - limit - (count - 1), [1] * (count - 1)
    while surplus > 0:
        candidates = [i for i in range(count - 1) if counts[i] < limit]
        mass, budget = sum([weights[i] for i in candidates]), surplus
        for i in candidates:
            extra = min(limit - counts[i], max(1, budget * weights[i] // mass), surplus)
            counts[i] = counts[i] + extra
            surplus = surplus - extra
    return np.array([limit] + counts)


def uneven(key, amount, total, bound, lean):
    if amount == 2:
        one = jax.random.randint(key, (), max(1, total - bound), min(bound, total - 1) + 1)
        return jnp.stack([one, total - one])
    lengths = jnp.asarray(split_up(amount, total, bound, lean), jnp.int32)
    pairs = (amount - 1) // 2
    source_of, sink = lengths[1:1 + 2 * pairs:2], lengths[2:2 + 2 * pairs:2]
    slack = jnp.minimum(source_of - 1, bound - sink)
    moved = jax.random.randint(jax.random.fold_in(key, 1), (pairs,), 0, 1 << 20) % (slack + 1)
    lengths = lengths.at[1:1 + 2 * pairs:2].set(source_of - moved).at[2:2 + 2 * pairs:2].set(sink + moved)
    return lengths[jax.random.permutation(jax.random.fold_in(key, 2), amount)]


def normal_values(stream_key, shape, scale, limit, pieces=(), kind=jnp.bfloat16):
    result = scale * jax.random.normal(stream_key, shape, jnp.float32)
    if pieces:
        result = result * level_of(stream_key, shape, pieces, -0.22, 0.18)
    return jnp.clip(result, -limit, limit).astype(kind)


def bell_draw_with(own_key, extent, width, limit, pieces, heavy, held_as=jnp.bfloat16):
    entries = width * jax.random.normal(own_key, extent, jnp.float32)
    if pieces:
        entries = entries * level_of(own_key, extent, pieces, -0.22, 0.18)
    return jnp.clip(raised(entries, jax.random.fold_in(own_key, 3), *heavy), -limit, limit).astype(held_as)


def setup_inputs(seed: int = 0) -> dict:
    seeds = jax.random.split(jax.random.key(seed), 20)
    return {
        "boundary": normal_values(seeds[0], (LAYERS, ROWS, SEQ, D), 1.0, 6.0, ((0, 2), (1, 4), (2, 4))),
        "seg_ids": jax.vmap(lambda own: jnp.searchsorted(jnp.cumsum(uneven(own, 4, SEQ, SEQ // 2, 2)), jnp.arange(SEQ), side="right"))(jax.random.split(seeds[1], ROWS)).reshape((ROWS, SEQ)).astype(jnp.int32),
        "ln1_gain": jnp.clip(1.0 + 0.1 * jax.random.normal(seeds[2], (LAYERS, D), jnp.float32), 0.5, 1.5).astype(jnp.bfloat16),
        "ln1_bias": normal_values(seeds[3], (LAYERS, D), 0.2, 3.0, ((0, 2),)),
        "w_qkv": normal_values(seeds[4], (LAYERS, D, HEADS, 3 * HEAD_DIM), D ** -0.5, 0.1875, ((0, 2), (2, 4))),
        "b_qkv": normal_values(seeds[5], (LAYERS, HEADS, 3 * HEAD_DIM), 0.3, 4.0, ((0, 2), (1, 4))),
        "w_out": normal_values(seeds[6], (LAYERS, HEADS, HEAD_DIM, D), (D // 64) ** -0.5, 1.5, ((0, 2), (1, 4))),
        "b_out": normal_values(seeds[7], (LAYERS, D), 0.3, 4.0, ((0, 2),)),
        "ln2_gain": jnp.clip(1.0 + 0.1 * jax.random.normal(seeds[8], (LAYERS, D), jnp.float32), 0.5, 1.5).astype(jnp.bfloat16),
        "ln2_bias": normal_values(seeds[9], (LAYERS, D), 0.2, 3.0, ((0, 2),)),
        "w_up": normal_values(seeds[10], (LAYERS, D, FF), D ** -0.5, 0.1875, ((0, 2), (2, 4))),
        "b_up": normal_values(seeds[11], (LAYERS, FF), 0.3, 4.0, ((0, 2), (1, 4))),
        "w_down": normal_values(seeds[12], (LAYERS, FF, D), FF ** -0.5, 0.09375, ((0, 2), (1, 4))),
        "b_down": normal_values(seeds[13], (LAYERS, D), 0.3, 4.0, ((0, 2),)),
        "prefix_embed": normal_values(seeds[14], (PREFIX, D), 1.0, 6.0),
        "reparam_w1": normal_values(seeds[15], (D, RHID), D ** -0.5, 0.1875),
        "reparam_b1": normal_values(seeds[16], (RHID,), 0.3, 4.0),
        "reparam_w2": bell_draw_with(seeds[17], (RHID, LAYERS, HEADS, 2 * HEAD_DIM), RHID ** -0.5, 0.375, ((1, 2), (2, 4)), (2, 0, 4, 2.0)),
        "reparam_b2": normal_values(seeds[18], (LAYERS, HEADS, 2 * HEAD_DIM), 0.3, 4.0, ((0, 2), (1, 4))),
    }


@jax.custom_vjp
def low(v):
    return lax.optimization_barrier(v.astype(jnp.bfloat16)).astype(jnp.float32)

@jax.custom_vjp
def low_back(v):
    return v

def low_keep(v):
    return (low(v), None)

def low_pass(kept, grad):
    return (grad,)

def back_keep(v):
    return (v, None)

def back_low(kept, grad):
    return (low(grad),)
low.defvjp(low_keep, low_pass)
low_back.defvjp(back_keep, back_low)
epsilon = 1e-05
masked_value = -1e+30
highest = lax.Precision.HIGHEST

def layer_norm(values, ln_gain, ln_bias):
    row_mean = lax.optimization_barrier(jnp.mean(values, axis=-1, keepdims=True))
    centered = values - row_mean
    row_var = lax.optimization_barrier(jnp.mean(centered * centered, axis=-1, keepdims=True))
    return centered * lax.rsqrt(row_var + epsilon) * ln_gain + ln_bias

def row_layer(residual_in, seg_row, layer_index, frozen, prefix_pairs):
    ln1_gain, ln1_bias, w_qkv, b_qkv, w_out, b_out, ln2_gain, ln2_bias, w_up, b_up, w_down, b_down = frozen
    normed = low(layer_norm(residual_in, ln1_gain[layer_index], ln1_bias[layer_index]))
    packed = jnp.dot(normed, w_qkv[layer_index].reshape(D, HEADS * 3 * HEAD_DIM), precision=highest, preferred_element_type=jnp.float32)
    packed = packed + b_qkv[layer_index].reshape(HEADS * 3 * HEAD_DIM)
    packed = low_back(low(packed)).reshape(SEQ, HEADS, 3, HEAD_DIM)
    queries = packed[:, :, 0]
    key_rows = packed[:, :, 1]
    value_rows = packed[:, :, 2]
    prefix_keys = prefix_pairs[:, layer_index, :, 0]
    prefix_values = prefix_pairs[:, layer_index, :, 1]
    scaling = HEAD_DIM ** (-0.5)
    main_scores = jnp.einsum('qhd,khd->hqk', queries, key_rows, precision=highest) * scaling
    prefix_scores = jnp.einsum('qhd,phd->hqp', queries, prefix_keys, precision=highest) * scaling
    scores = low_back(jnp.concatenate([prefix_scores, main_scores], axis=2))
    positions = jnp.arange(SEQ)
    allowed = (seg_row[:, None] == seg_row[None, :]) & (positions[None, :] <= positions[:, None])
    allowed = jnp.concatenate([jnp.ones((SEQ, PREFIX), dtype=bool), allowed], axis=1)
    scores = jnp.where(allowed[None], scores, masked_value)
    probabilities = low(jax.nn.softmax(scores, axis=-1))
    all_values = jnp.concatenate([prefix_values, value_rows], axis=0)
    context = jnp.einsum('hqk,khd->qhd', probabilities, all_values, precision=highest)
    context = low_back(low(context)).reshape(SEQ, HEADS * HEAD_DIM)
    attn_branch = jnp.dot(context, w_out[layer_index].reshape(HEADS * HEAD_DIM, D), precision=highest, preferred_element_type=jnp.float32) + b_out[layer_index]
    middle = residual_in + low_back(attn_branch)
    normed_two = low(layer_norm(middle, ln2_gain[layer_index], ln2_bias[layer_index]))
    hidden_pre = low_back(jnp.dot(normed_two, w_up[layer_index], precision=highest, preferred_element_type=jnp.float32) + b_up[layer_index])
    hidden = low(jax.nn.gelu(hidden_pre, approximate=True))
    ffn_branch = jnp.dot(hidden, w_down[layer_index], precision=highest, preferred_element_type=jnp.float32) + b_down[layer_index]
    return middle + low_back(ffn_branch)

def reference(boundary, seg_ids, ln1_gain, ln1_bias, w_qkv, b_qkv, w_out, b_out, ln2_gain, ln2_bias, w_up, b_up, w_down, b_down, prefix_embed, reparam_w1, reparam_b1, reparam_w2, reparam_b2):
    frozen = (ln1_gain.astype(jnp.float32), ln1_bias.astype(jnp.float32), w_qkv.astype(jnp.float32), b_qkv.astype(jnp.float32), w_out.astype(jnp.float32), b_out.astype(jnp.float32), ln2_gain.astype(jnp.float32), ln2_bias.astype(jnp.float32), w_up.astype(jnp.float32), b_up.astype(jnp.float32), w_down.astype(jnp.float32), b_down.astype(jnp.float32))
    layer_input = boundary[0].astype(jnp.float32)
    cotangent = boundary[1].astype(jnp.float32)

    def forward(inputs_all, embed_rows, weight_one, bias_one, weight_two, bias_two):
        prefix_pre = low_back(jnp.dot(embed_rows, weight_one, precision=highest, preferred_element_type=jnp.float32) + bias_one)
        prefix_hidden = low(jnp.tanh(prefix_pre))
        prefix_flat = jnp.dot(prefix_hidden, weight_two.reshape(RHID, LAYERS * HEADS * 2 * HEAD_DIM), precision=highest, preferred_element_type=jnp.float32)
        prefix_flat = prefix_flat + bias_two.reshape(LAYERS * HEADS * 2 * HEAD_DIM)
        prefix_pairs = low_back(low(prefix_flat)).reshape(PREFIX, LAYERS, HEADS, 2, HEAD_DIM)

        def one_row(residual_in, seg_row):
            current = residual_in
            for layer_index in range(LAYERS):
                if layer_index > 0:
                    current = low_back(low(current))
                current = row_layer(current, seg_row, layer_index, frozen, prefix_pairs)
            return current
        checked = jax.checkpoint(one_row)

        def scan_step(carry_value, row_pair):
            return (carry_value, checked(row_pair[0], row_pair[1]))
        unused, outputs = lax.scan(scan_step, jnp.zeros((), jnp.float32), (inputs_all, seg_ids))
        return outputs
    outputs, pullback = jax.vjp(forward, layer_input, prefix_embed.astype(jnp.float32), reparam_w1.astype(jnp.float32), reparam_b1.astype(jnp.float32), reparam_w2.astype(jnp.float32), reparam_b2.astype(jnp.float32))
    gradients = pullback(cotangent)
    boundary_out = jnp.stack([gradients[0], outputs], axis=0).astype(jnp.bfloat16)
    return (boundary_out, gradients[1], gradients[2], gradients[3], gradients[4], gradients[5])
```

```python
import functools

import jax
import jax.numpy as jnp
from jax import lax
from jax.experimental import pallas as pl
from jax.experimental.pallas import tpu as pltpu
from jax.sharding import PartitionSpec as P

epsilon = 1e-05
masked_value = -1e30
max_segment = 512
prefix_rows = 16
stat_rows = 8
f32 = jnp.float32
bf16 = jnp.bfloat16


def dot_nn(a, b):
    return lax.dot_general(a, b, (((1,), (0,)), ((), ())), preferred_element_type=f32)


def dot_nt(a, b):
    return lax.dot_general(a, b, (((1,), (1,)), ((), ())), preferred_element_type=f32)


def key_blocks(index, block_rows):
    reach = -(-(max_segment - 1) // block_rows)
    return list(range(max(0, index - reach), index + 1))


def gather_rows(order_ref, sources, target_ref, block_rows):
    for place in range(2 * len(sources)):
        start = pl.multiple_of(order_ref[place] * block_rows, block_rows)
        target_ref[pl.ds(start, block_rows), :] = sources[place // 2][
            pl.ds((place % 2) * block_rows, block_rows), :
        ]


def scatter_rows(order_ref, source_ref, targets, block_rows, columns):
    for place in range(2 * len(targets)):
        start = pl.multiple_of(order_ref[place] * block_rows, block_rows)
        targets[place // 2][pl.ds((place % 2) * block_rows, block_rows), columns] = source_ref[
            pl.ds(start, block_rows), :
        ].astype(targets[place // 2].dtype)


def segment_column(seg_ref, start, rows):
    row = seg_ref[0:1, start : start + rows]
    return jnp.transpose(jnp.broadcast_to(row, (128, rows)))[:, 0:1]


def attention_forward_kernel(count, block_rows, head_dim, prefix_len, order_ref, *refs):
    packed_refs = refs[:count]
    pairs_ref, seg_ref = refs[count : count + 2]
    context_refs = refs[count + 2 : 2 * count + 2]
    lse_ref, rows_ref, context_ref, bias_ref = refs[2 * count + 2 :]
    width = pairs_ref.shape[2]
    heads = width // head_dim
    blocks = 2 * count
    scaling = head_dim ** (-0.5)
    gather_rows(order_ref, packed_refs, rows_ref, block_rows)
    lane = lax.broadcasted_iota(jnp.int32, (1, width), 1) // head_dim
    stat_lane = lax.broadcasted_iota(jnp.int32, (1, 128), 1)
    prefix_bias = jnp.where(
        lax.broadcasted_iota(jnp.int32, (1, 128), 1) < prefix_len, 0.0, masked_value
    )
    prefix_keys, prefix_values = pairs_ref[0], pairs_ref[1]
    for index in range(blocks):
        start = index * block_rows
        keys = key_blocks(index, block_rows)
        seg_query = segment_column(seg_ref, start, block_rows)
        for slot, key in enumerate(keys):
            same = seg_query == seg_ref[0:1, key * block_rows : (key + 1) * block_rows]
            if key == index:
                shape = (block_rows, block_rows)
                same = same & (
                    lax.broadcasted_iota(jnp.int32, shape, 1)
                    <= lax.broadcasted_iota(jnp.int32, shape, 0)
                )
            bias_ref[slot] = jnp.where(same, 0.0, masked_value)
        queries = rows_ref[pl.ds(start, block_rows), 0:width]

        def one_head(head, carry):
            context_total, stats = carry
            chosen = lane == head
            query = jnp.where(chosen, queries, 0.0) * jnp.asarray(scaling, bf16)
            scores = [
                dot_nt(query, rows_ref[key * block_rows : (key + 1) * block_rows, width : 2 * width])
                + bias_ref[slot]
                for slot, key in enumerate(keys)
            ]
            prefix_scores = dot_nt(query, prefix_keys) + prefix_bias
            row_max = jnp.max(prefix_scores, axis=1, keepdims=True)
            for score in scores:
                row_max = jnp.maximum(row_max, jnp.max(score, axis=1, keepdims=True))
            prefix_exp = jnp.exp(prefix_scores - row_max)
            row_sum = jnp.sum(prefix_exp, axis=1, keepdims=True)
            context = dot_nn(prefix_exp.astype(bf16), prefix_values)
            for score, key in zip(scores, keys):
                exped = jnp.exp(score - row_max)
                row_sum = row_sum + jnp.sum(exped, axis=1, keepdims=True)
                context = context + dot_nn(
                    exped.astype(bf16),
                    rows_ref[key * block_rows : (key + 1) * block_rows, 2 * width :],
                )
            context_total = context_total + jnp.where(chosen, context * (1.0 / row_sum), 0.0)
            stats = jnp.where(stat_lane == head, row_max + jnp.log(row_sum), stats)
            return (context_total, stats)

        context_total, stats = lax.fori_loop(
            0,
            heads,
            one_head,
            (jnp.zeros((block_rows, width), f32), jnp.zeros((block_rows, 128), f32)),
        )
        context_ref[pl.ds(start, block_rows), :] = context_total.astype(bf16)
        lse_ref[:, start : start + block_rows] = jnp.transpose(stats)[0:stat_rows]
    scatter_rows(order_ref, context_ref, context_refs, block_rows, slice(0, width))


def attention_backward_kernel(count, block_rows, head_dim, prefix_len, order_ref, *refs):
    packed_refs = refs[:count]
    grad_refs = refs[count : 2 * count]
    pairs_ref, seg_ref, lse_ref = refs[2 * count : 2 * count + 3]
    out_refs = refs[2 * count + 3 : 3 * count + 3]
    prefix_out = refs[3 * count + 3]
    rows_ref, grad_ref, bias_ref, kt_ref, pkt_ref, dqt_ref, dq_ref, dk_ref, dv_ref = refs[
        3 * count + 4 :
    ]
    width = pairs_ref.shape[2]
    heads = width // head_dim
    blocks = 2 * count
    scaling = head_dim ** (-0.5)
    gather_rows(order_ref, packed_refs, rows_ref, block_rows)
    gather_rows(order_ref, grad_refs, grad_ref, block_rows)
    lane = lax.broadcasted_iota(jnp.int32, (1, width), 1) // head_dim
    prefix_bias = jnp.where(
        lax.broadcasted_iota(jnp.int32, (128, 1), 0) < prefix_len, 0.0, masked_value
    )
    prefix_keys, prefix_values = pairs_ref[0], pairs_ref[1]
    pkt_ref[...] = jnp.transpose(prefix_keys.astype(f32)).astype(bf16)
    dk_ref[...] = jnp.zeros_like(dk_ref)
    dv_ref[...] = jnp.zeros_like(dv_ref)
    prefix_out[...] = jnp.zeros_like(prefix_out)
    for index in range(blocks):
        kt_ref[index] = jnp.transpose(
            rows_ref[index * block_rows : (index + 1) * block_rows, width : 2 * width].astype(f32)
        ).astype(bf16)
    for index in range(blocks):
        start = index * block_rows
        keys = key_blocks(index, block_rows)
        seg_query = seg_ref[0:1, start : start + block_rows]
        for slot, key in enumerate(keys):
            same = segment_column(seg_ref, key * block_rows, block_rows) == seg_query
            if key == index:
                shape = (block_rows, block_rows)
                same = same & (
                    lax.broadcasted_iota(jnp.int32, shape, 0)
                    <= lax.broadcasted_iota(jnp.int32, shape, 1)
                )
            bias_ref[slot] = jnp.where(same, 0.0, masked_value)
        queries = rows_ref[pl.ds(start, block_rows), 0:width]
        grads = grad_ref[pl.ds(start, block_rows), :]

        def one_head(head, carry):
            chosen = lane == head
            query = jnp.where(chosen, queries, 0.0) * jnp.asarray(scaling, bf16)
            grad = jnp.where(chosen, grads, 0.0)
            lse = lse_ref[pl.ds(head, 1), start : start + block_rows]
            span = pl.ds(pl.multiple_of(head * head_dim, head_dim), head_dim)
            prefix_prob = jnp.exp(dot_nt(prefix_keys, query) + prefix_bias - lse)
            prefix_dp = dot_nt(prefix_values, grad)
            delta = jnp.sum(prefix_prob * prefix_dp, axis=0, keepdims=True)
            probs, dps = [], []
            for slot, key in enumerate(keys):
                rows = slice(key * block_rows, (key + 1) * block_rows)
                prob = jnp.exp(
                    dot_nt(rows_ref[rows, width : 2 * width], query) + bias_ref[slot] - lse
                )
                dp = dot_nt(rows_ref[rows, 2 * width :], grad)
                delta = delta + jnp.sum(prob * dp, axis=0, keepdims=True)
                probs.append(prob)
                dps.append(dp)
            prefix_ds = (prefix_prob * (prefix_dp - delta)).astype(bf16)
            prefix_out[0] += dot_nn(prefix_ds, query)
            prefix_out[1] += dot_nn(prefix_prob.astype(bf16), grad)
            dqt = dot_nn(pkt_ref[span, :], prefix_ds)
            for prob, dp, key in zip(probs, dps, keys):
                rows = slice(key * block_rows, (key + 1) * block_rows)
                ds = (prob * (dp - delta)).astype(bf16)
                dk_ref[rows, :] += dot_nn(ds, query)
                dv_ref[rows, :] += dot_nn(prob.astype(bf16), grad)
                dqt = dqt + dot_nn(kt_ref[key, span, :], ds)
            dqt_ref[span, :] = dqt
            return carry

        lax.fori_loop(0, heads, one_head, 0)
        dq_ref[pl.ds(start, block_rows), :] = jnp.transpose(dqt_ref[...]) * scaling
    scatter_rows(order_ref, dq_ref, out_refs, block_rows, slice(0, width))
    scatter_rows(order_ref, dk_ref, out_refs, block_rows, slice(width, 2 * width))
    scatter_rows(order_ref, dv_ref, out_refs, block_rows, slice(2 * width, 3 * width))


def whole(memory_space=pltpu.VMEM):
    return pl.BlockSpec(memory_space=memory_space)


def attention_forward(order, packed, pairs, seg_row, head_dim, prefix_len):
    count = len(packed)
    block_rows = packed[0].shape[0] // 2
    width = packed[0].shape[1] // 3
    seq_len = seg_row.shape[1]
    slots = len(key_blocks(2 * count - 1, block_rows))
    results = pl.pallas_call(
        functools.partial(attention_forward_kernel, count, block_rows, head_dim, prefix_len),
        out_shape=[jax.ShapeDtypeStruct((2 * block_rows, width), bf16)] * count
        + [jax.ShapeDtypeStruct((stat_rows, seq_len), f32)],
        in_specs=[whole(pltpu.SMEM)] + [whole()] * (count + 2),
        out_specs=[whole()] * (count + 1),
        scratch_shapes=[
            pltpu.VMEM((seq_len, 3 * width), bf16),
            pltpu.VMEM((seq_len, width), bf16),
            pltpu.VMEM((slots, block_rows, block_rows), f32),
        ],
        compiler_params=pltpu.CompilerParams(vmem_limit_bytes=32 << 20),
        cost_estimate=pl.CostEstimate(
            flops=8 * seq_len * seq_len * width, bytes_accessed=8 * seq_len * width, transcendentals=0
        ),
        name="attention_forward",
    )(order, *packed, pairs, seg_row)
    return (results[:count], results[count])


def attention_backward(order, packed, grads, pairs, seg_row, lse, head_dim, prefix_len):
    count = len(packed)
    block_rows = packed[0].shape[0] // 2
    width = packed[0].shape[1] // 3
    seq_len = seg_row.shape[1]
    blocks = 2 * count
    slots = len(key_blocks(blocks - 1, block_rows))
    results = pl.pallas_call(
        functools.partial(attention_backward_kernel, count, block_rows, head_dim, prefix_len),
        out_shape=[jax.ShapeDtypeStruct((2 * block_rows, 3 * width), bf16)] * count
        + [jax.ShapeDtypeStruct(pairs.shape, f32)],
        in_specs=[whole(pltpu.SMEM)] + [whole()] * (2 * count + 3),
        out_specs=[whole()] * (count + 1),
        scratch_shapes=[
            pltpu.VMEM((seq_len, 3 * width), bf16),
            pltpu.VMEM((seq_len, width), bf16),
            pltpu.VMEM((slots, block_rows, block_rows), f32),
            pltpu.VMEM((blocks, width, block_rows), bf16),
            pltpu.VMEM((width, pairs.shape[1]), bf16),
            pltpu.VMEM((width, block_rows), f32),
            pltpu.VMEM((seq_len, width), f32),
            pltpu.VMEM((seq_len, width), f32),
            pltpu.VMEM((seq_len, width), f32),
        ],
        compiler_params=pltpu.CompilerParams(vmem_limit_bytes=32 << 20),
        cost_estimate=pl.CostEstimate(
            flops=20 * seq_len * seq_len * width,
            bytes_accessed=20 * seq_len * width,
            transcendentals=0,
        ),
        name="attention_backward",
    )(order, *packed, *grads, pairs, seg_row, lse)
    return (results[:count], results[count])


def centered_values(values):
    centered = values - jnp.mean(values, axis=-1, keepdims=True)
    scale = lax.rsqrt(jnp.mean(centered * centered, axis=-1, keepdims=True) + epsilon)
    return (centered * scale, scale)


def layer_norm(values, ln_gain, ln_bias):
    return centered_values(values)[0] * ln_gain + ln_bias


def norm_back(values, ln_gain, grad_normed):
    unit, scale = centered_values(values)
    entry = grad_normed * ln_gain
    return scale * (
        entry
        - jnp.mean(entry, axis=-1, keepdims=True)
        - unit * jnp.mean(entry * unit, axis=-1, keepdims=True)
    )


def gelu_both(values):
    root = 0.7978845608028654
    inner = root * (values + 0.044715 * values * values * values)
    curve = jnp.tanh(inner)
    slope = root * (1.0 + 3 * 0.044715 * values * values)
    return (
        0.5 * values * (1.0 + curve),
        0.5 * (1.0 + curve) + 0.5 * values * (1.0 - curve * curve) * slope,
    )


class Group:
    def __init__(self, tensor_size):
        self.size = tensor_size
        self.count = tensor_size // 2

    def core_swap(self, value):
        return lax.ppermute(value, "section", [(0, 1), (1, 0)])

    def shift(self, value, distance):
        pairs = [
            (half * self.count + place, half * self.count + (place + distance) % self.count)
            for half in range(2)
            for place in range(self.count)
        ]
        return lax.ppermute(value, "tensor", pairs)

    def from_layer(self, value, layer):
        size, count = self.size, self.count
        pairs = [(layer * size + place, size + (place + count) % size) for place in range(size)]
        return lax.ppermute(value, ("section", "tensor"), pairs)

    def to_layer(self, value, core, layer):
        size, count = self.size, self.count
        pairs = [
            (core * size + place, layer * size + (place + core * count) % size)
            for place in range(size)
        ]
        return lax.ppermute(value, ("section", "tensor"), pairs)

    def down(self, value):
        return lax.ppermute(value, "section", [(1, 0)])

    def up(self, value):
        return lax.ppermute(value, "section", [(0, 1)])

    def gather(self, block):
        arrived = [block] + [self.shift(block, distance) for distance in range(1, self.count)]
        return [jnp.concatenate([part, self.core_swap(part)], axis=0) for part in arrived]

    def scatter(self, parts):
        rows = parts[0].shape[0] // 2
        total = None
        for distance in list(range(1, self.count)) + [0]:
            own, other = (parts[distance][:rows], parts[distance][rows:])
            summed = own.astype(f32) + self.core_swap(other).astype(f32)
            if distance:
                summed = self.shift(summed.astype(bf16), -distance).astype(f32)
            total = summed if total is None else total + summed
        return total


def local(
    boundary,
    seg_ids,
    ln1_gain,
    ln1_bias,
    w_qkv,
    b_qkv,
    w_out,
    b_out,
    ln2_gain,
    ln2_bias,
    w_up,
    b_up,
    w_down,
    b_down,
    prefix_embed,
    reparam_w1,
    reparam_b1,
    reparam_w2,
    reparam_b2,
):
    core = lax.axis_index("section")
    place = lax.axis_index("tensor")
    group = Group(lax.axis_size("tensor"))
    count = group.count
    tok_rows, width = boundary.shape[2:]
    heads_local = w_qkv.shape[2]
    head_dim = w_qkv.shape[3] // 3
    head_width = heads_local * head_dim
    prefix_len = prefix_embed.shape[0]
    row = place // count
    low = core == 0

    prefix_pre = dot_nn(prefix_embed, reparam_w1) + reparam_b1.astype(f32)
    curve = jnp.tanh(prefix_pre)
    hidden_low = curve.astype(bf16)
    w2_own = (
        reparam_w2.reshape(reparam_w2.shape[0], heads_local, 2, head_dim)
        .transpose(0, 2, 1, 3)
        .reshape(reparam_w2.shape[0], 2 * head_width)
    )
    b2_own = (
        reparam_b2.reshape(heads_local, 2, head_dim).transpose(1, 0, 2).reshape(2 * head_width)
    )
    prefix_own = (dot_nn(hidden_low, w2_own) + b2_own.astype(f32)).astype(bf16)

    def as_rows(value):
        value = value.reshape(-1, value.shape[-1])
        return jnp.pad(value, ((0, 0), (0, width - value.shape[1])))

    b_qkv_own = b_qkv.reshape(heads_local, 3, head_dim).transpose(1, 0, 2).reshape(1, 3 * head_width)
    pad_prefix = ((0, prefix_rows - prefix_len), (0, 0))
    small_own = jnp.concatenate(
        [
            as_rows(ln1_gain),
            as_rows(ln1_bias),
            as_rows(b_out),
            as_rows(ln2_gain),
            as_rows(ln2_bias),
            as_rows(b_down),
            as_rows(b_up),
            as_rows(b_qkv_own),
            as_rows(jnp.pad(prefix_own[:, :head_width], pad_prefix)),
            as_rows(jnp.pad(prefix_own[:, head_width:], pad_prefix)),
        ],
        axis=0,
    )
    qkv_own = (
        w_qkv.reshape(width, heads_local, 3, head_dim)
        .transpose(0, 2, 1, 3)
        .reshape(width, 3 * head_width)
    )
    out_own = w_out.reshape(head_width, width)

    def both_layers(value):
        return (
            jnp.where(low, value, group.from_layer(value, 0)),
            jnp.where(low, group.down(value), group.from_layer(value, 1)),
        )

    own_row = lax.dynamic_index_in_dim(boundary[0], row, 0, False)
    other_row = lax.dynamic_index_in_dim(boundary[0], 1 - row, 0, False)
    inputs = jnp.where(low, own_row, group.from_layer(other_row, 0)).astype(f32)
    cotangent = jnp.where(low, group.down(own_row), group.from_layer(other_row, 1))

    small = both_layers(small_own)
    qkv = both_layers(qkv_own)
    outs = both_layers(out_own)
    ups = both_layers(w_up[0])
    downs = both_layers(w_down[0])

    seg_row = lax.dynamic_index_in_dim(seg_ids, row, 0, True).astype(f32)
    chip = place % count
    order = jnp.stack(
        [
            jnp.bitwise_xor(row, jnp.bitwise_xor(core, swapped)) * count
            + (chip - distance + count) % count
            for distance in range(count)
            for swapped in range(2)
        ]
    ).astype(jnp.int32)

    class Layer:
        def __init__(self, index):
            vectors = small[index].astype(f32)
            (
                self.ln1_gain,
                self.ln1_bias,
                self.b_out,
                self.ln2_gain,
                self.ln2_bias,
                self.b_down,
                self.b_up,
                self.b_qkv,
            ) = [vectors[at : at + 1] for at in range(8)]
            self.b_up = self.b_up[:, : ups[index].shape[1]]
            self.b_qkv = self.b_qkv[:, : 3 * head_width]
            pairs = small[index][8 : 8 + 2 * prefix_rows, :head_width].reshape(
                2, prefix_rows, head_width
            )
            self.pairs = jnp.pad(pairs, ((0, 0), (0, 128 - prefix_rows), (0, 0)))
            self.qkv, self.out, self.up, self.down = (
                qkv[index],
                outs[index],
                ups[index],
                downs[index],
            )

        def forward(self, inputs):
            self.inputs = inputs
            normed = layer_norm(inputs, self.ln1_gain, self.ln1_bias).astype(bf16)
            self.packed = [
                (dot_nn(part, self.qkv) + self.b_qkv).astype(bf16) for part in group.gather(normed)
            ]
            context, self.lse = attention_forward(
                order, self.packed, self.pairs, seg_row, head_dim, prefix_len
            )
            attn = group.scatter([dot_nn(part, self.out).astype(bf16) for part in context])
            self.middle = inputs + (attn + self.b_out)
            normed_two = layer_norm(self.middle, self.ln2_gain, self.ln2_bias).astype(bf16)
            self.slopes = []
            parts = []
            for part in group.gather(normed_two):
                hidden, slope = gelu_both(dot_nn(part, self.up) + self.b_up)
                self.slopes.append(slope)
                parts.append(dot_nn(hidden.astype(bf16), self.down).astype(bf16))
            return self.middle + (group.scatter(parts) + self.b_down)

        def backward(self, grad_out):
            parts = []
            for part, slope in zip(group.gather(grad_out.astype(bf16)), self.slopes):
                grad_pre = (dot_nt(part, self.down) * slope).astype(bf16)
                parts.append(dot_nt(grad_pre, self.up).astype(bf16))
            grad_middle = grad_out + norm_back(self.middle, self.ln2_gain, group.scatter(parts))
            grads = [
                dot_nt(part, self.out).astype(bf16)
                for part in group.gather(grad_middle.astype(bf16))
            ]
            grad_packed, grad_pairs = attention_backward(
                order, self.packed, grads, self.pairs, seg_row, self.lse, head_dim, prefix_len
            )
            grad_normed = group.scatter(
                [dot_nt(part, self.qkv).astype(bf16) for part in grad_packed]
            )
            grad_in = grad_middle + norm_back(self.inputs, self.ln1_gain, grad_normed)
            return (grad_in, grad_pairs[:, :prefix_rows])

    layers = (Layer(0), Layer(1))
    first_out = layers[0].forward(inputs).astype(bf16)
    last_out = layers[1].forward(first_out.astype(f32)).astype(bf16)
    mid_grad, grad_pairs_one = layers[1].backward(cotangent.astype(f32))
    first_grad, grad_pairs_zero = layers[0].backward(mid_grad.astype(bf16).astype(f32))
    first_grad = first_grad.astype(bf16)

    own_result = jnp.where(low, first_grad, group.up(last_out))
    other_result = jnp.where(
        low, group.to_layer(first_grad, 1, 0), group.to_layer(last_out, 1, 1)
    )
    boundary_result = jnp.where(
        row == 0, jnp.stack([own_result, other_result]), jnp.stack([other_result, own_result])
    )[None]

    grad_prefix = jnp.where(
        low,
        grad_pairs_zero + group.to_layer(grad_pairs_zero, 1, 0),
        group.up(grad_pairs_one) + group.to_layer(grad_pairs_one, 1, 1),
    )
    grad_low = lax.psum(grad_prefix, "dp")[:, :prefix_len].astype(bf16)
    grad_flat = jnp.concatenate([grad_low[0], grad_low[1]], axis=1)
    w2_grad = (
        lax.dot_general(
            hidden_low, grad_flat, (((0,), (0,)), ((), ())), preferred_element_type=f32
        )
        .reshape(reparam_w2.shape[0], 2, heads_local, head_dim)
        .transpose(0, 2, 1, 3)
        .reshape(reparam_w2.shape)
    )
    b2_grad = (
        jnp.sum(grad_flat.astype(f32), axis=0)
        .reshape(2, heads_local, head_dim)
        .transpose(1, 0, 2)
        .reshape(reparam_b2.shape)
    )
    hidden_grad = lax.psum(dot_nt(grad_flat, w2_own), ("section", "tensor"))
    pre_grad = (hidden_grad * (1.0 - curve * curve)).astype(bf16)
    w1_grad = lax.dot_general(
        prefix_embed, pre_grad, (((0,), (0,)), ((), ())), preferred_element_type=f32
    )
    b1_grad = jnp.sum(pre_grad.astype(f32), axis=0)
    embed_grad = dot_nt(pre_grad, reparam_w1)
    return (boundary_result, embed_grad, w1_grad, b1_grad, w2_grad, b2_grad)


def solution(mesh):
    return jax.shard_map(
        local,
        mesh=mesh,
        in_specs=(
            P("section", "dp", "tensor", None),
            P("dp", None),
            P("section", None),
            P("section", None),
            P("section", None, "tensor", None),
            P("section", "tensor", None),
            P("section", "tensor", None, None),
            P("section", None),
            P("section", None),
            P("section", None),
            P("section", None, "tensor"),
            P("section", "tensor"),
            P("section", "tensor", None),
            P("section", None),
            P(),
            P(),
            P(),
            P(None, "section", "tensor", None),
            P("section", "tensor", None),
        ),
        out_specs=(
            P("section", "dp", "tensor", None),
            P(),
            P(),
            P(),
            P(None, "section", "tensor", None),
            P("section", "tensor", None),
        ),
        check_vma=False,
    )
```

```python
import functools

import jax
import jax.numpy as jnp
from jax import lax
from jax.experimental import pallas as pl
from jax.experimental.pallas import tpu as pltpu
from jax.sharding import PartitionSpec as P

epsilon = 1e-05
masked_value = -1e30
max_segment = 512
prefix_rows = 16
stat_rows = 8
f32 = jnp.float32
bf16 = jnp.bfloat16


small_cost = pl.CostEstimate(flops=1, bytes_accessed=1, transcendentals=0)


def dot_nn(a, b):
    return lax.dot_general(a, b, (((1,), (0,)), ((), ())), preferred_element_type=f32)


def dot_nt(a, b):
    return lax.dot_general(a, b, (((1,), (1,)), ((), ())), preferred_element_type=f32)


def key_blocks(index, block_rows):
    reach = -(-(max_segment - 1) // block_rows)
    return list(range(max(0, index - reach), index + 1))


def gather_rows(order_ref, sources, target_ref, block_rows):
    for place in range(2 * len(sources)):
        start = pl.multiple_of(order_ref[place] * block_rows, block_rows)
        target_ref[pl.ds(start, block_rows), :] = sources[place // 2][
            pl.ds((place % 2) * block_rows, block_rows), :
        ]


def scatter_rows(order_ref, source_ref, targets, block_rows, columns):
    for place in range(2 * len(targets)):
        start = pl.multiple_of(order_ref[place] * block_rows, block_rows)
        targets[place // 2][pl.ds((place % 2) * block_rows, block_rows), columns] = source_ref[
            pl.ds(start, block_rows), :
        ].astype(targets[place // 2].dtype)


def segment_column(seg_ref, start, rows):
    row = seg_ref[0:1, start : start + rows]
    return jnp.transpose(jnp.broadcast_to(row, (128, rows)))[:, 0:1]


def attention_forward_kernel(count, block_rows, head_dim, prefix_len, order_ref, *refs):
    packed_refs = refs[:count]
    pairs_ref, seg_ref = refs[count : count + 2]
    context_refs = refs[count + 2 : 2 * count + 2]
    lse_ref, rows_ref, context_ref, bias_ref, vt_ref, pvt_ref, ct_ref = refs[2 * count + 2 :]
    width = pairs_ref.shape[2]
    heads = width // head_dim
    blocks = 2 * count
    scaling = head_dim ** (-0.5)
    gather_rows(order_ref, packed_refs, rows_ref, block_rows)
    lane = lax.broadcasted_iota(jnp.int32, (1, width), 1) // head_dim
    prefix_bias = jnp.where(
        lax.broadcasted_iota(jnp.int32, (pairs_ref.shape[1], 1), 0) < prefix_len, 0.0, masked_value
    )
    prefix_keys = pairs_ref[0]
    pvt_ref[...] = jnp.transpose(pairs_ref[1].astype(f32)).astype(bf16)
    for index in range(blocks):
        vt_ref[index] = jnp.transpose(
            rows_ref[index * block_rows : (index + 1) * block_rows, 2 * width :].astype(f32)
        ).astype(bf16)
    for index in range(blocks):
        start = index * block_rows
        keys = key_blocks(index, block_rows)
        fill_bias(seg_ref, bias_ref, index, keys, block_rows)
        queries = rows_ref[pl.ds(start, block_rows), 0:width]

        def one_head(head, carry):
            query = jnp.where(lane == head, queries, 0.0) * jnp.asarray(scaling, bf16)
            span = pl.ds(pl.multiple_of(head * head_dim, head_dim), head_dim)
            prefix_scores = dot_nt(prefix_keys, query) + prefix_bias
            row_max = jnp.max(prefix_scores, axis=0, keepdims=True)
            scores = []
            for slot, key in enumerate(keys):
                rows = slice(key * block_rows, (key + 1) * block_rows)
                score = dot_nt(rows_ref[rows, width : 2 * width], query) + bias_ref[slot]
                row_max = jnp.maximum(row_max, jnp.max(score, axis=0, keepdims=True))
                scores.append(score)
            prefix_exp = jnp.exp(prefix_scores - row_max)
            row_sum = jnp.sum(prefix_exp, axis=0, keepdims=True)
            context = dot_nn(pvt_ref[span, :], prefix_exp.astype(bf16))
            for score, key in zip(scores, keys):
                exped = jnp.exp(score - row_max)
                row_sum = row_sum + jnp.sum(exped, axis=0, keepdims=True)
                context = context + dot_nn(vt_ref[key, span, :], exped.astype(bf16))
            ct_ref[span, :] = context * (1.0 / row_sum)
            lse_ref[pl.ds(head, 1), start : start + block_rows] = row_max + jnp.log(row_sum)
            return carry

        lax.fori_loop(0, heads, one_head, 0, unroll=True)
        context_ref[pl.ds(start, block_rows), :] = jnp.transpose(ct_ref[...]).astype(bf16)
    scatter_rows(order_ref, context_ref, context_refs, block_rows, slice(0, width))


def fill_bias(seg_ref, bias_ref, index, keys, block_rows):
    seg_query = seg_ref[0:1, index * block_rows : (index + 1) * block_rows]
    for slot, key in enumerate(keys):
        same = segment_column(seg_ref, key * block_rows, block_rows) == seg_query
        if key == index:
            shape = (block_rows, block_rows)
            same = same & (
                lax.broadcasted_iota(jnp.int32, shape, 0)
                <= lax.broadcasted_iota(jnp.int32, shape, 1)
            )
        bias_ref[slot] = jnp.where(same, 0.0, masked_value)


def attention_backward_kernel(count, block_rows, head_dim, prefix_len, order_ref, *refs):
    packed_refs = refs[:count]
    grad_refs = refs[count : 2 * count]
    pairs_ref, seg_ref, lse_ref = refs[2 * count : 2 * count + 3]
    out_refs = refs[2 * count + 3 : 3 * count + 3]
    prefix_out = refs[3 * count + 3]
    rows_ref, grad_ref, bias_ref, kt_ref, pkt_ref, dqt_ref, dq_ref, dk_ref, dv_ref = refs[
        3 * count + 4 :
    ]
    width = pairs_ref.shape[2]
    heads = width // head_dim
    blocks = 2 * count
    scaling = head_dim ** (-0.5)
    gather_rows(order_ref, packed_refs, rows_ref, block_rows)
    gather_rows(order_ref, grad_refs, grad_ref, block_rows)
    lane = lax.broadcasted_iota(jnp.int32, (1, width), 1) // head_dim
    prefix_bias = jnp.where(
        lax.broadcasted_iota(jnp.int32, (pairs_ref.shape[1], 1), 0) < prefix_len, 0.0, masked_value
    )
    prefix_keys, prefix_values = pairs_ref[0], pairs_ref[1]
    pkt_ref[...] = jnp.transpose(prefix_keys.astype(f32)).astype(bf16)
    dk_ref[...] = jnp.zeros_like(dk_ref)
    dv_ref[...] = jnp.zeros_like(dv_ref)
    prefix_out[...] = jnp.zeros_like(prefix_out)
    for index in range(blocks):
        kt_ref[index] = jnp.transpose(
            rows_ref[index * block_rows : (index + 1) * block_rows, width : 2 * width].astype(f32)
        ).astype(bf16)
    for index in range(blocks):
        start = index * block_rows
        keys = key_blocks(index, block_rows)
        fill_bias(seg_ref, bias_ref, index, keys, block_rows)
        queries = rows_ref[pl.ds(start, block_rows), 0:width]
        grads = grad_ref[pl.ds(start, block_rows), :]

        def one_head(head, carry):
            chosen = lane == head
            query = jnp.where(chosen, queries, 0.0) * jnp.asarray(scaling, bf16)
            grad = jnp.where(chosen, grads, 0.0)
            lse = lse_ref[pl.ds(head, 1), start : start + block_rows]
            span = pl.ds(pl.multiple_of(head * head_dim, head_dim), head_dim)
            prefix_prob = jnp.exp(dot_nt(prefix_keys, query) + prefix_bias - lse)
            prefix_dp = dot_nt(prefix_values, grad)
            delta = jnp.sum(prefix_prob * prefix_dp, axis=0, keepdims=True)
            probs, dps = [], []
            for slot, key in enumerate(keys):
                rows = slice(key * block_rows, (key + 1) * block_rows)
                prob = jnp.exp(
                    dot_nt(rows_ref[rows, width : 2 * width], query) + bias_ref[slot] - lse
                )
                dp = dot_nt(rows_ref[rows, 2 * width :], grad)
                delta = delta + jnp.sum(prob * dp, axis=0, keepdims=True)
                probs.append(prob)
                dps.append(dp)
            prefix_ds = (prefix_prob * (prefix_dp - delta)).astype(bf16)
            prefix_out[0] += dot_nn(prefix_ds, query)
            prefix_out[1] += dot_nn(prefix_prob.astype(bf16), grad)
            dqt = dot_nn(pkt_ref[span, :], prefix_ds)
            for prob, dp, key in zip(probs, dps, keys):
                rows = slice(key * block_rows, (key + 1) * block_rows)
                ds = (prob * (dp - delta)).astype(bf16)
                dk_ref[rows, :] += dot_nn(ds, query)
                dv_ref[rows, :] += dot_nn(prob.astype(bf16), grad)
                dqt = dqt + dot_nn(kt_ref[key, span, :], ds)
            dqt_ref[span, :] = dqt
            return carry

        lax.fori_loop(0, heads, one_head, 0, unroll=True)
        dq_ref[pl.ds(start, block_rows), :] = jnp.transpose(dqt_ref[...]) * scaling
    scatter_rows(order_ref, dq_ref, out_refs, block_rows, slice(0, width))
    scatter_rows(order_ref, dk_ref, out_refs, block_rows, slice(width, 2 * width))
    scatter_rows(order_ref, dv_ref, out_refs, block_rows, slice(2 * width, 3 * width))


def gelu_parts(values):
    root = 0.7978845608028654
    square = values * values
    curve = jnp.tanh(root * values * (1.0 + 0.044715 * square))
    return (square, curve, root)


def feed_forward_kernel(groups, per, with_output, with_grad, *refs):
    refs = list(refs)
    normed_own, normed_peer, bias_ref = refs[:3]
    del refs[:3]
    grad_own, grad_peer = (refs.pop(0), refs.pop(0)) if with_grad else (None, None)
    chunk_refs = refs[: per * groups]
    del refs[: per * groups]
    out_own, out_peer = (refs.pop(0), refs.pop(0)) if with_output else (None, None)
    back_own, back_peer = (refs.pop(0), refs.pop(0)) if with_grad else (None, None)
    weight_ref, sems, normed_ref, grad_ref, hidden_ref, back_ref = refs
    tokens, width = normed_own.shape
    hidden = bias_ref.shape[2]
    rows = hidden // per
    block = min(256, width)

    def copies_of(group):
        return [
            pltpu.make_async_copy(
                chunk_refs[per * group + part],
                weight_ref.at[pl.ds((per * group + part) * rows, rows)],
                sems.at[group, part],
            )
            for part in range(per)
        ]

    for group in range(min(2, groups)):
        for copy in copies_of(group):
            copy.start()
    normed_ref[0:tokens, :] = normed_own[...]
    normed_ref[tokens:, :] = normed_peer[...]
    if with_grad:
        grad_ref[0:tokens, :] = grad_own[...]
        grad_ref[tokens:, :] = grad_peer[...]
    for group in range(groups):
        span = slice(group * hidden, (group + 1) * hidden)
        for copy in copies_of(group):
            copy.wait()
        if group + 2 < groups:
            for copy in copies_of(group + 2):
                copy.start()
        pre = dot_nt(normed_ref[...], weight_ref[span, 0:width]) + bias_ref[group]
        square, curve, root = gelu_parts(pre)
        if with_output:
            hidden_ref[:, span] = (0.5 * pre * (1.0 + curve)).astype(bf16)
        if with_grad:
            slope = 0.5 * (1.0 + curve) + 0.5 * pre * (1.0 - curve * curve) * (
                root * (1.0 + 3 * 0.044715 * square)
            )
            back_ref[:, span] = (dot_nt(grad_ref[...], weight_ref[span, width:]) * slope).astype(bf16)

    for at in range(0, width, block):
        span = slice(at, at + block)
        if with_output:
            total = dot_nn(hidden_ref[...], weight_ref[:, width + at : width + at + block])
            out_own[:, span] = total[0:tokens]
            out_peer[:, span] = total[tokens:].astype(bf16)
        if with_grad:
            total = dot_nn(back_ref[...], weight_ref[:, span])
            back_own[:, span] = total[0:tokens]
            back_peer[:, span] = total[tokens:].astype(bf16)


def whole(memory_space=pltpu.VMEM):
    return pl.BlockSpec(memory_space=memory_space)


def attention_forward(order, packed, pairs, seg_row, head_dim, prefix_len):
    count = len(packed)
    block_rows = packed[0].shape[0] // 2
    width = packed[0].shape[1] // 3
    seq_len = seg_row.shape[1]
    slots = len(key_blocks(2 * count - 1, block_rows))
    results = pl.pallas_call(
        functools.partial(attention_forward_kernel, count, block_rows, head_dim, prefix_len),
        out_shape=[jax.ShapeDtypeStruct((2 * block_rows, width), bf16)] * count
        + [jax.ShapeDtypeStruct((stat_rows, seq_len), f32)],
        in_specs=[whole(pltpu.SMEM)] + [whole()] * (count + 2),
        out_specs=[whole()] * (count + 1),
        scratch_shapes=[
            pltpu.VMEM((seq_len, 3 * width), bf16),
            pltpu.VMEM((seq_len, width), bf16),
            pltpu.VMEM((slots, block_rows, block_rows), f32),
            pltpu.VMEM((2 * count, width, block_rows), bf16),
            pltpu.VMEM((width, pairs.shape[1]), bf16),
            pltpu.VMEM((width, block_rows), f32),
        ],
        compiler_params=pltpu.CompilerParams(vmem_limit_bytes=32 << 20),
        cost_estimate=small_cost,
        name="attention_forward",
    )(order, *packed, pairs, seg_row)
    return (results[:count], results[count])


def attention_backward(order, packed, grads, pairs, seg_row, lse, head_dim, prefix_len):
    count = len(packed)
    block_rows = packed[0].shape[0] // 2
    width = packed[0].shape[1] // 3
    seq_len = seg_row.shape[1]
    blocks = 2 * count
    slots = len(key_blocks(blocks - 1, block_rows))
    results = pl.pallas_call(
        functools.partial(attention_backward_kernel, count, block_rows, head_dim, prefix_len),
        out_shape=[jax.ShapeDtypeStruct((2 * block_rows, 3 * width), bf16)] * count
        + [jax.ShapeDtypeStruct(pairs.shape, f32)],
        in_specs=[whole(pltpu.SMEM)] + [whole()] * (2 * count + 3),
        out_specs=[whole()] * (count + 1),
        scratch_shapes=[
            pltpu.VMEM((seq_len, 3 * width), bf16),
            pltpu.VMEM((seq_len, width), bf16),
            pltpu.VMEM((slots, block_rows, block_rows), f32),
            pltpu.VMEM((blocks, width, block_rows), bf16),
            pltpu.VMEM((width, pairs.shape[1]), bf16),
            pltpu.VMEM((width, block_rows), f32),
            pltpu.VMEM((seq_len, width), f32),
            pltpu.VMEM((seq_len, width), f32),
            pltpu.VMEM((seq_len, width), f32),
        ],
        compiler_params=pltpu.CompilerParams(vmem_limit_bytes=32 << 20),
        cost_estimate=small_cost,
        name="attention_backward",
    )(order, *packed, *grads, pairs, seg_row, lse)
    return (results[:count], results[count])


def chunk_kernel(place_ref, up_ref, down_ref, keep_ref, give_ref, up, down, chunks, sems, out_sems):
    hidden, width = down.shape
    rows = hidden // 4
    core, parity = place_ref[0], place_ref[1]
    half = width // 2
    loads = []
    for at in range(2):
        span = pl.ds(at * half, half)
        loads.append(pltpu.make_async_copy(up_ref.at[span], up.at[span], sems.at[at]))
    for at in range(2):
        span = pl.ds(at * 2 * rows, 2 * rows)
        loads.append(pltpu.make_async_copy(down_ref.at[span], down.at[span], sems.at[2 + at]))
    for load in loads:
        load.start()
    spots = []
    for side in range(2):
        for which in range(2):
            spots.append(
                (1 - core if side else core, 1 - parity if which else parity, 2 * side + which)
            )
    for at in range(2):
        loads[at].wait()
        span = slice(at * half, (at + 1) * half)
        for side, slot, index in spots:
            chunks[side, slot, :, span] = jnp.transpose(up[span, index * rows : (index + 1) * rows])
    for at in range(2):
        loads[2 + at].wait()
        for side, slot, index in spots[2 * at : 2 * at + 2]:
            chunks[side, slot, :, width:] = down[index * rows : (index + 1) * rows, :]
    stores = [
        pltpu.make_async_copy(chunks.at[side], target, out_sems.at[side])
        for side, target in enumerate((keep_ref, give_ref))
    ]
    for store in stores:
        store.start()
    for store in stores:
        store.wait()


def feed_forward_chunks(place, up, down):
    hidden, width = down.shape
    shape = (2, hidden // 4, 2 * width)
    return pl.pallas_call(
        chunk_kernel,
        out_shape=[jax.ShapeDtypeStruct(shape, bf16)] * 2,
        in_specs=[whole(pltpu.SMEM), whole(pltpu.HBM), whole(pltpu.HBM)],
        out_specs=[whole(pltpu.HBM)] * 2,
        scratch_shapes=[
            pltpu.VMEM((width, hidden), bf16),
            pltpu.VMEM((hidden, width), bf16),
            pltpu.VMEM((2,) + shape, bf16),
            pltpu.SemaphoreType.DMA((4,)),
            pltpu.SemaphoreType.DMA((2,)),
        ],
        compiler_params=pltpu.CompilerParams(vmem_limit_bytes=20 << 20),
        cost_estimate=small_cost,
        name="feed_forward_chunks",
    )(place, up, down)


def feed_forward(normed, bias, chunks, grads, with_output, per):
    rows = chunks[0].shape[0]
    groups, hidden = (len(chunks) // per, per * rows)
    bias = bias.reshape(groups, 1, hidden)
    tokens, width = normed[0].shape
    with_grad = grads is not None
    kinds = with_output + with_grad
    small = (8, 128)
    return pl.pallas_call(
        functools.partial(feed_forward_kernel, groups, per, with_output, with_grad),
        out_shape=[
            jax.ShapeDtypeStruct((tokens, width), f32),
            jax.ShapeDtypeStruct((tokens, width), bf16),
        ]
        * kinds,
        in_specs=[whole()] * (3 + 2 * with_grad) + [whole(pltpu.HBM)] * len(chunks),
        out_specs=[whole()] * (2 * kinds),
        scratch_shapes=[
            pltpu.VMEM((groups * hidden, 2 * width), bf16),
            pltpu.SemaphoreType.DMA((groups, per)),
            pltpu.VMEM((2 * tokens, width), bf16),
            pltpu.VMEM((2 * tokens, width) if with_grad else small, bf16),
            pltpu.VMEM((2 * tokens, groups * hidden) if with_output else small, bf16),
            pltpu.VMEM((2 * tokens, groups * hidden) if with_grad else small, bf16),
        ],
        compiler_params=pltpu.CompilerParams(vmem_limit_bytes=58 << 20),
        cost_estimate=small_cost,
        name="feed_forward",
    )(*normed, bias, *(grads if with_grad else ()), *chunks)


def place_kernel(spot_ref, low_own, low_other, high_own, high_other, out_ref):
    row = spot_ref[1]

    @pl.when(spot_ref[0] == 0)
    def _():
        out_ref[row] = low_own[...]
        out_ref[1 - row] = low_other[...]

    @pl.when(spot_ref[0] == 1)
    def _():
        out_ref[row] = high_own[...]
        out_ref[1 - row] = high_other[...]


def place_rows(spot, *blocks):
    return pl.pallas_call(
        place_kernel,
        out_shape=jax.ShapeDtypeStruct((2,) + blocks[0].shape, bf16),
        in_specs=[whole(pltpu.SMEM)] + [whole()] * 4,
        out_specs=whole(),
        compiler_params=pltpu.CompilerParams(vmem_limit_bytes=8 << 20),
        cost_estimate=small_cost,
        name="place_rows",
    )(spot, *blocks)


def centered_values(values):
    centered = values - jnp.mean(values, axis=-1, keepdims=True)
    scale = lax.rsqrt(jnp.mean(centered * centered, axis=-1, keepdims=True) + epsilon)
    return (centered * scale, scale)


def layer_norm(values, ln_gain, ln_bias):
    return centered_values(values)[0] * ln_gain + ln_bias


def norm_back(values, ln_gain, grad_normed):
    unit, scale = centered_values(values)
    entry = grad_normed * ln_gain
    return scale * (
        entry
        - jnp.mean(entry, axis=-1, keepdims=True)
        - unit * jnp.mean(entry * unit, axis=-1, keepdims=True)
    )


class Group:
    def __init__(self, tensor_size):
        self.size = tensor_size
        self.count = tensor_size // 2

    def core_swap(self, value):
        return lax.ppermute(value, "section", [(0, 1), (1, 0)])

    def shift(self, value, distance):
        pairs = [
            (half * self.count + place, half * self.count + (place + distance) % self.count)
            for half in range(2)
            for place in range(self.count)
        ]
        return lax.ppermute(value, "tensor", pairs)

    def cross(self, value):
        size, count = self.size, self.count
        pairs = [
            (core * size + place, (1 - core) * size + (place + count) % size)
            for core in range(2)
            for place in range(size)
        ]
        return lax.ppermute(value, ("section", "tensor"), pairs)

    def half_swap(self, value):
        pairs = [(place, (place + self.count) % self.size) for place in range(self.size)]
        return lax.ppermute(value, "tensor", pairs)

    def plane_swap(self, value, distance=1):
        planes = lax.axis_size("dp")
        pairs = [(plane, plane ^ distance) for plane in range(planes)]
        return lax.ppermute(value, "dp", pairs)

    def cross_from(self, value, core):
        size, count = self.size, self.count
        pairs = [
            (core * size + place, (1 - core) * size + (place + count) % size)
            for place in range(size)
        ]
        return lax.ppermute(value, ("section", "tensor"), pairs)

    def sum_planes(self, value):
        planes = lax.axis_size("dp")
        if planes & (planes - 1):
            return lax.psum(value, "dp")
        distance = 1
        while distance < planes:
            value = value + self.plane_swap(value, distance)
            distance *= 2
        return value

    def sum_shards(self, value):
        if self.size & (self.size - 1):
            return lax.psum(value, ("section", "tensor"))
        value = value + self.core_swap(value)
        distance = 1
        while distance < self.size:
            pairs = [(place, place ^ distance) for place in range(self.size)]
            value = value + lax.ppermute(value, "tensor", pairs)
            distance *= 2
        return value

    def shifts(self, stages, block):
        return [
            stages.send(functools.partial(self.shift, distance=distance), block)
            for distance in range(1, self.count)
        ]

    def paired(self, blocks):
        return [jnp.concatenate([part, self.core_swap(part)], axis=0) for part in blocks]

    def gather(self, stages, block):
        return self.paired([block] + self.shifts(stages, block))

    def scatter(self, stages, parts):
        rows = parts[0].shape[0] // 2
        total = None
        for distance in list(range(1, self.count)) + [0]:
            own, other = (parts[distance][:rows], parts[distance][rows:])
            summed = own.astype(f32) + self.core_swap(other).astype(f32)
            if distance:
                back = functools.partial(self.shift, distance=-distance)
                self.leaving = summed.astype(bf16)
                self.arrived = stages.send(back, self.leaving)
                summed = self.arrived.astype(f32)
            total = summed if total is None else total + summed
        return total


class Stages:
    def __init__(self):
        self.before, self.now = ([], [])

    def send(self, transfer, value):
        if self.before:
            value = lax.optimization_barrier((value, *self.before))[0]
        self.now.append(transfer(value))
        return self.now[-1]

    def next(self):
        self.before, self.now = (self.now, [])


def local(
    boundary,
    seg_ids,
    ln1_gain,
    ln1_bias,
    w_qkv,
    b_qkv,
    w_out,
    b_out,
    ln2_gain,
    ln2_bias,
    w_up,
    b_up,
    w_down,
    b_down,
    prefix_embed,
    reparam_w1,
    reparam_b1,
    reparam_w2,
    reparam_b2,
):
    core = lax.axis_index("section")
    place = lax.axis_index("tensor")
    group = Group(lax.axis_size("tensor"))
    count = group.count
    tok_rows, width = boundary.shape[2:]
    heads_local = w_qkv.shape[2]
    head_dim = w_qkv.shape[3] // 3
    head_width = heads_local * head_dim
    prefix_len = prefix_embed.shape[0]
    row = place // count
    low = core == 0

    def tied(value, *others):
        return lax.optimization_barrier((value,) + others)[0]

    stages = Stages()
    steps = range(1, count)

    own_row = lax.dynamic_index_in_dim(boundary[0], row, 0, False)
    other_row = lax.dynamic_index_in_dim(boundary[0], 1 - row, 0, False)
    came_row = stages.send(functools.partial(group.cross_from, core=0), other_row)
    inputs = jnp.where(low, own_row, came_row).astype(f32)
    proj_own = w_out.reshape(head_width, width)

    def layer_pair(own, far):
        return (jnp.where(low, own, far), jnp.where(low, far, own))


    def as_rows(value):
        value = value.reshape(-1, value.shape[-1])
        return jnp.pad(value, ((0, 0), (0, width - value.shape[1])))

    b_qkv_own = b_qkv.reshape(heads_local, 3, head_dim).transpose(1, 0, 2).reshape(1, 3 * head_width)
    small_parts = (ln1_gain, ln1_bias, b_out, ln2_gain, ln2_bias, b_down, b_up, b_up)
    small_own = jnp.concatenate([as_rows(part) for part in small_parts], axis=0)

    def on_chip(value):
        peer = group.core_swap(value)
        return jnp.stack([jnp.where(low, value, peer), jnp.where(low, peer, value)])

    small_chip = on_chip(small_own)

    def vectors_of(layer):
        return small_chip[layer, :8].astype(f32)

    def normed_one(layer, values):
        vectors = vectors_of(layer)
        return layer_norm(values, vectors[0:1], vectors[1:2]).astype(bf16)

    hidden_width = w_up.shape[2]
    rows = hidden_width // 4
    shared = lax.axis_size("dp") % 2 == 0
    parity = lax.axis_index("dp") % 2
    spot = jnp.stack([core, parity]).astype(jnp.int32)
    keep, give = feed_forward_chunks(spot, w_up[0], w_down[0])
    handed = group.core_swap(give)
    even_0 = jnp.where(low, keep[0], handed[0])
    later_keep, later_handed, _ = lax.optimization_barrier((keep, handed, even_0))
    even = [even_0, jnp.where(low, later_handed[0], later_keep[0])]
    odd = [
        jnp.where(low, later_keep[1], later_handed[1]),
        jnp.where(low, later_handed[1], later_keep[1]),
    ]

    prefix_pre = dot_nn(tied(prefix_embed, even[0]), reparam_w1) + reparam_b1.astype(f32)
    curve = jnp.tanh(prefix_pre)
    hidden_low = curve.astype(bf16)
    w2_own = (
        tied(reparam_w2, even[0])
        .reshape(reparam_w2.shape[0], heads_local, 2, head_dim)
        .transpose(0, 2, 1, 3)
        .reshape(reparam_w2.shape[0], 2 * head_width)
    )
    b2_own = (
        reparam_b2.reshape(heads_local, 2, head_dim).transpose(1, 0, 2).reshape(2 * head_width)
    )
    prefix_own = (dot_nn(hidden_low, w2_own) + b2_own.astype(f32)).astype(bf16)
    pairs_own = jnp.concatenate(
        [
            jnp.pad(value, ((0, prefix_rows - value.shape[0]), (0, width - value.shape[1])))
            for value in (prefix_own[:, :head_width], prefix_own[:, head_width:], b_qkv_own)
        ],
        axis=0,
    )
    qkv_own = (
        w_qkv.reshape(width, heads_local, 3, head_dim)
        .transpose(0, 2, 1, 3)
        .reshape(width, 3 * head_width)
    )

    def plane_send(value):
        return stages.send(group.plane_swap, value)

    def half_send(value):
        return stages.send(group.half_swap, value)

    stages.next()
    normed_0 = normed_one(0, inputs)
    gathered_0 = [normed_0] + group.shifts(stages, normed_0)
    side_even_0 = group.shifts(stages, tied(even[0], *gathered_0[1:]))
    small_half = half_send(small_chip)
    qkv_far = stages.send(group.cross, qkv_own)
    proj_far = stages.send(group.cross, proj_own)

    stages.next()
    came_grad = stages.send(functools.partial(group.cross_from, core=1), other_row)
    cotangent = jnp.where(low, came_grad, own_row)
    qkv = layer_pair(qkv_own, qkv_far)
    projs = layer_pair(proj_own, proj_far)
    pairs = layer_pair(pairs_own, stages.send(group.cross, pairs_own))
    up_bias = jnp.stack([small_chip[:, 6, :hidden_width], small_half[:, 6, :hidden_width]], axis=1)
    up_bias = jnp.stack([up_bias] + group.shifts(stages, up_bias), axis=1).astype(f32)
    up_bias = up_bias.reshape(2, 2 * count, 2, 2, rows)
    up_bias = jnp.where(low, up_bias[:, :, 0], up_bias[:, :, 1])
    up_bias = jnp.where(parity == 0, up_bias, up_bias[:, :, ::-1])
    up_bias = up_bias.reshape(2, 4 * count, rows)
    half_even_0 = half_send(even[0])
    side_even_1 = group.shifts(stages, even[1])
    if shared:
        side_odd_0 = [plane_send(value) for value in side_even_0]
    else:
        side_odd_0 = group.shifts(stages, odd[0])

    def all_chunks(layer, half, side, corner):
        chunks = [even[layer], odd[layer], *half]
        for at in range(count - 1):
            chunks += [side[0][at], side[1][at], corner[0][at], corner[1][at]]
        return chunks

    seg_row = lax.dynamic_index_in_dim(seg_ids, row, 0, True).astype(f32)
    chip = place % count
    orders = [
        jnp.stack(
            [
                jnp.bitwise_xor(row, jnp.bitwise_xor(core, swapped ^ layer)) * count
                + (chip - distance + count) % count
                for distance in range(count)
                for swapped in range(2)
            ]
        ).astype(jnp.int32)
        for layer in range(2)
    ]

    class Layer:
        def __init__(self, index):
            self.vectors = vectors_of(index)
            self.ln1_gain, self.ln1_bias, self.b_out = [self.vectors[at : at + 1] for at in range(3)]
            shard = tied(pairs[index], up_bias)
            self.pairs = shard[: 2 * prefix_rows, :head_width].reshape(2, prefix_rows, head_width)
            self.b_qkv = shard[2 * prefix_rows : 2 * prefix_rows + 1, : 3 * head_width].astype(f32)
            self.order = orders[index]
            self.qkv, self.out = (tied(qkv[index], *stages.before), projs[index])
            self.bias = up_bias[index]

        def attention(self, inputs, gathered):
            self.inputs = inputs
            gathered = lax.optimization_barrier((*gathered, *stages.before))[:count]
            self.packed = [
                (dot_nn(part, self.qkv) + self.b_qkv).astype(bf16)
                for part in group.paired(gathered)
            ]
            self.context, self.lse = attention_forward(
                self.order, self.packed, self.pairs, seg_row, head_dim, prefix_len
            )

        def project(self):
            context = lax.optimization_barrier((*self.context, *stages.before))[:count]
            parts = [dot_nn(part, self.out).astype(bf16) for part in context]
            self.middle = self.inputs + (group.scatter(stages, parts) + self.b_out)

        def project_here(self):
            context = lax.optimization_barrier((*self.context, *stages.before))[:count]
            branch = dot_nn(context[0], self.out)
            for distance in steps:
                came = group.shift(context[distance], -distance)
                branch = branch + dot_nn(came, self.out_side[distance - 1])
            rows = branch.shape[0] // 2
            own, peer = (branch[:rows], branch[rows:].astype(bf16))
            self.middle = self.inputs + (self.shared((own, peer)) + self.b_out)

        def norm_two(self, values):
            return layer_norm(values, self.vectors[3:4], self.vectors[4:5]).astype(bf16)

        def shared(self, *pairs):
            return sum([own + group.core_swap(peer).astype(f32) for own, peer in pairs])

        def output(self, middle, *pairs):
            return (middle + (self.shared(*pairs) + self.vectors[5:6])).astype(bf16)

        def middle_back(self, grad_out, *pairs):
            branch = self.shared(*pairs)
            return grad_out.astype(f32) + norm_back(self.middle, self.vectors[3:4], branch)

        def feed_forward(self, normed, grads, with_output):
            return feed_forward(normed, self.bias, self.chunks, grads, with_output, 2)

        def backward(self, grad_middle):
            stages.before = []
            grad_branch = grad_middle.astype(bf16)
            (grad_chip,) = group.paired([grad_branch])
            sides = [dot_nt(grad_chip, side).astype(bf16) for side in self.out_side]
            came = [group.shift(side, at + 1) for at, side in enumerate(sides)]
            grads = [dot_nt(grad_chip, self.out).astype(bf16)] + came
            grad_packed, grad_pairs = attention_backward(
                self.order, self.packed, grads, self.pairs, seg_row, self.lse, head_dim, prefix_len
            )
            parts = [dot_nt(part, self.qkv).astype(bf16) for part in grad_packed]
            grad_normed = group.scatter(stages, parts)
            grad_in = grad_middle + norm_back(self.inputs, self.ln1_gain, grad_normed)
            return (grad_in.astype(bf16), grad_pairs)

    layer_0 = Layer(0)
    layer_0.attention(inputs, gathered_0)

    stages.next()
    corner_even_0 = group.shifts(stages, half_even_0)
    half_even_1 = half_send(even[1])
    if shared:
        side_odd_1 = [plane_send(value) for value in side_even_1]
    else:
        side_odd_1 = group.shifts(stages, odd[1])
    layer_0.project()

    stages.next()
    half_odd_0 = half_send(odd[0])
    if shared:
        corner_odd_0 = [plane_send(value) for value in corner_even_0]
    else:
        corner_odd_0 = group.shifts(stages, half_odd_0)
    corner_even_1 = group.shifts(stages, half_even_1)
    layer_0.chunks = all_chunks(
        0,
        (half_even_0, half_odd_0),
        (side_even_0, side_odd_0),
        (corner_even_0, corner_odd_0),
    )
    middle_peer = group.core_swap(layer_0.middle)
    normed_pair = (layer_0.norm_two(layer_0.middle), layer_0.norm_two(middle_peer))

    stages.next()
    half_odd_1 = half_send(odd[1])
    if shared:
        corner_odd_1 = [plane_send(value) for value in corner_even_1]
    else:
        corner_odd_1 = group.shifts(stages, half_odd_1)
    out_sides = [
        [stages.send(functools.partial(group.shift, distance=-distance), proj) for distance in steps]
        for proj in projs
    ]
    normed_swapped = (tied(normed_pair[1], *stages.before), normed_pair[0])
    out_kept, out_sent = layer_0.feed_forward(normed_swapped, None, True)
    first_out = layer_0.output(middle_peer, (out_kept, tied(out_sent, *stages.now)))
    inputs_1 = first_out.astype(f32)
    normed_1 = normed_one(1, inputs_1)
    gathered_1 = [normed_1] + group.shifts(stages, normed_1)
    layer_1 = Layer(1)
    layer_0.out_side, layer_1.out_side = out_sides
    layer_1.attention(inputs_1, gathered_1)
    layer_1.chunks = all_chunks(
        1,
        (half_even_1, half_odd_1),
        (side_even_1, side_odd_1),
        (corner_even_1, corner_odd_1),
    )

    stages.next()
    w2_far = stages.send(group.cross, w2_own)
    w2_side = layer_pair(w2_own, w2_far)
    layer_1.project_here()
    normed = layer_1.norm_two(layer_1.middle)
    normed = (normed, group.core_swap(normed))
    cotangents = (cotangent, group.core_swap(cotangent))
    parts = layer_1.feed_forward(normed, cotangents, True)
    last_out = layer_1.output(layer_1.middle, parts[:2])
    grad_middle = layer_1.middle_back(cotangent, parts[2:])
    mid_grad, grad_pairs_one = layer_1.backward(grad_middle)
    high_other = group.cross_from(last_out, 0)
    mid_grad = tied(mid_grad, high_other, w2_far)
    mid_peer = group.core_swap(mid_grad)
    back_part = layer_0.feed_forward(normed_pair, (mid_peer, mid_grad), False)
    grad_middle = layer_0.middle_back(mid_peer, back_part)
    first_grad, grad_pairs_zero = layer_0.backward(grad_middle)

    low_other = group.cross_from(first_grad, 1)
    spot = jnp.stack([core, row]).astype(jnp.int32)
    boundary_result = place_rows(spot, first_grad, low_other, last_out, high_other)[None]

    def joined(pairs):
        return jnp.concatenate([pairs[0], pairs[1]], axis=1)

    grads = (joined(grad_pairs_zero), joined(grad_pairs_one))
    hidden_part = sum(
        lax.dot_general(
            grad,
            side.astype(f32),
            (((1,), (1,)), ((), ())),
            precision=lax.Precision.HIGHEST,
            preferred_element_type=f32,
        )
        for grad, side in zip(grads, w2_side)
    )
    kept, sent = layer_pair(*grads)
    summed = tied(jnp.concatenate([hidden_part, kept, sent], axis=1), group.leaving)
    summed = group.sum_planes(summed)
    hidden_width = hidden_part.shape[1]
    hidden_part = tied(summed[:, :hidden_width], group.arrived)
    hidden_grad = group.sum_shards(hidden_part)[:prefix_len]
    kept = summed[:, hidden_width : hidden_width + 2 * head_width]
    sent = summed[:, hidden_width + 2 * head_width :]
    grad_low = (kept + group.cross(sent))[:prefix_len].astype(bf16)
    grad_flat = (
        grad_low.reshape(prefix_len, 2, heads_local, head_dim)
        .transpose(0, 2, 1, 3)
        .reshape(prefix_len, 2 * head_width)
    )
    w2_grad = lax.dot_general(
        hidden_low, grad_flat, (((0,), (0,)), ((), ())), preferred_element_type=f32
    ).reshape(reparam_w2.shape)
    b2_grad = jnp.sum(grad_flat.astype(f32), axis=0).reshape(reparam_b2.shape)
    pre_grad = (hidden_grad * (1.0 - curve * curve)).astype(bf16)
    w1_grad = lax.dot_general(
        prefix_embed, pre_grad, (((0,), (0,)), ((), ())), preferred_element_type=f32
    )
    b1_grad = jnp.sum(pre_grad.astype(f32), axis=0)
    embed_grad = dot_nt(pre_grad, reparam_w1)
    return (boundary_result, embed_grad, w1_grad, b1_grad, w2_grad, b2_grad)


def solution(mesh):
    return jax.shard_map(
        local,
        mesh=mesh,
        in_specs=(
            P("section", "dp", "tensor", None),
            P("dp", None),
            P("section", None),
            P("section", None),
            P("section", None, "tensor", None),
            P("section", "tensor", None),
            P("section", "tensor", None, None),
            P("section", None),
            P("section", None),
            P("section", None),
            P("section", None, "tensor"),
            P("section", "tensor"),
            P("section", "tensor", None),
            P("section", None),
            P(),
            P(),
            P(),
            P(None, "section", "tensor", None),
            P("section", "tensor", None),
        ),
        out_specs=(
            P("section", "dp", "tensor", None),
            P(),
            P(),
            P(),
            P(None, "section", "tensor", None),
            P("section", "tensor", None),
        ),
        check_vma=False,
    )
```

```python
import functools

import jax
import jax.numpy as jnp
from jax import lax
from jax.experimental import pallas as pl
from jax.experimental.pallas import tpu as pltpu
from jax.sharding import PartitionSpec as P

epsilon = 1e-05
masked_value = -1e30
max_segment = 512
prefix_rows = 16
stat_rows = 8
f32 = jnp.float32
bf16 = jnp.bfloat16


small_cost = pl.CostEstimate(flops=1, bytes_accessed=1, transcendentals=0)


def dot_nn(a, b):
    return lax.dot_general(a, b, (((1,), (0,)), ((), ())), preferred_element_type=f32)


def dot_nt(a, b):
    return lax.dot_general(a, b, (((1,), (1,)), ((), ())), preferred_element_type=f32)


def key_blocks(index, block_rows):
    reach = -(-(max_segment - 1) // block_rows)
    return list(range(max(0, index - reach), index + 1))


def gather_rows(order_ref, sources, target_ref, block_rows):
    for place in range(2 * len(sources)):
        start = pl.multiple_of(order_ref[place] * block_rows, block_rows)
        target_ref[pl.ds(start, block_rows), :] = sources[place // 2][
            pl.ds((place % 2) * block_rows, block_rows), :
        ]


def scatter_rows(order_ref, source_ref, targets, block_rows, columns):
    for place in range(2 * len(targets)):
        start = pl.multiple_of(order_ref[place] * block_rows, block_rows)
        targets[place // 2][pl.ds((place % 2) * block_rows, block_rows), columns] = source_ref[
            pl.ds(start, block_rows), :
        ].astype(targets[place // 2].dtype)


def segment_column(seg_ref, start, rows):
    row = seg_ref[0:1, start : start + rows]
    return jnp.transpose(jnp.broadcast_to(row, (128, rows)))[:, 0:1]


def attention_forward_kernel(count, block_rows, head_dim, prefix_len, order_ref, *refs):
    packed_refs = refs[:count]
    pairs_ref, seg_ref = refs[count : count + 2]
    context_refs = refs[count + 2 : 2 * count + 2]
    lse_ref, rows_ref, context_ref, bias_ref, vt_ref, pvt_ref, ct_ref = refs[2 * count + 2 :]
    width = pairs_ref.shape[2]
    heads = width // head_dim
    blocks = 2 * count
    scaling = head_dim ** (-0.5)
    gather_rows(order_ref, packed_refs, rows_ref, block_rows)
    lane = lax.broadcasted_iota(jnp.int32, (1, width), 1) // head_dim
    prefix_bias = jnp.where(
        lax.broadcasted_iota(jnp.int32, (pairs_ref.shape[1], 1), 0) < prefix_len, 0.0, masked_value
    )
    prefix_keys = pairs_ref[0]
    pvt_ref[...] = jnp.transpose(pairs_ref[1].astype(f32)).astype(bf16)
    for index in range(blocks):
        vt_ref[index] = jnp.transpose(
            rows_ref[index * block_rows : (index + 1) * block_rows, 2 * width :].astype(f32)
        ).astype(bf16)
    for index in range(blocks):
        start = index * block_rows
        keys = key_blocks(index, block_rows)
        fill_bias(seg_ref, bias_ref, index, keys, block_rows)
        queries = rows_ref[pl.ds(start, block_rows), 0:width]

        def one_head(head, carry):
            query = jnp.where(lane == head, queries, 0.0) * jnp.asarray(scaling, bf16)
            span = pl.ds(pl.multiple_of(head * head_dim, head_dim), head_dim)
            prefix_scores = dot_nt(prefix_keys, query) + prefix_bias
            row_max = jnp.max(prefix_scores, axis=0, keepdims=True)
            scores = []
            for slot, key in enumerate(keys):
                rows = slice(key * block_rows, (key + 1) * block_rows)
                score = dot_nt(rows_ref[rows, width : 2 * width], query) + bias_ref[slot]
                row_max = jnp.maximum(row_max, jnp.max(score, axis=0, keepdims=True))
                scores.append(score)
            prefix_exp = jnp.exp(prefix_scores - row_max)
            row_sum = jnp.sum(prefix_exp, axis=0, keepdims=True)
            context = dot_nn(pvt_ref[span, :], prefix_exp.astype(bf16))
            for score, key in zip(scores, keys):
                exped = jnp.exp(score - row_max)
                row_sum = row_sum + jnp.sum(exped, axis=0, keepdims=True)
                context = context + dot_nn(vt_ref[key, span, :], exped.astype(bf16))
            ct_ref[span, :] = context * (1.0 / row_sum)
            lse_ref[pl.ds(head, 1), start : start + block_rows] = row_max + jnp.log(row_sum)
            return carry

        lax.fori_loop(0, heads, one_head, 0, unroll=True)
        context_ref[pl.ds(start, block_rows), :] = jnp.transpose(ct_ref[...]).astype(bf16)
    scatter_rows(order_ref, context_ref, context_refs, block_rows, slice(0, width))


def fill_bias(seg_ref, bias_ref, index, keys, block_rows):
    seg_query = seg_ref[0:1, index * block_rows : (index + 1) * block_rows]
    for slot, key in enumerate(keys):
        same = segment_column(seg_ref, key * block_rows, block_rows) == seg_query
        if key == index:
            shape = (block_rows, block_rows)
            same = same & (
                lax.broadcasted_iota(jnp.int32, shape, 0)
                <= lax.broadcasted_iota(jnp.int32, shape, 1)
            )
        bias_ref[slot] = jnp.where(same, 0.0, masked_value)


def attention_backward_kernel(count, block_rows, head_dim, prefix_len, order_ref, *refs):
    packed_refs = refs[:count]
    grad_refs = refs[count : 2 * count]
    pairs_ref, seg_ref, lse_ref = refs[2 * count : 2 * count + 3]
    out_refs = refs[2 * count + 3 : 3 * count + 3]
    prefix_out = refs[3 * count + 3]
    rows_ref, grad_ref, bias_ref, kt_ref, pkt_ref, dqt_ref, dq_ref, dk_ref, dv_ref = refs[
        3 * count + 4 :
    ]
    width = pairs_ref.shape[2]
    heads = width // head_dim
    blocks = 2 * count
    scaling = head_dim ** (-0.5)
    gather_rows(order_ref, packed_refs, rows_ref, block_rows)
    gather_rows(order_ref, grad_refs, grad_ref, block_rows)
    lane = lax.broadcasted_iota(jnp.int32, (1, width), 1) // head_dim
    prefix_bias = jnp.where(
        lax.broadcasted_iota(jnp.int32, (pairs_ref.shape[1], 1), 0) < prefix_len, 0.0, masked_value
    )
    prefix_keys, prefix_values = pairs_ref[0], pairs_ref[1]
    pkt_ref[...] = jnp.transpose(prefix_keys.astype(f32)).astype(bf16)
    dk_ref[...] = jnp.zeros_like(dk_ref)
    dv_ref[...] = jnp.zeros_like(dv_ref)
    prefix_out[...] = jnp.zeros_like(prefix_out)
    for index in range(blocks):
        kt_ref[index] = jnp.transpose(
            rows_ref[index * block_rows : (index + 1) * block_rows, width : 2 * width].astype(f32)
        ).astype(bf16)
    for index in range(blocks):
        start = index * block_rows
        keys = key_blocks(index, block_rows)
        fill_bias(seg_ref, bias_ref, index, keys, block_rows)
        queries = rows_ref[pl.ds(start, block_rows), 0:width]
        grads = grad_ref[pl.ds(start, block_rows), :]

        def one_head(head, carry):
            chosen = lane == head
            query = jnp.where(chosen, queries, 0.0) * jnp.asarray(scaling, bf16)
            grad = jnp.where(chosen, grads, 0.0)
            lse = lse_ref[pl.ds(head, 1), start : start + block_rows]
            span = pl.ds(pl.multiple_of(head * head_dim, head_dim), head_dim)
            prefix_prob = jnp.exp(dot_nt(prefix_keys, query) + prefix_bias - lse)
            prefix_dp = dot_nt(prefix_values, grad)
            delta = jnp.sum(prefix_prob * prefix_dp, axis=0, keepdims=True)
            probs, dps = [], []
            for slot, key in enumerate(keys):
                rows = slice(key * block_rows, (key + 1) * block_rows)
                prob = jnp.exp(
                    dot_nt(rows_ref[rows, width : 2 * width], query) + bias_ref[slot] - lse
                )
                dp = dot_nt(rows_ref[rows, 2 * width :], grad)
                delta = delta + jnp.sum(prob * dp, axis=0, keepdims=True)
                probs.append(prob)
                dps.append(dp)
            prefix_ds = (prefix_prob * (prefix_dp - delta)).astype(bf16)
            prefix_out[0] += dot_nn(prefix_ds, query)
            prefix_out[1] += dot_nn(prefix_prob.astype(bf16), grad)
            dqt = dot_nn(pkt_ref[span, :], prefix_ds)
            for prob, dp, key in zip(probs, dps, keys):
                rows = slice(key * block_rows, (key + 1) * block_rows)
                ds = (prob * (dp - delta)).astype(bf16)
                dk_ref[rows, :] += dot_nn(ds, query)
                dv_ref[rows, :] += dot_nn(prob.astype(bf16), grad)
                dqt = dqt + dot_nn(kt_ref[key, span, :], ds)
            dqt_ref[span, :] = dqt
            return carry

        lax.fori_loop(0, heads, one_head, 0, unroll=True)
        dq_ref[pl.ds(start, block_rows), :] = jnp.transpose(dqt_ref[...]) * scaling
    scatter_rows(order_ref, dq_ref, out_refs, block_rows, slice(0, width))
    scatter_rows(order_ref, dk_ref, out_refs, block_rows, slice(width, 2 * width))
    scatter_rows(order_ref, dv_ref, out_refs, block_rows, slice(2 * width, 3 * width))


def gelu_parts(values):
    root = 0.7978845608028654
    square = values * values
    curve = jnp.tanh(root * values * (1.0 + 0.044715 * square))
    return (square, curve, root)


def feed_forward_kernel(groups, per, with_output, with_grad, *refs):
    refs = list(refs)
    normed_own, normed_peer, bias_ref = refs[:3]
    del refs[:3]
    grad_own, grad_peer = (refs.pop(0), refs.pop(0)) if with_grad else (None, None)
    chunk_refs = refs[: per * groups]
    del refs[: per * groups]
    out_own, out_peer = (refs.pop(0), refs.pop(0)) if with_output else (None, None)
    back_own, back_peer = (refs.pop(0), refs.pop(0)) if with_grad else (None, None)
    weight_ref, sems, normed_ref, grad_ref, hidden_ref, back_ref = refs
    tokens, width = normed_own.shape
    hidden = bias_ref.shape[2]
    rows = hidden // per
    block = min(256, width)

    def copies_of(group):
        return [
            pltpu.make_async_copy(
                chunk_refs[per * group + part],
                weight_ref.at[pl.ds((per * group + part) * rows, rows)],
                sems.at[group, part],
            )
            for part in range(per)
        ]

    for group in range(min(2, groups)):
        for copy in copies_of(group):
            copy.start()
    normed_ref[0:tokens, :] = normed_own[...]
    normed_ref[tokens:, :] = normed_peer[...]
    if with_grad:
        grad_ref[0:tokens, :] = grad_own[...]
        grad_ref[tokens:, :] = grad_peer[...]
    @pl.loop(0, groups)
    def _(group):
        for part in range(per):
            pltpu.make_async_copy(
                chunk_refs[0], weight_ref.at[pl.ds(0, rows)], sems.at[group, part]
            ).wait()
        for later in range(2, groups):

            @pl.when(group == later - 2)
            def _():
                for copy in copies_of(later):
                    copy.start()

        span = pl.ds(pl.multiple_of(group * hidden, hidden), hidden)
        pre = dot_nt(normed_ref[...], weight_ref[span, 0:width]) + bias_ref[group]
        square, curve, root = gelu_parts(pre)
        if with_output:
            hidden_ref[group] = (0.5 * pre * (1.0 + curve)).astype(bf16)
        if with_grad:
            slope = 0.5 * (1.0 + curve) + 0.5 * pre * (1.0 - curve * curve) * (
                root * (1.0 + 3 * 0.044715 * square)
            )
            back_ref[group] = (dot_nt(grad_ref[...], weight_ref[span, width:]) * slope).astype(bf16)

    def summed(values_ref, columns):
        return sum(
            dot_nn(values_ref[group], weight_ref[group * hidden : (group + 1) * hidden, columns])
            for group in range(groups)
        )

    for at in range(0, width, block):
        span = slice(at, at + block)
        if with_output:
            total = summed(hidden_ref, slice(width + at, width + at + block))
            out_own[:, span] = total[0:tokens]
            out_peer[:, span] = total[tokens:].astype(bf16)
        if with_grad:
            total = summed(back_ref, span)
            back_own[:, span] = total[0:tokens]
            back_peer[:, span] = total[tokens:].astype(bf16)


def whole(memory_space=pltpu.VMEM):
    return pl.BlockSpec(memory_space=memory_space)


def attention_forward(order, packed, pairs, seg_row, head_dim, prefix_len):
    count = len(packed)
    block_rows = packed[0].shape[0] // 2
    width = packed[0].shape[1] // 3
    seq_len = seg_row.shape[1]
    slots = len(key_blocks(2 * count - 1, block_rows))
    results = pl.pallas_call(
        functools.partial(attention_forward_kernel, count, block_rows, head_dim, prefix_len),
        out_shape=[jax.ShapeDtypeStruct((2 * block_rows, width), bf16)] * count
        + [jax.ShapeDtypeStruct((stat_rows, seq_len), f32)],
        in_specs=[whole(pltpu.SMEM)] + [whole()] * (count + 2),
        out_specs=[whole()] * (count + 1),
        scratch_shapes=[
            pltpu.VMEM((seq_len, 3 * width), bf16),
            pltpu.VMEM((seq_len, width), bf16),
            pltpu.VMEM((slots, block_rows, block_rows), f32),
            pltpu.VMEM((2 * count, width, block_rows), bf16),
            pltpu.VMEM((width, pairs.shape[1]), bf16),
            pltpu.VMEM((width, block_rows), f32),
        ],
        compiler_params=pltpu.CompilerParams(vmem_limit_bytes=32 << 20),
        cost_estimate=small_cost,
        name="attention_forward",
    )(order, *packed, pairs, seg_row)
    return (results[:count], results[count])


def attention_backward(order, packed, grads, pairs, seg_row, lse, head_dim, prefix_len):
    count = len(packed)
    block_rows = packed[0].shape[0] // 2
    width = packed[0].shape[1] // 3
    seq_len = seg_row.shape[1]
    blocks = 2 * count
    slots = len(key_blocks(blocks - 1, block_rows))
    results = pl.pallas_call(
        functools.partial(attention_backward_kernel, count, block_rows, head_dim, prefix_len),
        out_shape=[jax.ShapeDtypeStruct((2 * block_rows, 3 * width), bf16)] * count
        + [jax.ShapeDtypeStruct(pairs.shape, f32)],
        in_specs=[whole(pltpu.SMEM)] + [whole()] * (2 * count + 3),
        out_specs=[whole()] * (count + 1),
        scratch_shapes=[
            pltpu.VMEM((seq_len, 3 * width), bf16),
            pltpu.VMEM((seq_len, width), bf16),
            pltpu.VMEM((slots, block_rows, block_rows), f32),
            pltpu.VMEM((blocks, width, block_rows), bf16),
            pltpu.VMEM((width, pairs.shape[1]), bf16),
            pltpu.VMEM((width, block_rows), f32),
            pltpu.VMEM((seq_len, width), f32),
            pltpu.VMEM((seq_len, width), f32),
            pltpu.VMEM((seq_len, width), f32),
        ],
        compiler_params=pltpu.CompilerParams(vmem_limit_bytes=32 << 20),
        cost_estimate=small_cost,
        name="attention_backward",
    )(order, *packed, *grads, pairs, seg_row, lse)
    return (results[:count], results[count])


def chunk_kernel(place_ref, up_ref, down_ref, keep_ref, give_ref, up, down, chunks, sems, out_sems):
    hidden, width = down.shape
    rows = hidden // 4
    core, parity = place_ref[0], place_ref[1]
    half = width // 2
    loads = []
    for at in range(2):
        span = pl.ds(at * half, half)
        loads.append(pltpu.make_async_copy(up_ref.at[span], up.at[span], sems.at[at]))
    for at in range(2):
        span = pl.ds(at * 2 * rows, 2 * rows)
        loads.append(pltpu.make_async_copy(down_ref.at[span], down.at[span], sems.at[2 + at]))
    for load in loads:
        load.start()
    spots = []
    for side in range(2):
        for which in range(2):
            spots.append(
                (1 - core if side else core, 1 - parity if which else parity, 2 * side + which)
            )
    for at in range(2):
        loads[at].wait()
        span = slice(at * half, (at + 1) * half)
        for side, slot, index in spots:
            chunks[side, slot, :, span] = jnp.transpose(up[span, index * rows : (index + 1) * rows])
    for at in range(2):
        loads[2 + at].wait()
        for side, slot, index in spots[2 * at : 2 * at + 2]:
            chunks[side, slot, :, width:] = down[index * rows : (index + 1) * rows, :]
    stores = [
        pltpu.make_async_copy(chunks.at[side], target, out_sems.at[side])
        for side, target in enumerate((keep_ref, give_ref))
    ]
    for store in stores:
        store.start()
    for store in stores:
        store.wait()


def feed_forward_chunks(place, up, down):
    hidden, width = down.shape
    shape = (2, hidden // 4, 2 * width)
    return pl.pallas_call(
        chunk_kernel,
        out_shape=[jax.ShapeDtypeStruct(shape, bf16)] * 2,
        in_specs=[whole(pltpu.SMEM), whole(pltpu.HBM), whole(pltpu.HBM)],
        out_specs=[whole(pltpu.HBM)] * 2,
        scratch_shapes=[
            pltpu.VMEM((width, hidden), bf16),
            pltpu.VMEM((hidden, width), bf16),
            pltpu.VMEM((2,) + shape, bf16),
            pltpu.SemaphoreType.DMA((4,)),
            pltpu.SemaphoreType.DMA((2,)),
        ],
        compiler_params=pltpu.CompilerParams(vmem_limit_bytes=20 << 20),
        cost_estimate=small_cost,
        name="feed_forward_chunks",
    )(place, up, down)


def feed_forward(normed, bias, chunks, grads, with_output, per):
    rows = chunks[0].shape[0]
    groups, hidden = (len(chunks) // per, per * rows)
    bias = bias.reshape(groups, 1, hidden)
    tokens, width = normed[0].shape
    with_grad = grads is not None
    kinds = with_output + with_grad
    small = (8, 128)
    return pl.pallas_call(
        functools.partial(feed_forward_kernel, groups, per, with_output, with_grad),
        out_shape=[
            jax.ShapeDtypeStruct((tokens, width), f32),
            jax.ShapeDtypeStruct((tokens, width), bf16),
        ]
        * kinds,
        in_specs=[whole()] * (3 + 2 * with_grad) + [whole(pltpu.HBM)] * len(chunks),
        out_specs=[whole()] * (2 * kinds),
        scratch_shapes=[
            pltpu.VMEM((groups * hidden, 2 * width), bf16),
            pltpu.SemaphoreType.DMA((groups, per)),
            pltpu.VMEM((2 * tokens, width), bf16),
            pltpu.VMEM((2 * tokens, width) if with_grad else small, bf16),
            pltpu.VMEM((groups, 2 * tokens, hidden) if with_output else small, bf16),
            pltpu.VMEM((groups, 2 * tokens, hidden) if with_grad else small, bf16),
        ],
        compiler_params=pltpu.CompilerParams(vmem_limit_bytes=58 << 20),
        cost_estimate=small_cost,
        name="feed_forward",
    )(*normed, bias, *(grads if with_grad else ()), *chunks)


def dot_tn(a, b):
    return lax.dot_general(a, b, (((0,), (0,)), ((), ())), preferred_element_type=f32)


def second_grad_kernel(head_dim, kept_ref, came_ref, hidden_ref, w2_ref, b2_ref):
    grad = (kept_ref[...] + came_ref[...]).astype(bf16)
    heads = w2_ref.shape[1]
    for head in range(heads):
        columns = [
            grad[:, (heads * side + head) * head_dim : (heads * side + head + 1) * head_dim]
            for side in range(2)
        ]
        block = jnp.concatenate(columns, axis=1)
        w2_ref[:, head, :] = dot_tn(hidden_ref[...], block)
        b2_ref[head : head + 1, :] = jnp.sum(block.astype(f32), axis=0, keepdims=True)


def second_grads(kept, came, hidden, heads):
    head_dim = kept.shape[1] // (2 * heads)
    return pl.pallas_call(
        functools.partial(second_grad_kernel, head_dim),
        out_shape=[
            jax.ShapeDtypeStruct((hidden.shape[1], heads, 2 * head_dim), f32),
            jax.ShapeDtypeStruct((heads, 2 * head_dim), f32),
        ],
        in_specs=[whole()] * 3,
        out_specs=[whole()] * 2,
        compiler_params=pltpu.CompilerParams(vmem_limit_bytes=8 << 20),
        cost_estimate=small_cost,
        name="second_grads",
    )(kept, came, hidden)


def first_grad_kernel(grad_ref, curve_ref, embed_ref, w1_ref, embed_out, w1_out, b1_out):
    curve = curve_ref[...]
    grad = (grad_ref[...] * (1.0 - curve * curve)).astype(bf16)
    w1_out[...] = dot_tn(embed_ref[...], grad)
    b1_out[...] = jnp.sum(grad.astype(f32), axis=0, keepdims=True)
    embed_out[...] = dot_nt(grad, w1_ref[...])[: embed_out.shape[0]]


def first_grads(grad, curve, embed, w1, prefix_len):
    return pl.pallas_call(
        first_grad_kernel,
        out_shape=[
            jax.ShapeDtypeStruct((prefix_len, embed.shape[1]), f32),
            jax.ShapeDtypeStruct(w1.shape, f32),
            jax.ShapeDtypeStruct((1, w1.shape[1]), f32),
        ],
        in_specs=[whole()] * 4,
        out_specs=[whole()] * 3,
        compiler_params=pltpu.CompilerParams(vmem_limit_bytes=12 << 20),
        cost_estimate=small_cost,
        name="first_grads",
    )(grad, curve, embed, w1)


def place_kernel(spot_ref, low_own, low_other, high_own, high_other, out_ref):
    row = spot_ref[1]

    @pl.when(spot_ref[0] == 0)
    def _():
        out_ref[row] = low_own[...]
        out_ref[1 - row] = low_other[...]

    @pl.when(spot_ref[0] == 1)
    def _():
        out_ref[row] = high_own[...]
        out_ref[1 - row] = high_other[...]


def place_rows(spot, *blocks):
    return pl.pallas_call(
        place_kernel,
        out_shape=jax.ShapeDtypeStruct((2,) + blocks[0].shape, bf16),
        in_specs=[whole(pltpu.SMEM)] + [whole()] * 4,
        out_specs=whole(),
        compiler_params=pltpu.CompilerParams(vmem_limit_bytes=8 << 20),
        cost_estimate=small_cost,
        name="place_rows",
    )(spot, *blocks)


def centered_values(values):
    centered = values - jnp.mean(values, axis=-1, keepdims=True)
    scale = lax.rsqrt(jnp.mean(centered * centered, axis=-1, keepdims=True) + epsilon)
    return (centered * scale, scale)


def layer_norm(values, ln_gain, ln_bias):
    return centered_values(values)[0] * ln_gain + ln_bias


def norm_back(values, ln_gain, grad_normed):
    unit, scale = centered_values(values)
    entry = grad_normed * ln_gain
    return scale * (
        entry
        - jnp.mean(entry, axis=-1, keepdims=True)
        - unit * jnp.mean(entry * unit, axis=-1, keepdims=True)
    )


class Group:
    def __init__(self, tensor_size):
        self.size = tensor_size
        self.count = tensor_size // 2

    def core_swap(self, value):
        return lax.ppermute(value, "section", [(0, 1), (1, 0)])

    def shift(self, value, distance):
        pairs = [
            (half * self.count + place, half * self.count + (place + distance) % self.count)
            for half in range(2)
            for place in range(self.count)
        ]
        return lax.ppermute(value, "tensor", pairs)

    def cross(self, value):
        size, count = self.size, self.count
        pairs = [
            (core * size + place, (1 - core) * size + (place + count) % size)
            for core in range(2)
            for place in range(size)
        ]
        return lax.ppermute(value, ("section", "tensor"), pairs)

    def half_swap(self, value):
        pairs = [(place, (place + self.count) % self.size) for place in range(self.size)]
        return lax.ppermute(value, "tensor", pairs)

    def plane_swap(self, value, distance=1):
        planes = lax.axis_size("dp")
        pairs = [(plane, plane ^ distance) for plane in range(planes)]
        return lax.ppermute(value, "dp", pairs)

    def cross_from(self, value, core):
        size, count = self.size, self.count
        pairs = [
            (core * size + place, (1 - core) * size + (place + count) % size)
            for place in range(size)
        ]
        return lax.ppermute(value, ("section", "tensor"), pairs)

    def sum_planes(self, value):
        planes = lax.axis_size("dp")
        if planes & (planes - 1):
            return lax.psum(value, "dp")
        step = min(planes, 4)
        value = sum([value] + [self.plane_swap(value, distance) for distance in range(1, step)])
        distance = step
        while distance < planes:
            value = value + self.plane_swap(value, distance)
            distance *= 2
        return value

    def tensor_swap(self, value, distance):
        pairs = [(place, place ^ distance) for place in range(self.size)]
        return lax.ppermute(value, "tensor", pairs)

    def sum_shards(self, value):
        if self.size & (self.size - 1):
            return lax.psum(value, ("section", "tensor"))
        value = value + self.core_swap(value)
        step = min(self.size, 4)
        value = sum([value] + [self.tensor_swap(value, distance) for distance in range(1, step)])
        distance = step
        while distance < self.size:
            value = value + self.tensor_swap(value, distance)
            distance *= 2
        return value

    def shifts(self, stages, block):
        return [
            stages.send(functools.partial(self.shift, distance=distance), block)
            for distance in range(1, self.count)
        ]

    def paired(self, blocks):
        return [jnp.concatenate([part, self.core_swap(part)], axis=0) for part in blocks]

    def gather(self, stages, block):
        return self.paired([block] + self.shifts(stages, block))

    def scatter(self, stages, parts):
        rows = parts[0].shape[0] // 2
        total = None
        for distance in list(range(1, self.count)) + [0]:
            own, other = (parts[distance][:rows], parts[distance][rows:])
            if total is not None:
                other = lax.optimization_barrier((other, leaving))[0]
            self.swapped = self.core_swap(other)
            summed = own.astype(f32) + self.swapped.astype(f32)
            if distance:
                back = functools.partial(self.shift, distance=-distance)
                leaving = summed.astype(bf16)
                summed = stages.send(back, leaving).astype(f32)
            total = summed if total is None else total + summed
        return total


class Stages:
    def __init__(self):
        self.before, self.now = ([], [])

    def send(self, transfer, value):
        if self.before:
            value = lax.optimization_barrier((value, *self.before))[0]
        self.now.append(transfer(value))
        return self.now[-1]

    def next(self):
        self.before, self.now = (self.now, [])


def local(
    boundary,
    seg_ids,
    ln1_gain,
    ln1_bias,
    w_qkv,
    b_qkv,
    w_out,
    b_out,
    ln2_gain,
    ln2_bias,
    w_up,
    b_up,
    w_down,
    b_down,
    prefix_embed,
    reparam_w1,
    reparam_b1,
    reparam_w2,
    reparam_b2,
):
    core = lax.axis_index("section")
    place = lax.axis_index("tensor")
    group = Group(lax.axis_size("tensor"))
    count = group.count
    tok_rows, width = boundary.shape[2:]
    heads_local = w_qkv.shape[2]
    head_dim = w_qkv.shape[3] // 3
    head_width = heads_local * head_dim
    prefix_len = prefix_embed.shape[0]
    row = place // count
    low = core == 0

    def tied(value, *others):
        return lax.optimization_barrier((value,) + others)[0]

    stages = Stages()
    steps = range(1, count)

    own_row = lax.dynamic_index_in_dim(boundary[0], row, 0, False)
    other_row = lax.dynamic_index_in_dim(boundary[0], 1 - row, 0, False)
    came_row = stages.send(functools.partial(group.cross_from, core=0), other_row)
    inputs = jnp.where(low, own_row, came_row).astype(f32)
    proj_own = w_out.reshape(head_width, width)

    def layer_pair(own, far):
        return (jnp.where(low, own, far), jnp.where(low, far, own))


    def as_rows(value):
        value = value.reshape(-1, value.shape[-1])
        return jnp.pad(value, ((0, 0), (0, width - value.shape[1])))

    b_qkv_own = b_qkv.reshape(heads_local, 3, head_dim).transpose(1, 0, 2).reshape(1, 3 * head_width)
    small_parts = (ln1_gain, ln1_bias, b_out, ln2_gain, ln2_bias, b_down, b_up, b_up)
    small_own = jnp.concatenate([as_rows(part) for part in small_parts], axis=0)

    def on_chip(value):
        peer = group.core_swap(value)
        return jnp.stack([jnp.where(low, value, peer), jnp.where(low, peer, value)])

    small_chip = on_chip(small_own)

    def vectors_of(layer):
        return small_chip[layer, :8].astype(f32)

    def normed_one(layer, values):
        vectors = vectors_of(layer)
        return layer_norm(values, vectors[0:1], vectors[1:2]).astype(bf16)

    hidden_width = w_up.shape[2]
    rows = hidden_width // 4
    shared = lax.axis_size("dp") % 2 == 0
    parity = lax.axis_index("dp") % 2
    spot = jnp.stack([core, parity]).astype(jnp.int32)
    keep, give = feed_forward_chunks(tied(spot, other_row), w_up[0], w_down[0])
    handed = group.core_swap(give)
    even_0 = jnp.where(low, keep[0], handed[0])
    later_keep, later_handed, _ = lax.optimization_barrier((keep, handed, even_0))
    even = [even_0, jnp.where(low, later_handed[0], later_keep[0])]
    odd = [
        jnp.where(low, later_keep[1], later_handed[1]),
        jnp.where(low, later_handed[1], later_keep[1]),
    ]

    prefix_pre = dot_nn(tied(prefix_embed, even[0]), reparam_w1) + reparam_b1.astype(f32)
    curve = jnp.tanh(prefix_pre)
    hidden_low = curve.astype(bf16)
    w2_own = (
        tied(reparam_w2, even[0])
        .reshape(reparam_w2.shape[0], heads_local, 2, head_dim)
        .transpose(0, 2, 1, 3)
        .reshape(reparam_w2.shape[0], 2 * head_width)
    )
    b2_own = (
        reparam_b2.reshape(heads_local, 2, head_dim).transpose(1, 0, 2).reshape(2 * head_width)
    )
    prefix_own = (dot_nn(hidden_low, w2_own) + b2_own.astype(f32)).astype(bf16)
    pairs_own = jnp.concatenate(
        [
            jnp.pad(value, ((0, prefix_rows - value.shape[0]), (0, width - value.shape[1])))
            for value in (prefix_own[:, :head_width], prefix_own[:, head_width:], b_qkv_own)
        ],
        axis=0,
    )
    qkv_own = (
        w_qkv.reshape(width, heads_local, 3, head_dim)
        .transpose(0, 2, 1, 3)
        .reshape(width, 3 * head_width)
    )

    def plane_send(value):
        return stages.send(group.plane_swap, value)

    def half_send(value):
        return stages.send(group.half_swap, value)

    def far(value, layer):
        return stages.send(functools.partial(group.cross_from, core=layer), value)

    side_bias = small_chip[:, 6, : w_up.shape[2]]
    side_bias = jnp.stack([side_bias] + group.shifts(stages, side_bias), axis=1)

    stages.next()
    half_bias = half_send(side_bias)
    normed_0 = normed_one(0, inputs)
    gathered_0 = [normed_0] + group.shifts(stages, normed_0)
    side_even_0 = group.shifts(stages, tied(even[0], *gathered_0[1:]))
    qkv_far = stages.send(group.cross, tied(qkv_own, half_bias))

    stages.next()
    pairs = layer_pair(pairs_own, stages.send(group.cross, pairs_own))
    proj_far_0 = far(proj_own, 0)
    half_even_0 = half_send(even[0])
    side_even_1 = group.shifts(stages, even[1])
    if shared:
        side_odd_0 = [plane_send(value) for value in side_even_0]
    else:
        side_odd_0 = group.shifts(stages, odd[0])

    def all_chunks(layer, half, side, corner):
        chunks = [even[layer], odd[layer], *half]
        for at in range(count - 1):
            chunks += [side[0][at], side[1][at], corner[0][at], corner[1][at]]
        return chunks

    seg_row = lax.dynamic_index_in_dim(seg_ids, row, 0, True).astype(f32)
    chip = place % count
    orders = [
        jnp.stack(
            [
                jnp.bitwise_xor(row, jnp.bitwise_xor(core, swapped ^ layer)) * count
                + (chip - distance + count) % count
                for distance in range(count)
                for swapped in range(2)
            ]
        ).astype(jnp.int32)
        for layer in range(2)
    ]

    class Layer:
        def __init__(self, index, qkv):
            self.vectors = vectors_of(index)
            self.ln1_gain, self.ln1_bias, self.b_out = [self.vectors[at : at + 1] for at in range(3)]
            shard = pairs[index]
            self.pairs = shard[: 2 * prefix_rows, :head_width].reshape(2, prefix_rows, head_width)
            self.b_qkv = shard[2 * prefix_rows : 2 * prefix_rows + 1, : 3 * head_width].astype(f32)
            self.order = orders[index]
            self.qkv = tied(qkv, *stages.before)

        def attention(self, inputs, gathered):
            self.inputs = inputs
            gathered = lax.optimization_barrier((*gathered, *stages.before))[:count]
            self.packed = [
                (dot_nn(part, self.qkv) + self.b_qkv).astype(bf16)
                for part in group.paired(gathered)
            ]
            self.context, self.lse = attention_forward(
                self.order, self.packed, self.pairs, seg_row, head_dim, prefix_len
            )

        def project(self):
            context = lax.optimization_barrier((*self.context, *stages.before))[:count]
            own, far_own = lax.optimization_barrier((*self.far_out, *self.context))[:2]
            self.out = jnp.where(low, own, far_own)
            parts = [dot_nn(part, self.out).astype(bf16) for part in context]
            self.middle = self.inputs + (group.scatter(stages, parts) + self.b_out)

        def project_here(self):
            context = lax.optimization_barrier((*self.context, *stages.before))[:count]
            branch = dot_nn(context[0], self.out)
            for distance in steps:
                came = group.shift(context[distance], -distance)
                branch = branch + dot_nn(came, self.out_side[distance - 1])
            rows = branch.shape[0] // 2
            own, peer = (branch[:rows], branch[rows:].astype(bf16))
            self.middle = self.inputs + (self.shared((own, peer)) + self.b_out)

        def norm_two(self, values):
            return layer_norm(values, self.vectors[3:4], self.vectors[4:5]).astype(bf16)

        def shared(self, *pairs):
            return sum([own + group.core_swap(peer).astype(f32) for own, peer in pairs])

        def output(self, middle, *pairs):
            return (middle + (self.shared(*pairs) + self.vectors[5:6])).astype(bf16)

        def middle_back(self, grad_out, *pairs):
            branch = self.shared(*pairs)
            return grad_out.astype(f32) + norm_back(self.middle, self.vectors[3:4], branch)

        def feed_forward(self, normed, grads, with_output):
            return feed_forward(normed, self.bias, self.chunks, grads, with_output, 2)

        def backward(self, grad_middle):
            stages.before = []
            grad_branch = grad_middle.astype(bf16)
            (grad_chip,) = group.paired([grad_branch])
            sides = [dot_nt(grad_chip, side).astype(bf16) for side in self.out_side]
            came = [group.shift(side, at + 1) for at, side in enumerate(sides)]
            grads = [dot_nt(grad_chip, self.out).astype(bf16)] + came
            grad_packed, grad_pairs = attention_backward(
                self.order, self.packed, grads, self.pairs, seg_row, self.lse, head_dim, prefix_len
            )
            parts = [dot_nt(part, self.qkv).astype(bf16) for part in grad_packed]
            grad_normed = group.scatter(stages, parts)
            grad_in = grad_middle + norm_back(self.inputs, self.ln1_gain, grad_normed)
            return (grad_in.astype(bf16), grad_pairs)

    pack_own = jnp.concatenate([proj_own, other_row], axis=0)
    layer_0 = Layer(0, tied(jnp.where(low, qkv_own, qkv_far), pack_own))
    layer_0.far_out = (proj_own, proj_far_0)
    layer_0.attention(inputs, gathered_0)

    stages.next()
    corner_even_0 = group.shifts(stages, half_even_0)
    half_even_1 = half_send(even[1])
    far_pack = far(pack_own, 1)
    if shared:
        side_odd_1 = [plane_send(value) for value in side_even_1]
    else:
        side_odd_1 = group.shifts(stages, odd[1])
    layer_0.project()

    stages.next()
    half_odd_0 = half_send(odd[0])
    if shared:
        corner_odd_0 = [plane_send(value) for value in corner_even_0]
    else:
        corner_odd_0 = group.shifts(stages, half_odd_0)
    corner_even_1 = group.shifts(stages, half_even_1)
    up_bias = jnp.stack([side_bias, half_bias], axis=2).astype(f32)
    up_bias = up_bias.reshape(2, 2 * count, 2, 2, rows)
    up_bias = jnp.where(low, up_bias[:, :, 0], up_bias[:, :, 1])
    up_bias = jnp.where(parity == 0, up_bias, up_bias[:, :, ::-1])
    up_bias = up_bias.reshape(2, 4 * count, rows)
    layer_0.bias = up_bias[0]
    layer_0.chunks = all_chunks(
        0,
        (half_even_0, half_odd_0),
        (side_even_0, side_odd_0),
        (corner_even_0, corner_odd_0),
    )
    middle_peer = group.core_swap(layer_0.middle)
    normed_pair = (layer_0.norm_two(layer_0.middle), layer_0.norm_two(middle_peer))

    stages.next()
    half_odd_1 = half_send(odd[1])
    own_proj, far_pack = lax.optimization_barrier((proj_own, far_pack, *stages.before))[:2]
    cotangent = jnp.where(low, far_pack[head_width:], own_row)
    proj_1 = jnp.where(low, far_pack[:head_width], own_proj)
    projs = (layer_0.out, proj_1)
    if shared:
        corner_odd_1 = [plane_send(value) for value in corner_even_1]
    else:
        corner_odd_1 = group.shifts(stages, half_odd_1)
    out_sides = [
        [stages.send(functools.partial(group.shift, distance=-distance), proj) for distance in steps]
        for proj in projs
    ]
    normed_swapped = (tied(normed_pair[1], *stages.before), normed_pair[0])
    out_kept, out_sent = layer_0.feed_forward(normed_swapped, None, True)
    first_out = layer_0.output(middle_peer, (out_kept, tied(out_sent, *stages.now)))
    inputs_1 = first_out.astype(f32)
    normed_1 = normed_one(1, inputs_1)
    gathered_1 = [normed_1] + group.shifts(stages, normed_1)
    w2_far = group.cross(tied(w2_own, first_out))
    layer_1 = Layer(1, jnp.where(low, *lax.optimization_barrier((qkv_far, qkv_own, w2_far))[:2]))
    layer_0.out_side, layer_1.out_side = out_sides
    layer_1.out = proj_1
    layer_1.bias = up_bias[1]
    layer_1.attention(inputs_1, gathered_1)
    layer_1.chunks = all_chunks(
        1,
        (half_even_1, half_odd_1),
        (side_even_1, side_odd_1),
        (corner_even_1, corner_odd_1),
    )

    stages.next()
    w2_side = layer_pair(w2_own, w2_far)
    layer_1.project_here()
    normed = layer_1.norm_two(layer_1.middle)
    normed = (normed, group.core_swap(normed))
    cotangents = (cotangent, group.core_swap(cotangent))
    parts = layer_1.feed_forward(normed, cotangents, True)
    last_out = layer_1.output(layer_1.middle, parts[:2])
    grad_middle = layer_1.middle_back(cotangent, parts[2:])
    mid_grad, grad_pairs_one = layer_1.backward(grad_middle)
    high_other = group.cross_from(last_out, 0)
    mid_grad = tied(mid_grad, high_other)
    mid_peer = group.core_swap(mid_grad)
    back_part = layer_0.feed_forward(normed_pair, (mid_peer, mid_grad), False)
    grad_middle = layer_0.middle_back(mid_peer, back_part)
    first_grad, grad_pairs_zero = layer_0.backward(grad_middle)

    low_other = group.cross_from(first_grad, 1)
    spot = jnp.stack([core, row]).astype(jnp.int32)
    boundary_result = place_rows(spot, first_grad, low_other, last_out, high_other)[None]

    def joined(pairs):
        return jnp.concatenate([pairs[0], pairs[1]], axis=1)

    grads = (joined(grad_pairs_zero), joined(grad_pairs_one))
    hidden_part = sum(
        lax.dot_general(
            grad,
            side.astype(f32),
            (((1,), (1,)), ((), ())),
            precision=lax.Precision.HIGHEST,
            preferred_element_type=f32,
        )
        for grad, side in zip(grads, w2_side)
    )
    kept, sent = layer_pair(*grads)
    message = jnp.concatenate([hidden_part, kept, sent], axis=1)
    summed = tied(message, group.swapped)
    summed = group.sum_planes(summed)
    hidden_width = hidden_part.shape[1]
    hidden_part = summed[:, :hidden_width]
    hidden_grad = group.sum_shards(hidden_part)
    kept = summed[:, hidden_width : hidden_width + 2 * head_width]
    sent = summed[:, hidden_width + 2 * head_width :]
    pad = ((0, prefix_rows - prefix_len), (0, 0))
    w2_grad, b2_grad = second_grads(kept, group.cross(sent), jnp.pad(hidden_low, pad), heads_local)
    embed_grad, w1_grad, b1_grad = first_grads(
        hidden_grad, jnp.pad(curve, pad), jnp.pad(prefix_embed, pad), reparam_w1, prefix_len
    )
    return (
        boundary_result,
        embed_grad,
        w1_grad,
        b1_grad.reshape(reparam_b1.shape),
        w2_grad.reshape(reparam_w2.shape),
        b2_grad.reshape(reparam_b2.shape),
    )


def solution(mesh):
    return jax.shard_map(
        local,
        mesh=mesh,
        in_specs=(
            P("section", "dp", "tensor", None),
            P("dp", None),
            P("section", None),
            P("section", None),
            P("section", None, "tensor", None),
            P("section", "tensor", None),
            P("section", "tensor", None, None),
            P("section", None),
            P("section", None),
            P("section", None),
            P("section", None, "tensor"),
            P("section", "tensor"),
            P("section", "tensor", None),
            P("section", None),
            P(),
            P(),
            P(),
            P(None, "section", "tensor", None),
            P("section", "tensor", None),
        ),
        out_specs=(
            P("section", "dp", "tensor", None),
            P(),
            P(),
            P(),
            P(None, "section", "tensor", None),
            P("section", "tensor", None),
        ),
        check_vma=False,
    )
```

```python
import functools

import jax
import jax.numpy as jnp
from jax import lax
from jax.experimental import pallas as pl
from jax.experimental.pallas import tpu as pltpu
from jax.sharding import PartitionSpec as P

epsilon = 1e-05
masked_value = -1e30
max_segment = 512
prefix_rows = 16
stat_rows = 8
f32 = jnp.float32
bf16 = jnp.bfloat16


small_cost = pl.CostEstimate(flops=1, bytes_accessed=1, transcendentals=0)


def dot_nn(a, b):
    return lax.dot_general(a, b, (((1,), (0,)), ((), ())), preferred_element_type=f32)


def dot_nt(a, b):
    return lax.dot_general(a, b, (((1,), (1,)), ((), ())), preferred_element_type=f32)


def key_blocks(index, block_rows):
    reach = -(-(max_segment - 1) // block_rows)
    return list(range(max(0, index - reach), index + 1))


def gather_rows(order_ref, sources, target_ref, block_rows):
    for place in range(2 * len(sources)):
        start = pl.multiple_of(order_ref[place] * block_rows, block_rows)
        target_ref[pl.ds(start, block_rows), :] = sources[place // 2][
            pl.ds((place % 2) * block_rows, block_rows), :
        ]


def scatter_rows(order_ref, source_ref, targets, block_rows, columns):
    for place in range(2 * len(targets)):
        start = pl.multiple_of(order_ref[place] * block_rows, block_rows)
        targets[place // 2][pl.ds((place % 2) * block_rows, block_rows), columns] = source_ref[
            pl.ds(start, block_rows), :
        ].astype(targets[place // 2].dtype)


def segment_column(seg_ref, start, rows):
    row = seg_ref[0:1, start : start + rows]
    return jnp.transpose(jnp.broadcast_to(row, (128, rows)))[:, 0:1]


def attention_forward_kernel(count, block_rows, head_dim, prefix_len, order_ref, *refs):
    packed_refs = refs[:count]
    pairs_ref, seg_ref = refs[count : count + 2]
    context_refs = refs[count + 2 : 2 * count + 2]
    lse_ref, rows_ref, context_ref, bias_ref, vt_ref, pvt_ref, ct_ref = refs[2 * count + 2 :]
    width = pairs_ref.shape[2]
    heads = width // head_dim
    blocks = 2 * count
    scaling = head_dim ** (-0.5)
    gather_rows(order_ref, packed_refs, rows_ref, block_rows)
    lane = lax.broadcasted_iota(jnp.int32, (1, width), 1) // head_dim
    prefix_bias = jnp.where(
        lax.broadcasted_iota(jnp.int32, (pairs_ref.shape[1], 1), 0) < prefix_len, 0.0, masked_value
    )
    prefix_keys = pairs_ref[0]
    pvt_ref[...] = jnp.transpose(pairs_ref[1].astype(f32)).astype(bf16)
    for index in range(blocks):
        vt_ref[index] = jnp.transpose(
            rows_ref[index * block_rows : (index + 1) * block_rows, 2 * width :].astype(f32)
        ).astype(bf16)
    for index in range(blocks):
        start = index * block_rows
        keys = key_blocks(index, block_rows)
        fill_bias(seg_ref, bias_ref, index, keys, block_rows)
        queries = rows_ref[pl.ds(start, block_rows), 0:width]

        def one_head(head, carry):
            query = jnp.where(lane == head, queries, 0.0) * jnp.asarray(scaling, bf16)
            span = pl.ds(pl.multiple_of(head * head_dim, head_dim), head_dim)
            prefix_scores = dot_nt(prefix_keys, query) + prefix_bias
            row_max = jnp.max(prefix_scores, axis=0, keepdims=True)
            scores = []
            for slot, key in enumerate(keys):
                rows = slice(key * block_rows, (key + 1) * block_rows)
                score = dot_nt(rows_ref[rows, width : 2 * width], query) + bias_ref[slot]
                row_max = jnp.maximum(row_max, jnp.max(score, axis=0, keepdims=True))
                scores.append(score)
            prefix_exp = jnp.exp(prefix_scores - row_max)
            row_sum = jnp.sum(prefix_exp, axis=0, keepdims=True)
            context = dot_nn(pvt_ref[span, :], prefix_exp.astype(bf16))
            for score, key in zip(scores, keys):
                exped = jnp.exp(score - row_max)
                row_sum = row_sum + jnp.sum(exped, axis=0, keepdims=True)
                context = context + dot_nn(vt_ref[key, span, :], exped.astype(bf16))
            ct_ref[span, :] = context * (1.0 / row_sum)
            lse_ref[pl.ds(head, 1), start : start + block_rows] = row_max + jnp.log(row_sum)
            return carry

        lax.fori_loop(0, heads, one_head, 0, unroll=True)
        context_ref[pl.ds(start, block_rows), :] = jnp.transpose(ct_ref[...]).astype(bf16)
    scatter_rows(order_ref, context_ref, context_refs, block_rows, slice(0, width))


def fill_bias(seg_ref, bias_ref, index, keys, block_rows):
    seg_query = seg_ref[0:1, index * block_rows : (index + 1) * block_rows]
    for slot, key in enumerate(keys):
        same = segment_column(seg_ref, key * block_rows, block_rows) == seg_query
        if key == index:
            shape = (block_rows, block_rows)
            same = same & (
                lax.broadcasted_iota(jnp.int32, shape, 0)
                <= lax.broadcasted_iota(jnp.int32, shape, 1)
            )
        bias_ref[slot] = jnp.where(same, 0.0, masked_value)


def attention_backward_kernel(count, block_rows, head_dim, prefix_len, order_ref, *refs):
    packed_refs = refs[:count]
    grad_refs = refs[count : 2 * count]
    pairs_ref, seg_ref, lse_ref = refs[2 * count : 2 * count + 3]
    out_refs = refs[2 * count + 3 : 3 * count + 3]
    prefix_out = refs[3 * count + 3]
    rows_ref, grad_ref, bias_ref, kt_ref, pkt_ref, dqt_ref, dq_ref, dk_ref, dv_ref = refs[
        3 * count + 4 :
    ]
    width = pairs_ref.shape[2]
    heads = width // head_dim
    blocks = 2 * count
    scaling = head_dim ** (-0.5)
    gather_rows(order_ref, packed_refs, rows_ref, block_rows)
    gather_rows(order_ref, grad_refs, grad_ref, block_rows)
    lane = lax.broadcasted_iota(jnp.int32, (1, width), 1) // head_dim
    prefix_bias = jnp.where(
        lax.broadcasted_iota(jnp.int32, (pairs_ref.shape[1], 1), 0) < prefix_len, 0.0, masked_value
    )
    prefix_keys, prefix_values = pairs_ref[0], pairs_ref[1]
    pkt_ref[...] = jnp.transpose(prefix_keys.astype(f32)).astype(bf16)
    dk_ref[...] = jnp.zeros_like(dk_ref)
    dv_ref[...] = jnp.zeros_like(dv_ref)
    prefix_out[...] = jnp.zeros_like(prefix_out)
    for index in range(blocks):
        kt_ref[index] = jnp.transpose(
            rows_ref[index * block_rows : (index + 1) * block_rows, width : 2 * width].astype(f32)
        ).astype(bf16)
    for index in range(blocks):
        start = index * block_rows
        keys = key_blocks(index, block_rows)
        fill_bias(seg_ref, bias_ref, index, keys, block_rows)
        queries = rows_ref[pl.ds(start, block_rows), 0:width]
        grads = grad_ref[pl.ds(start, block_rows), :]

        def one_head(head, carry):
            chosen = lane == head
            query = jnp.where(chosen, queries, 0.0) * jnp.asarray(scaling, bf16)
            grad = jnp.where(chosen, grads, 0.0)
            lse = lse_ref[pl.ds(head, 1), start : start + block_rows]
            span = pl.ds(pl.multiple_of(head * head_dim, head_dim), head_dim)
            prefix_prob = jnp.exp(dot_nt(prefix_keys, query) + prefix_bias - lse)
            prefix_dp = dot_nt(prefix_values, grad)
            delta = jnp.sum(prefix_prob * prefix_dp, axis=0, keepdims=True)
            probs, dps = [], []
            for slot, key in enumerate(keys):
                rows = slice(key * block_rows, (key + 1) * block_rows)
                prob = jnp.exp(
                    dot_nt(rows_ref[rows, width : 2 * width], query) + bias_ref[slot] - lse
                )
                dp = dot_nt(rows_ref[rows, 2 * width :], grad)
                delta = delta + jnp.sum(prob * dp, axis=0, keepdims=True)
                probs.append(prob)
                dps.append(dp)
            prefix_ds = (prefix_prob * (prefix_dp - delta)).astype(bf16)
            prefix_out[0] += dot_nn(prefix_ds, query)
            prefix_out[1] += dot_nn(prefix_prob.astype(bf16), grad)
            dqt = dot_nn(pkt_ref[span, :], prefix_ds)
            for prob, dp, key in zip(probs, dps, keys):
                rows = slice(key * block_rows, (key + 1) * block_rows)
                ds = (prob * (dp - delta)).astype(bf16)
                dk_ref[rows, :] += dot_nn(ds, query)
                dv_ref[rows, :] += dot_nn(prob.astype(bf16), grad)
                dqt = dqt + dot_nn(kt_ref[key, span, :], ds)
            dqt_ref[span, :] = dqt
            return carry

        lax.fori_loop(0, heads, one_head, 0, unroll=True)
        dq_ref[pl.ds(start, block_rows), :] = jnp.transpose(dqt_ref[...]) * scaling
    scatter_rows(order_ref, dq_ref, out_refs, block_rows, slice(0, width))
    scatter_rows(order_ref, dk_ref, out_refs, block_rows, slice(width, 2 * width))
    scatter_rows(order_ref, dv_ref, out_refs, block_rows, slice(2 * width, 3 * width))


def gelu_parts(values):
    root = 0.7978845608028654
    square = values * values
    curve = jnp.tanh(root * values * (1.0 + 0.044715 * square))
    return (square, curve, root)


def feed_forward_kernel(groups, per, with_output, with_grad, *refs):
    refs = list(refs)
    normed_own, normed_peer, bias_ref = refs[:3]
    del refs[:3]
    grad_own, grad_peer = (refs.pop(0), refs.pop(0)) if with_grad else (None, None)
    chunk_refs = refs[: per * groups]
    del refs[: per * groups]
    out_own, out_peer = (refs.pop(0), refs.pop(0)) if with_output else (None, None)
    back_own, back_peer = (refs.pop(0), refs.pop(0)) if with_grad else (None, None)
    weight_ref, sems, normed_ref, grad_ref, hidden_ref, back_ref = refs
    tokens, width = normed_own.shape
    hidden = bias_ref.shape[2]
    rows = hidden // per
    block = min(256, width)

    def copies_of(group):
        return [
            pltpu.make_async_copy(
                chunk_refs[per * group + part],
                weight_ref.at[pl.ds((per * group + part) * rows, rows)],
                sems.at[group, part],
            )
            for part in range(per)
        ]

    for group in range(min(2, groups)):
        for copy in copies_of(group):
            copy.start()
    normed_ref[0:tokens, :] = normed_own[...]
    normed_ref[tokens:, :] = normed_peer[...]
    if with_grad:
        grad_ref[0:tokens, :] = grad_own[...]
        grad_ref[tokens:, :] = grad_peer[...]
    @pl.loop(0, groups)
    def _(group):
        for part in range(per):
            pltpu.make_async_copy(
                chunk_refs[0], weight_ref.at[pl.ds(0, rows)], sems.at[group, part]
            ).wait()
        for later in range(2, groups):

            @pl.when(group == later - 2)
            def _():
                for copy in copies_of(later):
                    copy.start()

        span = pl.ds(pl.multiple_of(group * hidden, hidden), hidden)
        pre = dot_nt(normed_ref[...], weight_ref[span, 0:width]) + bias_ref[group]
        square, curve, root = gelu_parts(pre)
        if with_output:
            hidden_ref[group] = (0.5 * pre * (1.0 + curve)).astype(bf16)
        if with_grad:
            slope = 0.5 * (1.0 + curve) + 0.5 * pre * (1.0 - curve * curve) * (
                root * (1.0 + 3 * 0.044715 * square)
            )
            back_ref[group] = (dot_nt(grad_ref[...], weight_ref[span, width:]) * slope).astype(bf16)

    def summed(values_ref, columns):
        return sum(
            dot_nn(values_ref[group], weight_ref[group * hidden : (group + 1) * hidden, columns])
            for group in range(groups)
        )

    for at in range(0, width, block):
        span = slice(at, at + block)
        if with_output:
            total = summed(hidden_ref, slice(width + at, width + at + block))
            out_own[:, span] = total[0:tokens]
            out_peer[:, span] = total[tokens:].astype(bf16)
        if with_grad:
            total = summed(back_ref, span)
            back_own[:, span] = total[0:tokens]
            back_peer[:, span] = total[tokens:].astype(bf16)


def whole(memory_space=pltpu.VMEM):
    return pl.BlockSpec(memory_space=memory_space)


def attention_forward(order, packed, pairs, seg_row, head_dim, prefix_len):
    count = len(packed)
    block_rows = packed[0].shape[0] // 2
    width = packed[0].shape[1] // 3
    seq_len = seg_row.shape[1]
    slots = len(key_blocks(2 * count - 1, block_rows))
    results = pl.pallas_call(
        functools.partial(attention_forward_kernel, count, block_rows, head_dim, prefix_len),
        out_shape=[jax.ShapeDtypeStruct((2 * block_rows, width), bf16)] * count
        + [jax.ShapeDtypeStruct((stat_rows, seq_len), f32)],
        in_specs=[whole(pltpu.SMEM)] + [whole()] * (count + 2),
        out_specs=[whole()] * (count + 1),
        scratch_shapes=[
            pltpu.VMEM((seq_len, 3 * width), bf16),
            pltpu.VMEM((seq_len, width), bf16),
            pltpu.VMEM((slots, block_rows, block_rows), f32),
            pltpu.VMEM((2 * count, width, block_rows), bf16),
            pltpu.VMEM((width, pairs.shape[1]), bf16),
            pltpu.VMEM((width, block_rows), f32),
        ],
        compiler_params=pltpu.CompilerParams(vmem_limit_bytes=32 << 20),
        cost_estimate=small_cost,
        name="attention_forward",
    )(order, *packed, pairs, seg_row)
    return (results[:count], results[count])


def attention_backward(order, packed, grads, pairs, seg_row, lse, head_dim, prefix_len):
    count = len(packed)
    block_rows = packed[0].shape[0] // 2
    width = packed[0].shape[1] // 3
    seq_len = seg_row.shape[1]
    blocks = 2 * count
    slots = len(key_blocks(blocks - 1, block_rows))
    results = pl.pallas_call(
        functools.partial(attention_backward_kernel, count, block_rows, head_dim, prefix_len),
        out_shape=[jax.ShapeDtypeStruct((2 * block_rows, 3 * width), bf16)] * count
        + [jax.ShapeDtypeStruct(pairs.shape, f32)],
        in_specs=[whole(pltpu.SMEM)] + [whole()] * (2 * count + 3),
        out_specs=[whole()] * (count + 1),
        scratch_shapes=[
            pltpu.VMEM((seq_len, 3 * width), bf16),
            pltpu.VMEM((seq_len, width), bf16),
            pltpu.VMEM((slots, block_rows, block_rows), f32),
            pltpu.VMEM((blocks, width, block_rows), bf16),
            pltpu.VMEM((width, pairs.shape[1]), bf16),
            pltpu.VMEM((width, block_rows), f32),
            pltpu.VMEM((seq_len, width), f32),
            pltpu.VMEM((seq_len, width), f32),
            pltpu.VMEM((seq_len, width), f32),
        ],
        compiler_params=pltpu.CompilerParams(vmem_limit_bytes=32 << 20),
        cost_estimate=small_cost,
        name="attention_backward",
    )(order, *packed, *grads, pairs, seg_row, lse)
    return (results[:count], results[count])


def chunk_kernel(place_ref, up_ref, down_ref, keep_ref, give_ref, up, down, chunks, sems, out_sems):
    hidden, width = down.shape
    rows = hidden // 4
    core, parity = place_ref[0], place_ref[1]
    half = width // 2
    loads = []
    for at in range(2):
        span = pl.ds(at * half, half)
        loads.append(pltpu.make_async_copy(up_ref.at[span], up.at[span], sems.at[at]))
    for at in range(2):
        span = pl.ds(at * 2 * rows, 2 * rows)
        loads.append(pltpu.make_async_copy(down_ref.at[span], down.at[span], sems.at[2 + at]))
    for load in loads:
        load.start()
    spots = []
    for side in range(2):
        for which in range(2):
            spots.append(
                (1 - core if side else core, 1 - parity if which else parity, 2 * side + which)
            )
    for at in range(2):
        loads[at].wait()
        span = slice(at * half, (at + 1) * half)
        for side, slot, index in spots:
            chunks[side, slot, :, span] = jnp.transpose(up[span, index * rows : (index + 1) * rows])
    for at in range(2):
        loads[2 + at].wait()
        for side, slot, index in spots[2 * at : 2 * at + 2]:
            chunks[side, slot, :, width:] = down[index * rows : (index + 1) * rows, :]
    stores = [
        pltpu.make_async_copy(chunks.at[side], target, out_sems.at[side])
        for side, target in enumerate((keep_ref, give_ref))
    ]
    for store in stores:
        store.start()
    for store in stores:
        store.wait()


def feed_forward_chunks(place, up, down):
    hidden, width = down.shape
    shape = (2, hidden // 4, 2 * width)
    return pl.pallas_call(
        chunk_kernel,
        out_shape=[jax.ShapeDtypeStruct(shape, bf16)] * 2,
        in_specs=[whole(pltpu.SMEM), whole(pltpu.HBM), whole(pltpu.HBM)],
        out_specs=[whole(pltpu.HBM)] * 2,
        scratch_shapes=[
            pltpu.VMEM((width, hidden), bf16),
            pltpu.VMEM((hidden, width), bf16),
            pltpu.VMEM((2,) + shape, bf16),
            pltpu.SemaphoreType.DMA((4,)),
            pltpu.SemaphoreType.DMA((2,)),
        ],
        compiler_params=pltpu.CompilerParams(vmem_limit_bytes=20 << 20),
        cost_estimate=small_cost,
        name="feed_forward_chunks",
    )(place, up, down)


def feed_forward(normed, bias, chunks, grads, with_output, per):
    rows = chunks[0].shape[0]
    groups, hidden = (len(chunks) // per, per * rows)
    bias = bias.reshape(groups, 1, hidden)
    tokens, width = normed[0].shape
    with_grad = grads is not None
    kinds = with_output + with_grad
    small = (8, 128)
    return pl.pallas_call(
        functools.partial(feed_forward_kernel, groups, per, with_output, with_grad),
        out_shape=[
            jax.ShapeDtypeStruct((tokens, width), f32),
            jax.ShapeDtypeStruct((tokens, width), bf16),
        ]
        * kinds,
        in_specs=[whole()] * (3 + 2 * with_grad) + [whole(pltpu.HBM)] * len(chunks),
        out_specs=[whole()] * (2 * kinds),
        scratch_shapes=[
            pltpu.VMEM((groups * hidden, 2 * width), bf16),
            pltpu.SemaphoreType.DMA((groups, per)),
            pltpu.VMEM((2 * tokens, width), bf16),
            pltpu.VMEM((2 * tokens, width) if with_grad else small, bf16),
            pltpu.VMEM((groups, 2 * tokens, hidden) if with_output else small, bf16),
            pltpu.VMEM((groups, 2 * tokens, hidden) if with_grad else small, bf16),
        ],
        compiler_params=pltpu.CompilerParams(vmem_limit_bytes=58 << 20),
        cost_estimate=small_cost,
        name="feed_forward",
    )(*normed, bias, *(grads if with_grad else ()), *chunks)


def dot_tn(a, b):
    return lax.dot_general(a, b, (((0,), (0,)), ((), ())), preferred_element_type=f32)


def second_grad_kernel(head_dim, kept_ref, came_ref, hidden_ref, w2_ref, b2_ref):
    grad = (kept_ref[...] + came_ref[...]).astype(bf16)
    heads = w2_ref.shape[1]
    for head in range(heads):
        columns = [
            grad[:, (heads * side + head) * head_dim : (heads * side + head + 1) * head_dim]
            for side in range(2)
        ]
        block = jnp.concatenate(columns, axis=1)
        w2_ref[:, head, :] = dot_tn(hidden_ref[...], block)
        b2_ref[head : head + 1, :] = jnp.sum(block.astype(f32), axis=0, keepdims=True)


def second_grads(kept, came, hidden, heads):
    head_dim = kept.shape[1] // (2 * heads)
    return pl.pallas_call(
        functools.partial(second_grad_kernel, head_dim),
        out_shape=[
            jax.ShapeDtypeStruct((hidden.shape[1], heads, 2 * head_dim), f32),
            jax.ShapeDtypeStruct((heads, 2 * head_dim), f32),
        ],
        in_specs=[whole()] * 3,
        out_specs=[whole()] * 2,
        compiler_params=pltpu.CompilerParams(vmem_limit_bytes=8 << 20),
        cost_estimate=small_cost,
        name="second_grads",
    )(kept, came, hidden)


def first_grad_kernel(grad_ref, curve_ref, embed_ref, w1_ref, embed_out, w1_out, b1_out):
    curve = curve_ref[...]
    grad = (grad_ref[...] * (1.0 - curve * curve)).astype(bf16)
    w1_out[...] = dot_tn(embed_ref[...], grad)
    b1_out[...] = jnp.sum(grad.astype(f32), axis=0, keepdims=True)
    embed_out[...] = dot_nt(grad, w1_ref[...])[: embed_out.shape[0]]


def first_grads(grad, curve, embed, w1, prefix_len):
    return pl.pallas_call(
        first_grad_kernel,
        out_shape=[
            jax.ShapeDtypeStruct((prefix_len, embed.shape[1]), f32),
            jax.ShapeDtypeStruct(w1.shape, f32),
            jax.ShapeDtypeStruct((1, w1.shape[1]), f32),
        ],
        in_specs=[whole()] * 4,
        out_specs=[whole()] * 3,
        compiler_params=pltpu.CompilerParams(vmem_limit_bytes=12 << 20),
        cost_estimate=small_cost,
        name="first_grads",
    )(grad, curve, embed, w1)


def place_kernel(spot_ref, low_own, low_other, high_own, high_other, out_ref):
    row = spot_ref[1]

    @pl.when(spot_ref[0] == 0)
    def _():
        out_ref[row] = low_own[...]
        out_ref[1 - row] = low_other[...]

    @pl.when(spot_ref[0] == 1)
    def _():
        out_ref[row] = high_own[...]
        out_ref[1 - row] = high_other[...]


def place_rows(spot, *blocks):
    return pl.pallas_call(
        place_kernel,
        out_shape=jax.ShapeDtypeStruct((2,) + blocks[0].shape, bf16),
        in_specs=[whole(pltpu.SMEM)] + [whole()] * 4,
        out_specs=whole(),
        compiler_params=pltpu.CompilerParams(vmem_limit_bytes=8 << 20),
        cost_estimate=small_cost,
        name="place_rows",
    )(spot, *blocks)


def centered_values(values):
    centered = values - jnp.mean(values, axis=-1, keepdims=True)
    scale = lax.rsqrt(jnp.mean(centered * centered, axis=-1, keepdims=True) + epsilon)
    return (centered * scale, scale)


def layer_norm(values, ln_gain, ln_bias):
    return centered_values(values)[0] * ln_gain + ln_bias


def norm_back(values, ln_gain, grad_normed):
    unit, scale = centered_values(values)
    entry = grad_normed * ln_gain
    return scale * (
        entry
        - jnp.mean(entry, axis=-1, keepdims=True)
        - unit * jnp.mean(entry * unit, axis=-1, keepdims=True)
    )


class Group:
    def __init__(self, tensor_size):
        self.size = tensor_size
        self.count = tensor_size // 2

    def core_swap(self, value):
        return lax.ppermute(value, "section", [(0, 1), (1, 0)])

    def shift(self, value, distance):
        pairs = [
            (half * self.count + place, half * self.count + (place + distance) % self.count)
            for half in range(2)
            for place in range(self.count)
        ]
        return lax.ppermute(value, "tensor", pairs)

    def cross(self, value):
        size, count = self.size, self.count
        pairs = [
            (core * size + place, (1 - core) * size + (place + count) % size)
            for core in range(2)
            for place in range(size)
        ]
        return lax.ppermute(value, ("section", "tensor"), pairs)

    def half_swap(self, value):
        pairs = [(place, (place + self.count) % self.size) for place in range(self.size)]
        return lax.ppermute(value, "tensor", pairs)

    def plane_swap(self, value, distance=1):
        planes = lax.axis_size("dp")
        pairs = [(plane, plane ^ distance) for plane in range(planes)]
        return lax.ppermute(value, "dp", pairs)

    def cross_from(self, value, core):
        size, count = self.size, self.count
        pairs = [
            (core * size + place, (1 - core) * size + (place + count) % size)
            for place in range(size)
        ]
        return lax.ppermute(value, ("section", "tensor"), pairs)

    def sum_planes(self, value):
        planes = lax.axis_size("dp")
        if planes & (planes - 1):
            return lax.psum(value, "dp")
        step = min(planes, 4)
        value = sum([value] + [self.plane_swap(value, distance) for distance in range(1, step)])
        distance = step
        while distance < planes:
            value = value + self.plane_swap(value, distance)
            distance *= 2
        return value

    def tensor_swap(self, value, distance):
        pairs = [(place, place ^ distance) for place in range(self.size)]
        return lax.ppermute(value, "tensor", pairs)

    def sum_shards(self, value):
        if self.size & (self.size - 1):
            return lax.psum(value, ("section", "tensor"))
        value = value + self.core_swap(value)
        step = min(self.size, 4)
        value = sum([value] + [self.tensor_swap(value, distance) for distance in range(1, step)])
        distance = step
        while distance < self.size:
            value = value + self.tensor_swap(value, distance)
            distance *= 2
        return value

    def shifts(self, stages, block):
        return [
            stages.send(functools.partial(self.shift, distance=distance), block)
            for distance in range(1, self.count)
        ]

    def paired(self, blocks):
        return [jnp.concatenate([part, self.core_swap(part)], axis=0) for part in blocks]

    def gather(self, stages, block):
        return self.paired([block] + self.shifts(stages, block))

    def scatter(self, stages, parts):
        rows = parts[0].shape[0] // 2
        total = None
        for distance in list(range(1, self.count)) + [0]:
            own, other = (parts[distance][:rows], parts[distance][rows:])
            if total is not None:
                other = lax.optimization_barrier((other, leaving))[0]
            self.swapped = self.core_swap(other)
            summed = own.astype(f32) + self.swapped.astype(f32)
            if distance:
                back = functools.partial(self.shift, distance=-distance)
                leaving = summed.astype(bf16)
                summed = stages.send(back, leaving).astype(f32)
            total = summed if total is None else total + summed
        return total


class Stages:
    def __init__(self):
        self.before, self.now = ([], [])

    def send(self, transfer, value):
        if self.before:
            value = lax.optimization_barrier((value, *self.before))[0]
        self.now.append(transfer(value))
        return self.now[-1]

    def next(self):
        self.before, self.now = (self.now, [])


def local(
    boundary,
    seg_ids,
    ln1_gain,
    ln1_bias,
    w_qkv,
    b_qkv,
    w_out,
    b_out,
    ln2_gain,
    ln2_bias,
    w_up,
    b_up,
    w_down,
    b_down,
    prefix_embed,
    reparam_w1,
    reparam_b1,
    reparam_w2,
    reparam_b2,
):
    core = lax.axis_index("section")
    place = lax.axis_index("tensor")
    group = Group(lax.axis_size("tensor"))
    count = group.count
    tok_rows, width = boundary.shape[2:]
    heads_local = w_qkv.shape[2]
    head_dim = w_qkv.shape[3] // 3
    head_width = heads_local * head_dim
    prefix_len = prefix_embed.shape[0]
    row = place // count
    low = core == 0

    def tied(value, *others):
        return lax.optimization_barrier((value,) + others)[0]

    stages = Stages()
    steps = range(1, count)

    own_row = lax.dynamic_index_in_dim(boundary[0], row, 0, False)
    other_row = lax.dynamic_index_in_dim(boundary[0], 1 - row, 0, False)
    came_row = stages.send(functools.partial(group.cross_from, core=0), other_row)
    inputs = jnp.where(low, own_row, came_row).astype(f32)
    proj_own = w_out.reshape(head_width, width)

    def layer_pair(own, far):
        return (jnp.where(low, own, far), jnp.where(low, far, own))


    def as_rows(value):
        value = value.reshape(-1, value.shape[-1])
        return jnp.pad(value, ((0, 0), (0, width - value.shape[1])))

    b_qkv_own = b_qkv.reshape(heads_local, 3, head_dim).transpose(1, 0, 2).reshape(1, 3 * head_width)
    small_parts = (ln1_gain, ln1_bias, b_out, ln2_gain, ln2_bias, b_down, b_up, b_up)
    small_own = jnp.concatenate([as_rows(part) for part in small_parts], axis=0)

    def on_chip(value):
        peer = group.core_swap(value)
        return jnp.stack([jnp.where(low, value, peer), jnp.where(low, peer, value)])

    small_chip = on_chip(small_own)

    def vectors_of(layer):
        return small_chip[layer, :8].astype(f32)

    def normed_one(layer, values):
        vectors = vectors_of(layer)
        return layer_norm(values, vectors[0:1], vectors[1:2]).astype(bf16)

    hidden_width = w_up.shape[2]
    rows = hidden_width // 4
    shared = lax.axis_size("dp") % 2 == 0
    parity = lax.axis_index("dp") % 2
    spot = jnp.stack([core, parity]).astype(jnp.int32)
    keep, give = feed_forward_chunks(tied(spot, other_row), w_up[0], w_down[0])
    handed = group.core_swap(give)
    even_0 = jnp.where(low, keep[0], handed[0])
    later_keep, later_handed, _ = lax.optimization_barrier((keep, handed, even_0))
    even = [even_0, jnp.where(low, later_handed[0], later_keep[0])]
    odd = [
        jnp.where(low, later_keep[1], later_handed[1]),
        jnp.where(low, later_handed[1], later_keep[1]),
    ]

    prefix_pre = dot_nn(tied(prefix_embed, even[0]), reparam_w1) + reparam_b1.astype(f32)
    curve = jnp.tanh(prefix_pre)
    hidden_low = curve.astype(bf16)
    w2_own = (
        tied(reparam_w2, even[0])
        .reshape(reparam_w2.shape[0], heads_local, 2, head_dim)
        .transpose(0, 2, 1, 3)
        .reshape(reparam_w2.shape[0], 2 * head_width)
    )
    b2_own = (
        reparam_b2.reshape(heads_local, 2, head_dim).transpose(1, 0, 2).reshape(2 * head_width)
    )
    prefix_own = (dot_nn(hidden_low, w2_own) + b2_own.astype(f32)).astype(bf16)
    pairs_own = jnp.concatenate(
        [
            jnp.pad(value, ((0, prefix_rows - value.shape[0]), (0, width - value.shape[1])))
            for value in (prefix_own[:, :head_width], prefix_own[:, head_width:], b_qkv_own)
        ],
        axis=0,
    )
    qkv_own = (
        tied(w_qkv, even[0])
        .reshape(width, heads_local, 3, head_dim)
        .transpose(0, 2, 1, 3)
        .reshape(width, 3 * head_width)
    )

    def plane_send(value):
        return stages.send(group.plane_swap, value)

    def half_send(value):
        return stages.send(group.half_swap, value)

    def far(value, layer):
        return stages.send(functools.partial(group.cross_from, core=layer), value)

    side_even_0 = [group.shift(even[0], distance) for distance in steps]
    stages.next()
    normed_0 = tied(normed_one(0, inputs), *side_even_0)
    gathered_0 = [normed_0] + group.shifts(stages, normed_0)
    stages.now += side_even_0
    side_bias = small_chip[:, 6, : w_up.shape[2]]
    side_bias = jnp.stack([side_bias] + group.shifts(stages, side_bias), axis=1)
    qkv_far = stages.send(group.cross, qkv_own)

    stages.next()
    pairs = layer_pair(pairs_own, stages.send(group.cross, pairs_own))
    proj_far_0 = far(proj_own, 0)
    half_even_0 = half_send(even[0])
    side_even_1 = group.shifts(stages, even[1])
    if shared:
        side_odd_0 = [plane_send(value) for value in side_even_0]
    else:
        side_odd_0 = group.shifts(stages, odd[0])

    def all_chunks(layer, half, side, corner):
        chunks = [even[layer], odd[layer], *half]
        for at in range(count - 1):
            chunks += [side[0][at], side[1][at], corner[0][at], corner[1][at]]
        return chunks

    seg_row = lax.dynamic_index_in_dim(seg_ids, row, 0, True).astype(f32)
    chip = place % count
    orders = [
        jnp.stack(
            [
                jnp.bitwise_xor(row, jnp.bitwise_xor(core, swapped ^ layer)) * count
                + (chip - distance + count) % count
                for distance in range(count)
                for swapped in range(2)
            ]
        ).astype(jnp.int32)
        for layer in range(2)
    ]

    class Layer:
        def __init__(self, index, qkv):
            self.vectors = vectors_of(index)
            self.ln1_gain, self.ln1_bias, self.b_out = [self.vectors[at : at + 1] for at in range(3)]
            shard = pairs[index]
            self.pairs = shard[: 2 * prefix_rows, :head_width].reshape(2, prefix_rows, head_width)
            self.b_qkv = shard[2 * prefix_rows : 2 * prefix_rows + 1, : 3 * head_width].astype(f32)
            self.order = orders[index]
            self.qkv = tied(qkv, *stages.before)

        def attention(self, inputs, gathered):
            self.inputs = inputs
            gathered = lax.optimization_barrier((*gathered, *stages.before))[:count]
            self.packed = [
                (dot_nn(part, self.qkv) + self.b_qkv).astype(bf16)
                for part in group.paired(gathered)
            ]
            self.context, self.lse = attention_forward(
                self.order, self.packed, self.pairs, seg_row, head_dim, prefix_len
            )

        def project(self):
            context = lax.optimization_barrier((*self.context, *stages.before))[:count]
            own, far_own = lax.optimization_barrier((*self.far_out, *self.context))[:2]
            self.out = jnp.where(low, own, far_own)
            parts = [dot_nn(part, self.out).astype(bf16) for part in context]
            self.middle = self.inputs + (group.scatter(stages, parts) + self.b_out)

        def project_here(self):
            context = lax.optimization_barrier((*self.context, *stages.before))[:count]
            branch = dot_nn(context[0], self.out)
            for distance in steps:
                came = group.shift(context[distance], -distance)
                branch = branch + dot_nn(came, self.out_side[distance - 1])
            rows = branch.shape[0] // 2
            own, peer = (branch[:rows], branch[rows:].astype(bf16))
            self.middle = self.inputs + (self.shared((own, peer)) + self.b_out)

        def norm_two(self, values):
            return layer_norm(values, self.vectors[3:4], self.vectors[4:5]).astype(bf16)

        def shared(self, *pairs):
            return sum([own + group.core_swap(peer).astype(f32) for own, peer in pairs])

        def output(self, middle, *pairs):
            return (middle + (self.shared(*pairs) + self.vectors[5:6])).astype(bf16)

        def middle_back(self, grad_out, *pairs):
            branch = self.shared(*pairs)
            return grad_out.astype(f32) + norm_back(self.middle, self.vectors[3:4], branch)

        def feed_forward(self, normed, grads, with_output):
            return feed_forward(normed, self.bias, self.chunks, grads, with_output, 2)

        def backward(self, grad_middle):
            stages.before = []
            grad_branch = grad_middle.astype(bf16)
            (grad_chip,) = group.paired([grad_branch])
            sides = [dot_nt(grad_chip, side).astype(bf16) for side in self.out_side]
            came = [group.shift(side, at + 1) for at, side in enumerate(sides)]
            grads = [dot_nt(grad_chip, self.out).astype(bf16)] + came
            grad_packed, grad_pairs = attention_backward(
                self.order, self.packed, grads, self.pairs, seg_row, self.lse, head_dim, prefix_len
            )
            parts = [dot_nt(part, self.qkv).astype(bf16) for part in grad_packed]
            grad_normed = group.scatter(stages, parts)
            grad_in = grad_middle + norm_back(self.inputs, self.ln1_gain, grad_normed)
            return (grad_in.astype(bf16), grad_pairs)

    pack_own = jnp.concatenate([tied(proj_own, qkv_far), other_row], axis=0)
    layer_0 = Layer(0, tied(jnp.where(low, qkv_own, qkv_far), pack_own))
    layer_0.far_out = (proj_own, proj_far_0)
    layer_0.attention(inputs, gathered_0)

    stages.next()
    corner_even_0 = group.shifts(stages, half_even_0)
    half_even_1 = half_send(even[1])
    far_pack = far(pack_own, 1)
    if shared:
        side_odd_1 = [plane_send(value) for value in side_even_1]
    else:
        side_odd_1 = group.shifts(stages, odd[1])
    layer_0.project()

    stages.next()
    half_odd_0 = half_send(odd[0])
    if shared:
        corner_odd_0 = [plane_send(value) for value in corner_even_0]
    else:
        corner_odd_0 = group.shifts(stages, half_odd_0)
    corner_even_1 = group.shifts(stages, half_even_1)
    half_bias = half_send(side_bias)
    up_bias = jnp.stack([side_bias, half_bias], axis=2).astype(f32)
    up_bias = up_bias.reshape(2, 2 * count, 2, 2, rows)
    up_bias = jnp.where(low, up_bias[:, :, 0], up_bias[:, :, 1])
    up_bias = jnp.where(parity == 0, up_bias, up_bias[:, :, ::-1])
    up_bias = up_bias.reshape(2, 4 * count, rows)
    layer_0.bias = up_bias[0]
    layer_0.chunks = all_chunks(
        0,
        (half_even_0, half_odd_0),
        (side_even_0, side_odd_0),
        (corner_even_0, corner_odd_0),
    )
    middle_peer = group.core_swap(layer_0.middle)
    normed_pair = (layer_0.norm_two(layer_0.middle), layer_0.norm_two(middle_peer))

    stages.next()
    half_odd_1 = half_send(odd[1])
    own_proj, far_pack = lax.optimization_barrier((proj_own, far_pack, *stages.before))[:2]
    cotangent = jnp.where(low, far_pack[head_width:], own_row)
    proj_1 = jnp.where(low, far_pack[:head_width], own_proj)
    projs = (layer_0.out, proj_1)
    if shared:
        corner_odd_1 = [plane_send(value) for value in corner_even_1]
    else:
        corner_odd_1 = group.shifts(stages, half_odd_1)
    out_sides = [
        [stages.send(functools.partial(group.shift, distance=-distance), proj) for distance in steps]
        for proj in projs
    ]
    normed_swapped = (tied(normed_pair[1], *stages.before), normed_pair[0])
    out_kept, out_sent = layer_0.feed_forward(normed_swapped, None, True)
    first_out = layer_0.output(middle_peer, (out_kept, tied(out_sent, *stages.now)))
    inputs_1 = first_out.astype(f32)
    normed_1 = normed_one(1, inputs_1)
    gathered_1 = [normed_1] + group.shifts(stages, normed_1)
    w2_far = group.cross(tied(w2_own, first_out))
    layer_1 = Layer(1, jnp.where(low, *lax.optimization_barrier((qkv_far, qkv_own, w2_far))[:2]))
    layer_0.out_side, layer_1.out_side = out_sides
    layer_1.out = proj_1
    layer_1.bias = up_bias[1]
    layer_1.attention(inputs_1, gathered_1)
    layer_1.chunks = all_chunks(
        1,
        (half_even_1, half_odd_1),
        (side_even_1, side_odd_1),
        (corner_even_1, corner_odd_1),
    )

    stages.next()
    w2_side = layer_pair(w2_own, w2_far)
    layer_1.project_here()
    normed = layer_1.norm_two(layer_1.middle)
    normed = (normed, group.core_swap(normed))
    cotangents = (cotangent, group.core_swap(cotangent))
    parts = layer_1.feed_forward(normed, cotangents, True)
    last_out = layer_1.output(layer_1.middle, parts[:2])
    grad_middle = layer_1.middle_back(cotangent, parts[2:])
    mid_grad, grad_pairs_one = layer_1.backward(grad_middle)
    high_other = group.cross_from(last_out, 0)
    mid_grad = tied(mid_grad, high_other)
    mid_peer = group.core_swap(mid_grad)
    back_part = layer_0.feed_forward(normed_pair, (mid_peer, mid_grad), False)
    grad_middle = layer_0.middle_back(mid_peer, back_part)
    first_grad, grad_pairs_zero = layer_0.backward(grad_middle)

    low_other = group.cross_from(first_grad, 1)
    spot = jnp.stack([core, row]).astype(jnp.int32)
    boundary_result = place_rows(spot, first_grad, low_other, last_out, high_other)[None]

    def joined(pairs):
        return jnp.concatenate([pairs[0], pairs[1]], axis=1)

    grads = (joined(grad_pairs_zero), joined(grad_pairs_one))
    hidden_part = sum(
        lax.dot_general(
            grad,
            side.astype(f32),
            (((1,), (1,)), ((), ())),
            precision=lax.Precision.HIGHEST,
            preferred_element_type=f32,
        )
        for grad, side in zip(grads, w2_side)
    )
    kept, sent = layer_pair(*grads)
    message = jnp.concatenate([hidden_part, kept, sent], axis=1)
    summed = tied(message, group.swapped)
    summed = group.sum_planes(summed)
    hidden_width = hidden_part.shape[1]
    hidden_part = summed[:, :hidden_width]
    hidden_grad = group.sum_shards(hidden_part)
    kept = summed[:, hidden_width : hidden_width + 2 * head_width]
    sent = summed[:, hidden_width + 2 * head_width :]
    pad = ((0, prefix_rows - prefix_len), (0, 0))
    w2_grad, b2_grad = second_grads(kept, group.cross(sent), jnp.pad(hidden_low, pad), heads_local)
    embed_grad, w1_grad, b1_grad = first_grads(
        hidden_grad, jnp.pad(curve, pad), jnp.pad(prefix_embed, pad), reparam_w1, prefix_len
    )
    return (
        boundary_result,
        embed_grad,
        w1_grad,
        b1_grad.reshape(reparam_b1.shape),
        w2_grad.reshape(reparam_w2.shape),
        b2_grad.reshape(reparam_b2.shape),
    )


def solution(mesh):
    return jax.shard_map(
        local,
        mesh=mesh,
        in_specs=(
            P("section", "dp", "tensor", None),
            P("dp", None),
            P("section", None),
            P("section", None),
            P("section", None, "tensor", None),
            P("section", "tensor", None),
            P("section", "tensor", None, None),
            P("section", None),
            P("section", None),
            P("section", None),
            P("section", None, "tensor"),
            P("section", "tensor"),
            P("section", "tensor", None),
            P("section", None),
            P(),
            P(),
            P(),
            P(None, "section", "tensor", None),
            P("section", "tensor", None),
        ),
        out_specs=(
            P("section", "dp", "tensor", None),
            P(),
            P(),
            P(),
            P(None, "section", "tensor", None),
            P("section", "tensor", None),
        ),
        check_vma=False,
    )
```

```python
import functools

import jax
import jax.numpy as jnp
from jax import lax
from jax.experimental import pallas as pl
from jax.experimental.pallas import tpu as pltpu
from jax.sharding import PartitionSpec as P

epsilon = 1e-05
masked_value = -1e30
max_segment = 512
prefix_rows = 16
stat_rows = 8
f32 = jnp.float32
bf16 = jnp.bfloat16


small_cost = pl.CostEstimate(flops=1, bytes_accessed=1, transcendentals=0)


def dot_nn(a, b):
    return lax.dot_general(a, b, (((1,), (0,)), ((), ())), preferred_element_type=f32)


def dot_nt(a, b):
    return lax.dot_general(a, b, (((1,), (1,)), ((), ())), preferred_element_type=f32)


def key_blocks(index, block_rows):
    reach = -(-(max_segment - 1) // block_rows)
    return list(range(max(0, index - reach), index + 1))


def gather_rows(order_ref, sources, target_ref, block_rows):
    for place in range(2 * len(sources)):
        start = pl.multiple_of(order_ref[place] * block_rows, block_rows)
        target_ref[pl.ds(start, block_rows), :] = sources[place // 2][
            pl.ds((place % 2) * block_rows, block_rows), :
        ]


def scatter_rows(order_ref, source_ref, targets, block_rows, columns):
    for place in range(2 * len(targets)):
        start = pl.multiple_of(order_ref[place] * block_rows, block_rows)
        targets[place // 2][pl.ds((place % 2) * block_rows, block_rows), columns] = source_ref[
            pl.ds(start, block_rows), :
        ].astype(targets[place // 2].dtype)


def segment_column(seg_ref, start, rows):
    row = seg_ref[0:1, start : start + rows]
    return jnp.transpose(jnp.broadcast_to(row, (128, rows)))[:, 0:1]


def attention_forward_kernel(count, block_rows, head_dim, prefix_len, order_ref, *refs):
    packed_refs = refs[:count]
    pairs_ref, seg_ref = refs[count : count + 2]
    context_refs = refs[count + 2 : 2 * count + 2]
    lse_ref, rows_ref, context_ref, bias_ref, vt_ref, pvt_ref, ct_ref = refs[2 * count + 2 :]
    width = pairs_ref.shape[2]
    heads = width // head_dim
    blocks = 2 * count
    scaling = head_dim ** (-0.5)
    gather_rows(order_ref, packed_refs, rows_ref, block_rows)
    lane = lax.broadcasted_iota(jnp.int32, (1, width), 1) // head_dim
    prefix_bias = jnp.where(
        lax.broadcasted_iota(jnp.int32, (pairs_ref.shape[1], 1), 0) < prefix_len, 0.0, masked_value
    )
    prefix_keys = pairs_ref[0]
    pvt_ref[...] = jnp.transpose(pairs_ref[1].astype(f32)).astype(bf16)
    for index in range(blocks):
        vt_ref[index] = jnp.transpose(
            rows_ref[index * block_rows : (index + 1) * block_rows, 2 * width :].astype(f32)
        ).astype(bf16)
    for index in range(blocks):
        start = index * block_rows
        keys = key_blocks(index, block_rows)
        fill_bias(seg_ref, bias_ref, index, keys, block_rows)
        queries = rows_ref[pl.ds(start, block_rows), 0:width]

        def one_head(head, carry):
            query = jnp.where(lane == head, queries, 0.0) * jnp.asarray(scaling, bf16)
            span = pl.ds(pl.multiple_of(head * head_dim, head_dim), head_dim)
            prefix_scores = dot_nt(prefix_keys, query) + prefix_bias
            row_max = jnp.max(prefix_scores, axis=0, keepdims=True)
            scores = []
            for slot, key in enumerate(keys):
                rows = slice(key * block_rows, (key + 1) * block_rows)
                score = dot_nt(rows_ref[rows, width : 2 * width], query) + bias_ref[slot]
                row_max = jnp.maximum(row_max, jnp.max(score, axis=0, keepdims=True))
                scores.append(score)
            prefix_exp = jnp.exp(prefix_scores - row_max)
            row_sum = jnp.sum(prefix_exp, axis=0, keepdims=True)
            context = dot_nn(pvt_ref[span, :], prefix_exp.astype(bf16))
            for score, key in zip(scores, keys):
                exped = jnp.exp(score - row_max)
                row_sum = row_sum + jnp.sum(exped, axis=0, keepdims=True)
                context = context + dot_nn(vt_ref[key, span, :], exped.astype(bf16))
            ct_ref[span, :] = context * (1.0 / row_sum)
            lse_ref[pl.ds(head, 1), start : start + block_rows] = row_max + jnp.log(row_sum)
            return carry

        lax.fori_loop(0, heads, one_head, 0, unroll=True)
        context_ref[pl.ds(start, block_rows), :] = jnp.transpose(ct_ref[...]).astype(bf16)
    scatter_rows(order_ref, context_ref, context_refs, block_rows, slice(0, width))


def fill_bias(seg_ref, bias_ref, index, keys, block_rows):
    seg_query = seg_ref[0:1, index * block_rows : (index + 1) * block_rows]
    for slot, key in enumerate(keys):
        same = segment_column(seg_ref, key * block_rows, block_rows) == seg_query
        if key == index:
            shape = (block_rows, block_rows)
            same = same & (
                lax.broadcasted_iota(jnp.int32, shape, 0)
                <= lax.broadcasted_iota(jnp.int32, shape, 1)
            )
        bias_ref[slot] = jnp.where(same, 0.0, masked_value)


def attention_backward_kernel(count, block_rows, head_dim, prefix_len, order_ref, *refs):
    packed_refs = refs[:count]
    grad_refs = refs[count : 2 * count]
    pairs_ref, seg_ref, lse_ref = refs[2 * count : 2 * count + 3]
    out_refs = refs[2 * count + 3 : 3 * count + 3]
    prefix_out = refs[3 * count + 3]
    rows_ref, grad_ref, bias_ref, kt_ref, pkt_ref, dqt_ref, dq_ref, dk_ref, dv_ref = refs[
        3 * count + 4 :
    ]
    width = pairs_ref.shape[2]
    heads = width // head_dim
    blocks = 2 * count
    scaling = head_dim ** (-0.5)
    gather_rows(order_ref, packed_refs, rows_ref, block_rows)
    gather_rows(order_ref, grad_refs, grad_ref, block_rows)
    lane = lax.broadcasted_iota(jnp.int32, (1, width), 1) // head_dim
    prefix_bias = jnp.where(
        lax.broadcasted_iota(jnp.int32, (pairs_ref.shape[1], 1), 0) < prefix_len, 0.0, masked_value
    )
    prefix_keys, prefix_values = pairs_ref[0], pairs_ref[1]
    pkt_ref[...] = jnp.transpose(prefix_keys.astype(f32)).astype(bf16)
    dk_ref[...] = jnp.zeros_like(dk_ref)
    dv_ref[...] = jnp.zeros_like(dv_ref)
    prefix_out[...] = jnp.zeros_like(prefix_out)
    for index in range(blocks):
        kt_ref[index] = jnp.transpose(
            rows_ref[index * block_rows : (index + 1) * block_rows, width : 2 * width].astype(f32)
        ).astype(bf16)
    for index in range(blocks):
        start = index * block_rows
        keys = key_blocks(index, block_rows)
        fill_bias(seg_ref, bias_ref, index, keys, block_rows)
        queries = rows_ref[pl.ds(start, block_rows), 0:width]
        grads = grad_ref[pl.ds(start, block_rows), :]

        def one_head(head, carry):
            chosen = lane == head
            query = jnp.where(chosen, queries, 0.0) * jnp.asarray(scaling, bf16)
            grad = jnp.where(chosen, grads, 0.0)
            lse = lse_ref[pl.ds(head, 1), start : start + block_rows]
            span = pl.ds(pl.multiple_of(head * head_dim, head_dim), head_dim)
            prefix_prob = jnp.exp(dot_nt(prefix_keys, query) + prefix_bias - lse)
            prefix_dp = dot_nt(prefix_values, grad)
            delta = jnp.sum(prefix_prob * prefix_dp, axis=0, keepdims=True)
            probs, dps = [], []
            for slot, key in enumerate(keys):
                rows = slice(key * block_rows, (key + 1) * block_rows)
                prob = jnp.exp(
                    dot_nt(rows_ref[rows, width : 2 * width], query) + bias_ref[slot] - lse
                )
                dp = dot_nt(rows_ref[rows, 2 * width :], grad)
                delta = delta + jnp.sum(prob * dp, axis=0, keepdims=True)
                probs.append(prob)
                dps.append(dp)
            prefix_ds = (prefix_prob * (prefix_dp - delta)).astype(bf16)
            prefix_out[0] += dot_nn(prefix_ds, query)
            prefix_out[1] += dot_nn(prefix_prob.astype(bf16), grad)
            dqt = dot_nn(pkt_ref[span, :], prefix_ds)
            for prob, dp, key in zip(probs, dps, keys):
                rows = slice(key * block_rows, (key + 1) * block_rows)
                ds = (prob * (dp - delta)).astype(bf16)
                dk_ref[rows, :] += dot_nn(ds, query)
                dv_ref[rows, :] += dot_nn(prob.astype(bf16), grad)
                dqt = dqt + dot_nn(kt_ref[key, span, :], ds)
            dqt_ref[span, :] = dqt
            return carry

        lax.fori_loop(0, heads, one_head, 0, unroll=True)
        dq_ref[pl.ds(start, block_rows), :] = jnp.transpose(dqt_ref[...]) * scaling
    scatter_rows(order_ref, dq_ref, out_refs, block_rows, slice(0, width))
    scatter_rows(order_ref, dk_ref, out_refs, block_rows, slice(width, 2 * width))
    scatter_rows(order_ref, dv_ref, out_refs, block_rows, slice(2 * width, 3 * width))


def gelu_parts(values):
    root = 0.7978845608028654
    square = values * values
    curve = jnp.tanh(root * values * (1.0 + 0.044715 * square))
    return (square, curve, root)


def feed_forward_kernel(groups, per, with_output, with_grad, *refs):
    refs = list(refs)
    normed_own, normed_peer, bias_ref = refs[:3]
    del refs[:3]
    grad_own, grad_peer = (refs.pop(0), refs.pop(0)) if with_grad else (None, None)
    chunk_refs = refs[: per * groups]
    del refs[: per * groups]
    out_own, out_peer = (refs.pop(0), refs.pop(0)) if with_output else (None, None)
    back_own, back_peer = (refs.pop(0), refs.pop(0)) if with_grad else (None, None)
    weight_ref, sems, normed_ref, grad_ref, hidden_ref, back_ref = refs
    tokens, width = normed_own.shape
    hidden = bias_ref.shape[2]
    rows = hidden // per
    block = min(256, width)

    def copies_of(group):
        return [
            pltpu.make_async_copy(
                chunk_refs[per * group + part],
                weight_ref.at[pl.ds((per * group + part) * rows, rows)],
                sems.at[group, part],
            )
            for part in range(per)
        ]

    for group in range(min(2, groups)):
        for copy in copies_of(group):
            copy.start()
    normed_ref[0:tokens, :] = normed_own[...]
    normed_ref[tokens:, :] = normed_peer[...]
    if with_grad:
        grad_ref[0:tokens, :] = grad_own[...]
        grad_ref[tokens:, :] = grad_peer[...]
    @pl.loop(0, groups)
    def _(group):
        for part in range(per):
            pltpu.make_async_copy(
                chunk_refs[0], weight_ref.at[pl.ds(0, rows)], sems.at[group, part]
            ).wait()
        for later in range(2, groups):

            @pl.when(group == later - 2)
            def _():
                for copy in copies_of(later):
                    copy.start()

        span = pl.ds(pl.multiple_of(group * hidden, hidden), hidden)
        pre = dot_nt(normed_ref[...], weight_ref[span, 0:width]) + bias_ref[group]
        square, curve, root = gelu_parts(pre)
        if with_output:
            hidden_ref[group] = (0.5 * pre * (1.0 + curve)).astype(bf16)
        if with_grad:
            slope = 0.5 * (1.0 + curve) + 0.5 * pre * (1.0 - curve * curve) * (
                root * (1.0 + 3 * 0.044715 * square)
            )
            back_ref[group] = (dot_nt(grad_ref[...], weight_ref[span, width:]) * slope).astype(bf16)

    def summed(values_ref, columns):
        return sum(
            dot_nn(values_ref[group], weight_ref[group * hidden : (group + 1) * hidden, columns])
            for group in range(groups)
        )

    for at in range(0, width, block):
        span = slice(at, at + block)
        if with_output:
            total = summed(hidden_ref, slice(width + at, width + at + block))
            out_own[:, span] = total[0:tokens]
            out_peer[:, span] = total[tokens:].astype(bf16)
        if with_grad:
            total = summed(back_ref, span)
            back_own[:, span] = total[0:tokens]
            back_peer[:, span] = total[tokens:].astype(bf16)


def whole(memory_space=pltpu.VMEM):
    return pl.BlockSpec(memory_space=memory_space)


def attention_forward(order, packed, pairs, seg_row, head_dim, prefix_len):
    count = len(packed)
    block_rows = packed[0].shape[0] // 2
    width = packed[0].shape[1] // 3
    seq_len = seg_row.shape[1]
    slots = len(key_blocks(2 * count - 1, block_rows))
    results = pl.pallas_call(
        functools.partial(attention_forward_kernel, count, block_rows, head_dim, prefix_len),
        out_shape=[jax.ShapeDtypeStruct((2 * block_rows, width), bf16)] * count
        + [jax.ShapeDtypeStruct((stat_rows, seq_len), f32)],
        in_specs=[whole(pltpu.SMEM)] + [whole()] * (count + 2),
        out_specs=[whole()] * (count + 1),
        scratch_shapes=[
            pltpu.VMEM((seq_len, 3 * width), bf16),
            pltpu.VMEM((seq_len, width), bf16),
            pltpu.VMEM((slots, block_rows, block_rows), f32),
            pltpu.VMEM((2 * count, width, block_rows), bf16),
            pltpu.VMEM((width, pairs.shape[1]), bf16),
            pltpu.VMEM((width, block_rows), f32),
        ],
        compiler_params=pltpu.CompilerParams(vmem_limit_bytes=32 << 20),
        cost_estimate=small_cost,
        name="attention_forward",
    )(order, *packed, pairs, seg_row)
    return (results[:count], results[count])


def attention_backward(order, packed, grads, pairs, seg_row, lse, head_dim, prefix_len):
    count = len(packed)
    block_rows = packed[0].shape[0] // 2
    width = packed[0].shape[1] // 3
    seq_len = seg_row.shape[1]
    blocks = 2 * count
    slots = len(key_blocks(blocks - 1, block_rows))
    results = pl.pallas_call(
        functools.partial(attention_backward_kernel, count, block_rows, head_dim, prefix_len),
        out_shape=[jax.ShapeDtypeStruct((2 * block_rows, 3 * width), bf16)] * count
        + [jax.ShapeDtypeStruct(pairs.shape, f32)],
        in_specs=[whole(pltpu.SMEM)] + [whole()] * (2 * count + 3),
        out_specs=[whole()] * (count + 1),
        scratch_shapes=[
            pltpu.VMEM((seq_len, 3 * width), bf16),
            pltpu.VMEM((seq_len, width), bf16),
            pltpu.VMEM((slots, block_rows, block_rows), f32),
            pltpu.VMEM((blocks, width, block_rows), bf16),
            pltpu.VMEM((width, pairs.shape[1]), bf16),
            pltpu.VMEM((width, block_rows), f32),
            pltpu.VMEM((seq_len, width), f32),
            pltpu.VMEM((seq_len, width), f32),
            pltpu.VMEM((seq_len, width), f32),
        ],
        compiler_params=pltpu.CompilerParams(vmem_limit_bytes=32 << 20),
        cost_estimate=small_cost,
        name="attention_backward",
    )(order, *packed, *grads, pairs, seg_row, lse)
    return (results[:count], results[count])


def chunk_kernel(place_ref, up_ref, down_ref, keep_ref, give_ref, up, down, chunks, sems, out_sems):
    hidden, width = down.shape
    rows = hidden // 4
    core, parity = place_ref[0], place_ref[1]
    half = width // 2
    loads = []
    for at in range(2):
        span = pl.ds(at * half, half)
        loads.append(pltpu.make_async_copy(up_ref.at[span], up.at[span], sems.at[at]))
    for at in range(2):
        span = pl.ds(at * 2 * rows, 2 * rows)
        loads.append(pltpu.make_async_copy(down_ref.at[span], down.at[span], sems.at[2 + at]))
    for load in loads:
        load.start()
    spots = []
    for side in range(2):
        for which in range(2):
            spots.append(
                (1 - core if side else core, 1 - parity if which else parity, 2 * side + which)
            )
    for at in range(2):
        loads[at].wait()
        span = slice(at * half, (at + 1) * half)
        for side, slot, index in spots:
            chunks[side, slot, :, span] = jnp.transpose(up[span, index * rows : (index + 1) * rows])
    for at in range(2):
        loads[2 + at].wait()
        for side, slot, index in spots[2 * at : 2 * at + 2]:
            chunks[side, slot, :, width:] = down[index * rows : (index + 1) * rows, :]
    stores = [
        pltpu.make_async_copy(chunks.at[side], target, out_sems.at[side])
        for side, target in enumerate((keep_ref, give_ref))
    ]
    for store in stores:
        store.start()
    for store in stores:
        store.wait()


def feed_forward_chunks(place, up, down):
    hidden, width = down.shape
    shape = (2, hidden // 4, 2 * width)
    return pl.pallas_call(
        chunk_kernel,
        out_shape=[jax.ShapeDtypeStruct(shape, bf16)] * 2,
        in_specs=[whole(pltpu.SMEM), whole(pltpu.HBM), whole(pltpu.HBM)],
        out_specs=[whole(pltpu.HBM)] * 2,
        scratch_shapes=[
            pltpu.VMEM((width, hidden), bf16),
            pltpu.VMEM((hidden, width), bf16),
            pltpu.VMEM((2,) + shape, bf16),
            pltpu.SemaphoreType.DMA((4,)),
            pltpu.SemaphoreType.DMA((2,)),
        ],
        compiler_params=pltpu.CompilerParams(vmem_limit_bytes=58 << 20),
        cost_estimate=small_cost,
        name="feed_forward_chunks",
    )(place, up, down)


def feed_forward(normed, bias, chunks, grads, with_output, per):
    rows = chunks[0].shape[0]
    groups, hidden = (len(chunks) // per, per * rows)
    bias = bias.reshape(groups, 1, hidden)
    tokens, width = normed[0].shape
    with_grad = grads is not None
    kinds = with_output + with_grad
    small = (8, 128)
    return pl.pallas_call(
        functools.partial(feed_forward_kernel, groups, per, with_output, with_grad),
        out_shape=[
            jax.ShapeDtypeStruct((tokens, width), f32),
            jax.ShapeDtypeStruct((tokens, width), bf16),
        ]
        * kinds,
        in_specs=[whole()] * (3 + 2 * with_grad) + [whole(pltpu.HBM)] * len(chunks),
        out_specs=[whole()] * (2 * kinds),
        scratch_shapes=[
            pltpu.VMEM((groups * hidden, 2 * width), bf16),
            pltpu.SemaphoreType.DMA((groups, per)),
            pltpu.VMEM((2 * tokens, width), bf16),
            pltpu.VMEM((2 * tokens, width) if with_grad else small, bf16),
            pltpu.VMEM((groups, 2 * tokens, hidden) if with_output else small, bf16),
            pltpu.VMEM((groups, 2 * tokens, hidden) if with_grad else small, bf16),
        ],
        compiler_params=pltpu.CompilerParams(vmem_limit_bytes=58 << 20),
        cost_estimate=small_cost,
        name="feed_forward",
    )(*normed, bias, *(grads if with_grad else ()), *chunks)


def dot_tn(a, b):
    return lax.dot_general(a, b, (((0,), (0,)), ((), ())), preferred_element_type=f32)


def second_grad_kernel(head_dim, kept_ref, came_ref, hidden_ref, w2_ref, b2_ref):
    grad = (kept_ref[...] + came_ref[...]).astype(bf16)
    heads = w2_ref.shape[1]
    for head in range(heads):
        columns = [
            grad[:, (heads * side + head) * head_dim : (heads * side + head + 1) * head_dim]
            for side in range(2)
        ]
        block = jnp.concatenate(columns, axis=1)
        w2_ref[:, head, :] = dot_tn(hidden_ref[...], block)
        b2_ref[head : head + 1, :] = jnp.sum(block.astype(f32), axis=0, keepdims=True)


def second_grads(kept, came, hidden, heads):
    head_dim = kept.shape[1] // (2 * heads)
    return pl.pallas_call(
        functools.partial(second_grad_kernel, head_dim),
        out_shape=[
            jax.ShapeDtypeStruct((hidden.shape[1], heads, 2 * head_dim), f32),
            jax.ShapeDtypeStruct((heads, 2 * head_dim), f32),
        ],
        in_specs=[whole()] * 3,
        out_specs=[whole()] * 2,
        compiler_params=pltpu.CompilerParams(vmem_limit_bytes=8 << 20),
        cost_estimate=small_cost,
        name="second_grads",
    )(kept, came, hidden)


def first_grad_kernel(grad_ref, curve_ref, embed_ref, w1_ref, embed_out, w1_out, b1_out):
    curve = curve_ref[...]
    grad = (grad_ref[...] * (1.0 - curve * curve)).astype(bf16)
    w1_out[...] = dot_tn(embed_ref[...], grad)
    b1_out[...] = jnp.sum(grad.astype(f32), axis=0, keepdims=True)
    embed_out[...] = dot_nt(grad, w1_ref[...])[: embed_out.shape[0]]


def first_grads(grad, curve, embed, w1, prefix_len):
    return pl.pallas_call(
        first_grad_kernel,
        out_shape=[
            jax.ShapeDtypeStruct((prefix_len, embed.shape[1]), f32),
            jax.ShapeDtypeStruct(w1.shape, f32),
            jax.ShapeDtypeStruct((1, w1.shape[1]), f32),
        ],
        in_specs=[whole()] * 4,
        out_specs=[whole()] * 3,
        compiler_params=pltpu.CompilerParams(vmem_limit_bytes=12 << 20),
        cost_estimate=small_cost,
        name="first_grads",
    )(grad, curve, embed, w1)


def place_kernel(spot_ref, low_own, low_other, high_own, high_other, out_ref):
    row = spot_ref[1]

    @pl.when(spot_ref[0] == 0)
    def _():
        out_ref[row] = low_own[...]
        out_ref[1 - row] = low_other[...]

    @pl.when(spot_ref[0] == 1)
    def _():
        out_ref[row] = high_own[...]
        out_ref[1 - row] = high_other[...]


def place_rows(spot, *blocks):
    return pl.pallas_call(
        place_kernel,
        out_shape=jax.ShapeDtypeStruct((2,) + blocks[0].shape, bf16),
        in_specs=[whole(pltpu.SMEM)] + [whole()] * 4,
        out_specs=whole(),
        compiler_params=pltpu.CompilerParams(vmem_limit_bytes=8 << 20),
        cost_estimate=small_cost,
        name="place_rows",
    )(spot, *blocks)


def centered_values(values):
    centered = values - jnp.mean(values, axis=-1, keepdims=True)
    scale = lax.rsqrt(jnp.mean(centered * centered, axis=-1, keepdims=True) + epsilon)
    return (centered * scale, scale)


def layer_norm(values, ln_gain, ln_bias):
    return centered_values(values)[0] * ln_gain + ln_bias


def norm_back(values, ln_gain, grad_normed):
    unit, scale = centered_values(values)
    entry = grad_normed * ln_gain
    return scale * (
        entry
        - jnp.mean(entry, axis=-1, keepdims=True)
        - unit * jnp.mean(entry * unit, axis=-1, keepdims=True)
    )


class Group:
    def __init__(self, tensor_size):
        self.size = tensor_size
        self.count = tensor_size // 2

    def core_swap(self, value):
        return lax.ppermute(value, "section", [(0, 1), (1, 0)])

    def shift(self, value, distance):
        pairs = [
            (half * self.count + place, half * self.count + (place + distance) % self.count)
            for half in range(2)
            for place in range(self.count)
        ]
        return lax.ppermute(value, "tensor", pairs)

    def cross(self, value):
        size, count = self.size, self.count
        pairs = [
            (core * size + place, (1 - core) * size + (place + count) % size)
            for core in range(2)
            for place in range(size)
        ]
        return lax.ppermute(value, ("section", "tensor"), pairs)

    def half_swap(self, value):
        pairs = [(place, (place + self.count) % self.size) for place in range(self.size)]
        return lax.ppermute(value, "tensor", pairs)

    def plane_swap(self, value, distance=1):
        planes = lax.axis_size("dp")
        pairs = [(plane, plane ^ distance) for plane in range(planes)]
        return lax.ppermute(value, "dp", pairs)

    def cross_from(self, value, core):
        size, count = self.size, self.count
        pairs = [
            (core * size + place, (1 - core) * size + (place + count) % size)
            for place in range(size)
        ]
        return lax.ppermute(value, ("section", "tensor"), pairs)

    def sum_planes(self, value):
        planes = lax.axis_size("dp")
        if planes & (planes - 1):
            return lax.psum(value, "dp")
        step = min(planes, 4)
        value = sum([value] + [self.plane_swap(value, distance) for distance in range(1, step)])
        distance = step
        while distance < planes:
            value = value + self.plane_swap(value, distance)
            distance *= 2
        return value

    def tensor_swap(self, value, distance):
        pairs = [(place, place ^ distance) for place in range(self.size)]
        return lax.ppermute(value, "tensor", pairs)

    def sum_shards(self, value):
        if self.size & (self.size - 1):
            return lax.psum(value, ("section", "tensor"))
        value = value + self.core_swap(value)
        step = min(self.size, 4)
        value = sum([value] + [self.tensor_swap(value, distance) for distance in range(1, step)])
        distance = step
        while distance < self.size:
            value = value + self.tensor_swap(value, distance)
            distance *= 2
        return value

    def shifts(self, stages, block):
        return [
            stages.send(functools.partial(self.shift, distance=distance), block)
            for distance in range(1, self.count)
        ]

    def paired(self, blocks):
        return [jnp.concatenate([part, self.core_swap(part)], axis=0) for part in blocks]

    def gather(self, stages, block):
        return self.paired([block] + self.shifts(stages, block))

    def scatter(self, stages, parts):
        rows = parts[0].shape[0] // 2
        total = None
        for distance in list(range(1, self.count)) + [0]:
            own, other = (parts[distance][:rows], parts[distance][rows:])
            if total is not None:
                other = lax.optimization_barrier((other, leaving))[0]
            self.swapped = self.core_swap(other)
            summed = own.astype(f32) + self.swapped.astype(f32)
            if distance:
                back = functools.partial(self.shift, distance=-distance)
                leaving = summed.astype(bf16)
                summed = stages.send(back, leaving).astype(f32)
            total = summed if total is None else total + summed
        return total


class Stages:
    def __init__(self):
        self.before, self.now = ([], [])

    def send(self, transfer, value):
        if self.before:
            value = lax.optimization_barrier((value, *self.before))[0]
        self.now.append(transfer(value))
        return self.now[-1]

    def next(self):
        self.before, self.now = (self.now, [])


def local(
    boundary,
    seg_ids,
    ln1_gain,
    ln1_bias,
    w_qkv,
    b_qkv,
    w_out,
    b_out,
    ln2_gain,
    ln2_bias,
    w_up,
    b_up,
    w_down,
    b_down,
    prefix_embed,
    reparam_w1,
    reparam_b1,
    reparam_w2,
    reparam_b2,
):
    core = lax.axis_index("section")
    place = lax.axis_index("tensor")
    group = Group(lax.axis_size("tensor"))
    count = group.count
    tok_rows, width = boundary.shape[2:]
    heads_local = w_qkv.shape[2]
    head_dim = w_qkv.shape[3] // 3
    head_width = heads_local * head_dim
    prefix_len = prefix_embed.shape[0]
    row = place // count
    low = core == 0

    def tied(value, *others):
        return lax.optimization_barrier((value,) + others)[0]

    stages = Stages()
    steps = range(1, count)

    own_row = lax.dynamic_index_in_dim(boundary[0], row, 0, False)
    other_row = lax.dynamic_index_in_dim(boundary[0], 1 - row, 0, False)
    came_row = stages.send(functools.partial(group.cross_from, core=0), other_row)
    inputs = jnp.where(low, own_row, came_row).astype(f32)
    proj_own = w_out.reshape(head_width, width)

    def layer_pair(own, far):
        return (jnp.where(low, own, far), jnp.where(low, far, own))


    def as_rows(value):
        value = value.reshape(-1, value.shape[-1])
        return jnp.pad(value, ((0, 0), (0, width - value.shape[1])))

    b_qkv_own = b_qkv.reshape(heads_local, 3, head_dim).transpose(1, 0, 2).reshape(1, 3 * head_width)
    small_parts = (ln1_gain, ln1_bias, b_out, ln2_gain, ln2_bias, b_down, b_up, b_up)
    small_own = jnp.concatenate([as_rows(part) for part in small_parts], axis=0)

    def on_chip(value):
        peer = group.core_swap(value)
        return jnp.stack([jnp.where(low, value, peer), jnp.where(low, peer, value)])

    small_chip = on_chip(small_own)

    def vectors_of(layer):
        return small_chip[layer, :8].astype(f32)

    def normed_one(layer, values):
        vectors = vectors_of(layer)
        return layer_norm(values, vectors[0:1], vectors[1:2]).astype(bf16)

    hidden_width = w_up.shape[2]
    rows = hidden_width // 4
    shared = lax.axis_size("dp") % 2 == 0
    parity = lax.axis_index("dp") % 2
    spot = jnp.stack([core, parity]).astype(jnp.int32)
    keep, give = feed_forward_chunks(tied(spot, other_row), w_up[0], w_down[0])
    handed = group.core_swap(give)
    even_0 = jnp.where(low, keep[0], handed[0])
    later_keep, later_handed, _ = lax.optimization_barrier((keep, handed, even_0))
    even = [even_0, jnp.where(low, later_handed[0], later_keep[0])]
    odd = [
        jnp.where(low, later_keep[1], later_handed[1]),
        jnp.where(low, later_handed[1], later_keep[1]),
    ]

    prefix_pre = dot_nn(tied(prefix_embed, even[0]), reparam_w1) + reparam_b1.astype(f32)
    curve = jnp.tanh(prefix_pre)
    hidden_low = curve.astype(bf16)
    w2_own = (
        tied(reparam_w2, even[0])
        .reshape(reparam_w2.shape[0], heads_local, 2, head_dim)
        .transpose(0, 2, 1, 3)
        .reshape(reparam_w2.shape[0], 2 * head_width)
    )
    b2_own = (
        reparam_b2.reshape(heads_local, 2, head_dim).transpose(1, 0, 2).reshape(2 * head_width)
    )
    prefix_own = (dot_nn(hidden_low, w2_own) + b2_own.astype(f32)).astype(bf16)
    pairs_own = jnp.concatenate(
        [
            jnp.pad(value, ((0, prefix_rows - value.shape[0]), (0, width - value.shape[1])))
            for value in (prefix_own[:, :head_width], prefix_own[:, head_width:], b_qkv_own)
        ],
        axis=0,
    )
    qkv_own = (
        tied(w_qkv, even[0])
        .reshape(width, heads_local, 3, head_dim)
        .transpose(0, 2, 1, 3)
        .reshape(width, 3 * head_width)
    )

    def plane_send(value):
        return stages.send(group.plane_swap, value)

    def half_send(value):
        return stages.send(group.half_swap, value)

    def far(value, layer):
        return stages.send(functools.partial(group.cross_from, core=layer), value)

    side_even_0 = [group.shift(even[0], distance) for distance in steps]
    stages.next()
    normed_0 = tied(normed_one(0, inputs), *side_even_0)
    gathered_0 = [normed_0] + group.shifts(stages, normed_0)
    stages.now += side_even_0
    side_bias = small_chip[:, 6, : w_up.shape[2]]
    side_bias = jnp.stack([side_bias] + group.shifts(stages, side_bias), axis=1)
    qkv_far = stages.send(group.cross, qkv_own)

    stages.next()
    pairs = layer_pair(pairs_own, stages.send(group.cross, pairs_own))
    proj_far_0 = far(proj_own, 0)
    half_even_0 = half_send(even[0])
    side_even_1 = group.shifts(stages, even[1])
    if shared:
        side_odd_0 = [plane_send(value) for value in side_even_0]
    else:
        side_odd_0 = group.shifts(stages, odd[0])

    def all_chunks(layer, half, side, corner):
        chunks = [even[layer], odd[layer], *half]
        for at in range(count - 1):
            chunks += [side[0][at], side[1][at], corner[0][at], corner[1][at]]
        return chunks

    seg_row = lax.dynamic_index_in_dim(seg_ids, row, 0, True).astype(f32)
    chip = place % count
    orders = [
        jnp.stack(
            [
                jnp.bitwise_xor(row, jnp.bitwise_xor(core, swapped ^ layer)) * count
                + (chip - distance + count) % count
                for distance in range(count)
                for swapped in range(2)
            ]
        ).astype(jnp.int32)
        for layer in range(2)
    ]

    class Layer:
        def __init__(self, index, qkv):
            self.vectors = vectors_of(index)
            self.ln1_gain, self.ln1_bias, self.b_out = [self.vectors[at : at + 1] for at in range(3)]
            shard = pairs[index]
            self.pairs = shard[: 2 * prefix_rows, :head_width].reshape(2, prefix_rows, head_width)
            self.b_qkv = shard[2 * prefix_rows : 2 * prefix_rows + 1, : 3 * head_width].astype(f32)
            self.order = orders[index]
            self.qkv = tied(qkv, *stages.before)

        def attention(self, inputs, gathered):
            self.inputs = inputs
            gathered = lax.optimization_barrier((*gathered, *stages.before))[:count]
            self.packed = [
                (dot_nn(part, self.qkv) + self.b_qkv).astype(bf16)
                for part in group.paired(gathered)
            ]
            self.context, self.lse = attention_forward(
                self.order, self.packed, self.pairs, seg_row, head_dim, prefix_len
            )

        def project(self):
            context = lax.optimization_barrier((*self.context, *stages.before))[:count]
            own, far_own = lax.optimization_barrier((*self.far_out, *self.context))[:2]
            self.out = jnp.where(low, own, far_own)
            parts = [dot_nn(part, self.out).astype(bf16) for part in context]
            self.middle = self.inputs + (group.scatter(stages, parts) + self.b_out)

        def project_here(self):
            context = lax.optimization_barrier((*self.context, *stages.before))[:count]
            branch = dot_nn(context[0], self.out)
            for distance in steps:
                came = group.shift(context[distance], -distance)
                branch = branch + dot_nn(came, self.out_side[distance - 1])
            rows = branch.shape[0] // 2
            own, peer = (branch[:rows], branch[rows:].astype(bf16))
            self.middle = self.inputs + (self.shared((own, peer)) + self.b_out)

        def norm_two(self, values):
            return layer_norm(values, self.vectors[3:4], self.vectors[4:5]).astype(bf16)

        def shared(self, *pairs):
            return sum([own + group.core_swap(peer).astype(f32) for own, peer in pairs])

        def output(self, middle, *pairs):
            return (middle + (self.shared(*pairs) + self.vectors[5:6])).astype(bf16)

        def middle_back(self, grad_out, *pairs):
            branch = self.shared(*pairs)
            return grad_out.astype(f32) + norm_back(self.middle, self.vectors[3:4], branch)

        def feed_forward(self, normed, grads, with_output):
            return feed_forward(normed, self.bias, self.chunks, grads, with_output, 2)

        def backward(self, grad_middle):
            stages.before = []
            grad_branch = grad_middle.astype(bf16)
            (grad_chip,) = group.paired([grad_branch])
            sides = [dot_nt(grad_chip, side).astype(bf16) for side in self.out_side]
            came = [group.shift(side, at + 1) for at, side in enumerate(sides)]
            grads = [dot_nt(grad_chip, self.out).astype(bf16)] + came
            grad_packed, grad_pairs = attention_backward(
                self.order, self.packed, grads, self.pairs, seg_row, self.lse, head_dim, prefix_len
            )
            parts = [dot_nt(part, self.qkv).astype(bf16) for part in grad_packed]
            grad_normed = group.scatter(stages, parts)
            grad_in = grad_middle + norm_back(self.inputs, self.ln1_gain, grad_normed)
            return (grad_in.astype(bf16), grad_pairs)

    pack_own = jnp.concatenate([tied(proj_own, qkv_far), other_row], axis=0)
    layer_0 = Layer(0, tied(jnp.where(low, qkv_own, qkv_far), pack_own))
    layer_0.far_out = (proj_own, proj_far_0)
    layer_0.attention(inputs, gathered_0)

    stages.next()
    corner_even_0 = group.shifts(stages, half_even_0)
    half_even_1 = half_send(even[1])
    far_pack = far(pack_own, 1)
    if shared:
        side_odd_1 = [plane_send(value) for value in side_even_1]
    else:
        side_odd_1 = group.shifts(stages, odd[1])
    layer_0.project()

    stages.next()
    half_odd_0 = half_send(odd[0])
    if shared:
        corner_odd_0 = [plane_send(value) for value in corner_even_0]
    else:
        corner_odd_0 = group.shifts(stages, half_odd_0)
    corner_even_1 = group.shifts(stages, half_even_1)
    half_bias = half_send(side_bias)
    up_bias = jnp.stack([side_bias, half_bias], axis=2).astype(f32)
    up_bias = up_bias.reshape(2, 2 * count, 2, 2, rows)
    up_bias = jnp.where(low, up_bias[:, :, 0], up_bias[:, :, 1])
    up_bias = jnp.where(parity == 0, up_bias, up_bias[:, :, ::-1])
    up_bias = up_bias.reshape(2, 4 * count, rows)
    layer_0.bias = up_bias[0]
    layer_0.chunks = all_chunks(
        0,
        (half_even_0, half_odd_0),
        (side_even_0, side_odd_0),
        (corner_even_0, corner_odd_0),
    )
    middle_peer = group.core_swap(layer_0.middle)
    normed_pair = (layer_0.norm_two(layer_0.middle), layer_0.norm_two(middle_peer))

    stages.next()
    own_proj, far_pack = lax.optimization_barrier((proj_own, far_pack, layer_0.middle))[:2]
    cotangent = jnp.where(low, far_pack[head_width:], own_row)
    proj_1 = jnp.where(low, far_pack[:head_width], own_proj)
    stages.before += [*normed_pair, proj_1, cotangent]
    half_odd_1 = half_send(odd[1])
    projs = (layer_0.out, proj_1)
    if shared:
        corner_odd_1 = [plane_send(value) for value in corner_even_1]
    else:
        corner_odd_1 = group.shifts(stages, half_odd_1)
    out_sides = [
        [stages.send(functools.partial(group.shift, distance=-distance), proj) for distance in steps]
        for proj in projs
    ]
    normed_swapped = (tied(normed_pair[1], *stages.before), normed_pair[0])
    out_kept, out_sent = layer_0.feed_forward(normed_swapped, None, True)
    first_out = layer_0.output(middle_peer, (out_kept, tied(out_sent, *stages.now)))
    inputs_1 = first_out.astype(f32)
    normed_1 = normed_one(1, inputs_1)
    gathered_1 = [normed_1] + group.shifts(stages, normed_1)
    w2_far = group.cross(tied(w2_own, first_out))
    layer_1 = Layer(1, jnp.where(low, *lax.optimization_barrier((qkv_far, qkv_own, w2_far))[:2]))
    layer_0.out_side, layer_1.out_side = out_sides
    layer_1.out = proj_1
    layer_1.bias = up_bias[1]
    layer_1.attention(inputs_1, gathered_1)
    layer_1.chunks = all_chunks(
        1,
        (half_even_1, half_odd_1),
        (side_even_1, side_odd_1),
        (corner_even_1, corner_odd_1),
    )

    stages.next()
    w2_side = layer_pair(w2_own, w2_far)
    layer_1.project_here()
    normed = layer_1.norm_two(layer_1.middle)
    normed = (normed, group.core_swap(normed))
    cotangents = (cotangent, group.core_swap(cotangent))
    parts = layer_1.feed_forward(normed, cotangents, True)
    last_out = layer_1.output(layer_1.middle, parts[:2])
    grad_middle = layer_1.middle_back(cotangent, parts[2:])
    mid_grad, grad_pairs_one = layer_1.backward(grad_middle)
    high_other = group.cross_from(last_out, 0)
    mid_grad = tied(mid_grad, high_other)
    mid_peer = group.core_swap(mid_grad)
    back_part = layer_0.feed_forward(normed_pair, (mid_peer, mid_grad), False)
    grad_middle = layer_0.middle_back(mid_peer, back_part)
    first_grad, grad_pairs_zero = layer_0.backward(grad_middle)

    low_other = group.cross_from(first_grad, 1)
    spot = jnp.stack([core, row]).astype(jnp.int32)
    boundary_result = place_rows(spot, first_grad, low_other, last_out, high_other)[None]

    def joined(pairs):
        return jnp.concatenate([pairs[0], pairs[1]], axis=1)

    grads = (joined(grad_pairs_zero), joined(grad_pairs_one))
    hidden_part = sum(
        lax.dot_general(
            grad,
            side.astype(f32),
            (((1,), (1,)), ((), ())),
            precision=lax.Precision.HIGHEST,
            preferred_element_type=f32,
        )
        for grad, side in zip(grads, w2_side)
    )
    kept, sent = layer_pair(*grads)
    message = jnp.concatenate([hidden_part, kept, sent], axis=1)
    summed = tied(message, group.swapped)
    summed = group.sum_planes(summed)
    hidden_width = hidden_part.shape[1]
    kept = summed[:, hidden_width : hidden_width + 2 * head_width]
    came = group.cross(summed[:, hidden_width + 2 * head_width :])
    hidden_grad = group.sum_shards(summed[:, :hidden_width])
    pad = ((0, prefix_rows - prefix_len), (0, 0))
    w2_grad, b2_grad = second_grads(kept, came, jnp.pad(hidden_low, pad), heads_local)
    embed_grad, w1_grad, b1_grad = first_grads(
        hidden_grad, jnp.pad(curve, pad), jnp.pad(prefix_embed, pad), reparam_w1, prefix_len
    )
    return (
        boundary_result,
        embed_grad,
        w1_grad,
        b1_grad.reshape(reparam_b1.shape),
        w2_grad.reshape(reparam_w2.shape),
        b2_grad.reshape(reparam_b2.shape),
    )


def solution(mesh):
    return jax.shard_map(
        local,
        mesh=mesh,
        in_specs=(
            P("section", "dp", "tensor", None),
            P("dp", None),
            P("section", None),
            P("section", None),
            P("section", None, "tensor", None),
            P("section", "tensor", None),
            P("section", "tensor", None, None),
            P("section", None),
            P("section", None),
            P("section", None),
            P("section", None, "tensor"),
            P("section", "tensor"),
            P("section", "tensor", None),
            P("section", None),
            P(),
            P(),
            P(),
            P(None, "section", "tensor", None),
            P("section", "tensor", None),
        ),
        out_specs=(
            P("section", "dp", "tensor", None),
            P(),
            P(),
            P(),
            P(None, "section", "tensor", None),
            P("section", "tensor", None),
        ),
        check_vma=False,
    )
```

```python
import functools

import jax
import jax.numpy as jnp
from jax import lax
from jax.experimental import pallas as pl
from jax.experimental.pallas import tpu as pltpu
from jax.sharding import PartitionSpec as P

epsilon = 1e-05
masked_value = -1e30
max_segment = 512
prefix_rows = 16
stat_rows = 8
f32 = jnp.float32
bf16 = jnp.bfloat16


small_cost = pl.CostEstimate(flops=1, bytes_accessed=1, transcendentals=0)


def dot_nn(a, b):
    return lax.dot_general(a, b, (((1,), (0,)), ((), ())), preferred_element_type=f32)


def dot_nt(a, b):
    return lax.dot_general(a, b, (((1,), (1,)), ((), ())), preferred_element_type=f32)


def key_blocks(index, block_rows):
    reach = -(-(max_segment - 1) // block_rows)
    return list(range(max(0, index - reach), index + 1))


def gather_rows(order_ref, sources, target_ref, block_rows):
    for place in range(2 * len(sources)):
        start = pl.multiple_of(order_ref[place] * block_rows, block_rows)
        target_ref[pl.ds(start, block_rows), :] = sources[place // 2][
            pl.ds((place % 2) * block_rows, block_rows), :
        ]


def scatter_rows(order_ref, source_ref, targets, block_rows, columns):
    for place in range(2 * len(targets)):
        start = pl.multiple_of(order_ref[place] * block_rows, block_rows)
        targets[place // 2][pl.ds((place % 2) * block_rows, block_rows), columns] = source_ref[
            pl.ds(start, block_rows), :
        ].astype(targets[place // 2].dtype)


def segment_column(seg_ref, start, rows):
    row = seg_ref[0:1, start : start + rows]
    return jnp.transpose(jnp.broadcast_to(row, (128, rows)))[:, 0:1]


def attention_forward_kernel(count, block_rows, head_dim, prefix_len, order_ref, *refs):
    packed_refs = refs[:count]
    pairs_ref, seg_ref = refs[count : count + 2]
    context_refs = refs[count + 2 : 2 * count + 2]
    lse_ref, rows_ref, context_ref, bias_ref, vt_ref, pvt_ref, ct_ref = refs[2 * count + 2 :]
    width = pairs_ref.shape[2]
    heads = width // head_dim
    blocks = 2 * count
    scaling = head_dim ** (-0.5)
    gather_rows(order_ref, packed_refs, rows_ref, block_rows)
    lane = lax.broadcasted_iota(jnp.int32, (1, width), 1) // head_dim
    prefix_bias = jnp.where(
        lax.broadcasted_iota(jnp.int32, (pairs_ref.shape[1], 1), 0) < prefix_len, 0.0, masked_value
    )
    prefix_keys = pairs_ref[0]
    pvt_ref[...] = jnp.transpose(pairs_ref[1].astype(f32)).astype(bf16)
    for index in range(blocks):
        vt_ref[index] = jnp.transpose(
            rows_ref[index * block_rows : (index + 1) * block_rows, 2 * width :].astype(f32)
        ).astype(bf16)
    for index in range(blocks):
        start = index * block_rows
        keys = key_blocks(index, block_rows)
        fill_bias(seg_ref, bias_ref, index, keys, block_rows)
        queries = rows_ref[pl.ds(start, block_rows), 0:width]

        def one_head(head, carry):
            query = jnp.where(lane == head, queries, 0.0) * jnp.asarray(scaling, bf16)
            span = pl.ds(pl.multiple_of(head * head_dim, head_dim), head_dim)
            prefix_scores = dot_nt(prefix_keys, query) + prefix_bias
            row_max = jnp.max(prefix_scores, axis=0, keepdims=True)
            scores = []
            for slot, key in enumerate(keys):
                rows = slice(key * block_rows, (key + 1) * block_rows)
                score = dot_nt(rows_ref[rows, width : 2 * width], query) + bias_ref[slot]
                row_max = jnp.maximum(row_max, jnp.max(score, axis=0, keepdims=True))
                scores.append(score)
            prefix_exp = jnp.exp(prefix_scores - row_max)
            row_sum = jnp.sum(prefix_exp, axis=0, keepdims=True)
            context = dot_nn(pvt_ref[span, :], prefix_exp.astype(bf16))
            for score, key in zip(scores, keys):
                exped = jnp.exp(score - row_max)
                row_sum = row_sum + jnp.sum(exped, axis=0, keepdims=True)
                context = context + dot_nn(vt_ref[key, span, :], exped.astype(bf16))
            ct_ref[span, :] = context * (1.0 / row_sum)
            lse_ref[pl.ds(head, 1), start : start + block_rows] = row_max + jnp.log(row_sum)
            return carry

        lax.fori_loop(0, heads, one_head, 0, unroll=True)
        context_ref[pl.ds(start, block_rows), :] = jnp.transpose(ct_ref[...]).astype(bf16)
    scatter_rows(order_ref, context_ref, context_refs, block_rows, slice(0, width))


def fill_bias(seg_ref, bias_ref, index, keys, block_rows):
    seg_query = seg_ref[0:1, index * block_rows : (index + 1) * block_rows]
    for slot, key in enumerate(keys):
        same = segment_column(seg_ref, key * block_rows, block_rows) == seg_query
        if key == index:
            shape = (block_rows, block_rows)
            same = same & (
                lax.broadcasted_iota(jnp.int32, shape, 0)
                <= lax.broadcasted_iota(jnp.int32, shape, 1)
            )
        bias_ref[slot] = jnp.where(same, 0.0, masked_value)


def attention_backward_kernel(count, block_rows, head_dim, prefix_len, order_ref, *refs):
    packed_refs = refs[:count]
    grad_refs = refs[count : 2 * count]
    pairs_ref, seg_ref, lse_ref = refs[2 * count : 2 * count + 3]
    out_refs = refs[2 * count + 3 : 3 * count + 3]
    prefix_out = refs[3 * count + 3]
    rows_ref, grad_ref, bias_ref, kt_ref, pkt_ref, dqt_ref, dq_ref, dk_ref, dv_ref = refs[
        3 * count + 4 :
    ]
    width = pairs_ref.shape[2]
    heads = width // head_dim
    blocks = 2 * count
    scaling = head_dim ** (-0.5)
    gather_rows(order_ref, packed_refs, rows_ref, block_rows)
    gather_rows(order_ref, grad_refs, grad_ref, block_rows)
    lane = lax.broadcasted_iota(jnp.int32, (1, width), 1) // head_dim
    prefix_bias = jnp.where(
        lax.broadcasted_iota(jnp.int32, (pairs_ref.shape[1], 1), 0) < prefix_len, 0.0, masked_value
    )
    prefix_keys, prefix_values = pairs_ref[0], pairs_ref[1]
    pkt_ref[...] = jnp.transpose(prefix_keys.astype(f32)).astype(bf16)
    dk_ref[...] = jnp.zeros_like(dk_ref)
    dv_ref[...] = jnp.zeros_like(dv_ref)
    prefix_out[...] = jnp.zeros_like(prefix_out)
    for index in range(blocks):
        kt_ref[index] = jnp.transpose(
            rows_ref[index * block_rows : (index + 1) * block_rows, width : 2 * width].astype(f32)
        ).astype(bf16)
    for index in range(blocks):
        start = index * block_rows
        keys = key_blocks(index, block_rows)
        fill_bias(seg_ref, bias_ref, index, keys, block_rows)
        queries = rows_ref[pl.ds(start, block_rows), 0:width]
        grads = grad_ref[pl.ds(start, block_rows), :]

        def one_head(head, carry):
            chosen = lane == head
            query = jnp.where(chosen, queries, 0.0) * jnp.asarray(scaling, bf16)
            grad = jnp.where(chosen, grads, 0.0)
            lse = lse_ref[pl.ds(head, 1), start : start + block_rows]
            span = pl.ds(pl.multiple_of(head * head_dim, head_dim), head_dim)
            prefix_prob = jnp.exp(dot_nt(prefix_keys, query) + prefix_bias - lse)
            prefix_dp = dot_nt(prefix_values, grad)
            delta = jnp.sum(prefix_prob * prefix_dp, axis=0, keepdims=True)
            probs, dps = [], []
            for slot, key in enumerate(keys):
                rows = slice(key * block_rows, (key + 1) * block_rows)
                prob = jnp.exp(
                    dot_nt(rows_ref[rows, width : 2 * width], query) + bias_ref[slot] - lse
                )
                dp = dot_nt(rows_ref[rows, 2 * width :], grad)
                delta = delta + jnp.sum(prob * dp, axis=0, keepdims=True)
                probs.append(prob)
                dps.append(dp)
            prefix_ds = (prefix_prob * (prefix_dp - delta)).astype(bf16)
            prefix_out[0] += dot_nn(prefix_ds, query)
            prefix_out[1] += dot_nn(prefix_prob.astype(bf16), grad)
            dqt = dot_nn(pkt_ref[span, :], prefix_ds)
            for prob, dp, key in zip(probs, dps, keys):
                rows = slice(key * block_rows, (key + 1) * block_rows)
                ds = (prob * (dp - delta)).astype(bf16)
                dk_ref[rows, :] += dot_nn(ds, query)
                dv_ref[rows, :] += dot_nn(prob.astype(bf16), grad)
                dqt = dqt + dot_nn(kt_ref[key, span, :], ds)
            dqt_ref[span, :] = dqt
            return carry

        lax.fori_loop(0, heads, one_head, 0, unroll=True)
        dq_ref[pl.ds(start, block_rows), :] = jnp.transpose(dqt_ref[...]) * scaling
    scatter_rows(order_ref, dq_ref, out_refs, block_rows, slice(0, width))
    scatter_rows(order_ref, dk_ref, out_refs, block_rows, slice(width, 2 * width))
    scatter_rows(order_ref, dv_ref, out_refs, block_rows, slice(2 * width, 3 * width))


def gelu_parts(values):
    root = 0.7978845608028654
    square = values * values
    curve = jnp.tanh(root * values * (1.0 + 0.044715 * square))
    return (square, curve, root)


def feed_forward_kernel(groups, per, with_output, with_grad, *refs):
    refs = list(refs)
    normed_own, normed_peer, bias_ref = refs[:3]
    del refs[:3]
    grad_own, grad_peer = (refs.pop(0), refs.pop(0)) if with_grad else (None, None)
    chunk_refs = refs[: per * groups]
    del refs[: per * groups]
    out_own, out_peer = (refs.pop(0), refs.pop(0)) if with_output else (None, None)
    back_own, back_peer = (refs.pop(0), refs.pop(0)) if with_grad else (None, None)
    weight_ref, sems, normed_ref, grad_ref, hidden_ref, back_ref = refs
    tokens, width = normed_own.shape
    hidden = bias_ref.shape[2]
    rows = hidden // per
    block = min(256, width)

    def copies_of(group):
        return [
            pltpu.make_async_copy(
                chunk_refs[per * group + part],
                weight_ref.at[pl.ds((per * group + part) * rows, rows)],
                sems.at[group, part],
            )
            for part in range(per)
        ]

    for group in range(min(2, groups)):
        for copy in copies_of(group):
            copy.start()
    normed_ref[0:tokens, :] = normed_own[...]
    normed_ref[tokens:, :] = normed_peer[...]
    if with_grad:
        grad_ref[0:tokens, :] = grad_own[...]
        grad_ref[tokens:, :] = grad_peer[...]
    @pl.loop(0, groups)
    def _(group):
        for part in range(per):
            pltpu.make_async_copy(
                chunk_refs[0], weight_ref.at[pl.ds(0, rows)], sems.at[group, part]
            ).wait()
        for later in range(2, groups):

            @pl.when(group == later - 2)
            def _():
                for copy in copies_of(later):
                    copy.start()

        span = pl.ds(pl.multiple_of(group * hidden, hidden), hidden)
        pre = dot_nt(normed_ref[...], weight_ref[span, 0:width]) + bias_ref[group]
        square, curve, root = gelu_parts(pre)
        if with_output:
            hidden_ref[group] = (0.5 * pre * (1.0 + curve)).astype(bf16)
        if with_grad:
            slope = 0.5 * (1.0 + curve) + 0.5 * pre * (1.0 - curve * curve) * (
                root * (1.0 + 3 * 0.044715 * square)
            )
            back_ref[group] = (dot_nt(grad_ref[...], weight_ref[span, width:]) * slope).astype(bf16)

    def summed(values_ref, columns):
        return sum(
            dot_nn(values_ref[group], weight_ref[group * hidden : (group + 1) * hidden, columns])
            for group in range(groups)
        )

    for at in range(0, width, block):
        span = slice(at, at + block)
        if with_output:
            total = summed(hidden_ref, slice(width + at, width + at + block))
            out_own[:, span] = total[0:tokens]
            out_peer[:, span] = total[tokens:].astype(bf16)
        if with_grad:
            total = summed(back_ref, span)
            back_own[:, span] = total[0:tokens]
            back_peer[:, span] = total[tokens:].astype(bf16)


def whole(memory_space=pltpu.VMEM):
    return pl.BlockSpec(memory_space=memory_space)


def attention_forward(order, packed, pairs, seg_row, head_dim, prefix_len):
    count = len(packed)
    block_rows = packed[0].shape[0] // 2
    width = packed[0].shape[1] // 3
    seq_len = seg_row.shape[1]
    slots = len(key_blocks(2 * count - 1, block_rows))
    results = pl.pallas_call(
        functools.partial(attention_forward_kernel, count, block_rows, head_dim, prefix_len),
        out_shape=[jax.ShapeDtypeStruct((2 * block_rows, width), bf16)] * count
        + [jax.ShapeDtypeStruct((stat_rows, seq_len), f32)],
        in_specs=[whole(pltpu.SMEM)] + [whole()] * (count + 2),
        out_specs=[whole()] * (count + 1),
        scratch_shapes=[
            pltpu.VMEM((seq_len, 3 * width), bf16),
            pltpu.VMEM((seq_len, width), bf16),
            pltpu.VMEM((slots, block_rows, block_rows), f32),
            pltpu.VMEM((2 * count, width, block_rows), bf16),
            pltpu.VMEM((width, pairs.shape[1]), bf16),
            pltpu.VMEM((width, block_rows), f32),
        ],
        compiler_params=pltpu.CompilerParams(vmem_limit_bytes=32 << 20),
        cost_estimate=small_cost,
        name="attention_forward",
    )(order, *packed, pairs, seg_row)
    return (results[:count], results[count])


def attention_backward(order, packed, grads, pairs, seg_row, lse, head_dim, prefix_len):
    count = len(packed)
    block_rows = packed[0].shape[0] // 2
    width = packed[0].shape[1] // 3
    seq_len = seg_row.shape[1]
    blocks = 2 * count
    slots = len(key_blocks(blocks - 1, block_rows))
    results = pl.pallas_call(
        functools.partial(attention_backward_kernel, count, block_rows, head_dim, prefix_len),
        out_shape=[jax.ShapeDtypeStruct((2 * block_rows, 3 * width), bf16)] * count
        + [jax.ShapeDtypeStruct(pairs.shape, f32)],
        in_specs=[whole(pltpu.SMEM)] + [whole()] * (2 * count + 3),
        out_specs=[whole()] * (count + 1),
        scratch_shapes=[
            pltpu.VMEM((seq_len, 3 * width), bf16),
            pltpu.VMEM((seq_len, width), bf16),
            pltpu.VMEM((slots, block_rows, block_rows), f32),
            pltpu.VMEM((blocks, width, block_rows), bf16),
            pltpu.VMEM((width, pairs.shape[1]), bf16),
            pltpu.VMEM((width, block_rows), f32),
            pltpu.VMEM((seq_len, width), f32),
            pltpu.VMEM((seq_len, width), f32),
            pltpu.VMEM((seq_len, width), f32),
        ],
        compiler_params=pltpu.CompilerParams(vmem_limit_bytes=32 << 20),
        cost_estimate=small_cost,
        name="attention_backward",
    )(order, *packed, *grads, pairs, seg_row, lse)
    return (results[:count], results[count])


def chunk_kernel(place_ref, up_ref, down_ref, keep_ref, give_ref, up, down, chunks, sems, out_sems):
    hidden, width = down.shape
    rows = hidden // 4
    core, parity = place_ref[0], place_ref[1]
    half = width // 2
    loads = []
    for at in range(2):
        span = pl.ds(at * half, half)
        loads.append(pltpu.make_async_copy(up_ref.at[span], up.at[span], sems.at[at]))
    for at in range(2):
        span = pl.ds(at * 2 * rows, 2 * rows)
        loads.append(pltpu.make_async_copy(down_ref.at[span], down.at[span], sems.at[2 + at]))
    for load in loads:
        load.start()
    spots = []
    for side in range(2):
        for which in range(2):
            spots.append(
                (1 - core if side else core, 1 - parity if which else parity, 2 * side + which)
            )
    for at in range(2):
        loads[at].wait()
        span = slice(at * half, (at + 1) * half)
        for side, slot, index in spots:
            chunks[side, slot, :, span] = jnp.transpose(up[span, index * rows : (index + 1) * rows])
    for at in range(2):
        loads[2 + at].wait()
        for side, slot, index in spots[2 * at : 2 * at + 2]:
            chunks[side, slot, :, width:] = down[index * rows : (index + 1) * rows, :]
    stores = [
        pltpu.make_async_copy(chunks.at[side], target, out_sems.at[side])
        for side, target in enumerate((keep_ref, give_ref))
    ]
    for store in stores:
        store.start()
    for store in stores:
        store.wait()


def feed_forward_chunks(place, up, down):
    hidden, width = down.shape
    shape = (2, hidden // 4, 2 * width)
    return pl.pallas_call(
        chunk_kernel,
        out_shape=[jax.ShapeDtypeStruct(shape, bf16)] * 2,
        in_specs=[whole(pltpu.SMEM), whole(pltpu.HBM), whole(pltpu.HBM)],
        out_specs=[whole(pltpu.HBM)] * 2,
        scratch_shapes=[
            pltpu.VMEM((width, hidden), bf16),
            pltpu.VMEM((hidden, width), bf16),
            pltpu.VMEM((2,) + shape, bf16),
            pltpu.SemaphoreType.DMA((4,)),
            pltpu.SemaphoreType.DMA((2,)),
        ],
        compiler_params=pltpu.CompilerParams(vmem_limit_bytes=58 << 20),
        cost_estimate=small_cost,
        name="feed_forward_chunks",
    )(place, up, down)


def feed_forward(normed, bias, chunks, grads, with_output, per):
    rows = chunks[0].shape[0]
    groups, hidden = (len(chunks) // per, per * rows)
    bias = bias.reshape(groups, 1, hidden)
    tokens, width = normed[0].shape
    with_grad = grads is not None
    kinds = with_output + with_grad
    small = (8, 128)
    return pl.pallas_call(
        functools.partial(feed_forward_kernel, groups, per, with_output, with_grad),
        out_shape=[
            jax.ShapeDtypeStruct((tokens, width), f32),
            jax.ShapeDtypeStruct((tokens, width), bf16),
        ]
        * kinds,
        in_specs=[whole()] * (3 + 2 * with_grad) + [whole(pltpu.HBM)] * len(chunks),
        out_specs=[whole()] * (2 * kinds),
        scratch_shapes=[
            pltpu.VMEM((groups * hidden, 2 * width), bf16),
            pltpu.SemaphoreType.DMA((groups, per)),
            pltpu.VMEM((2 * tokens, width), bf16),
            pltpu.VMEM((2 * tokens, width) if with_grad else small, bf16),
            pltpu.VMEM((groups, 2 * tokens, hidden) if with_output else small, bf16),
            pltpu.VMEM((groups, 2 * tokens, hidden) if with_grad else small, bf16),
        ],
        compiler_params=pltpu.CompilerParams(vmem_limit_bytes=58 << 20),
        cost_estimate=small_cost,
        name="feed_forward",
    )(*normed, bias, *(grads if with_grad else ()), *chunks)


def dot_tn(a, b):
    return lax.dot_general(a, b, (((0,), (0,)), ((), ())), preferred_element_type=f32)


def second_grad_kernel(head_dim, kept_ref, came_ref, hidden_ref, w2_ref, b2_ref):
    grad = (kept_ref[...] + came_ref[...]).astype(bf16)
    heads = w2_ref.shape[1]
    for head in range(heads):
        columns = [
            grad[:, (heads * side + head) * head_dim : (heads * side + head + 1) * head_dim]
            for side in range(2)
        ]
        block = jnp.concatenate(columns, axis=1)
        w2_ref[:, head, :] = dot_tn(hidden_ref[...], block)
        b2_ref[head : head + 1, :] = jnp.sum(block.astype(f32), axis=0, keepdims=True)


def second_grads(kept, came, hidden, heads):
    head_dim = kept.shape[1] // (2 * heads)
    return pl.pallas_call(
        functools.partial(second_grad_kernel, head_dim),
        out_shape=[
            jax.ShapeDtypeStruct((hidden.shape[1], heads, 2 * head_dim), f32),
            jax.ShapeDtypeStruct((heads, 2 * head_dim), f32),
        ],
        in_specs=[whole()] * 3,
        out_specs=[whole()] * 2,
        compiler_params=pltpu.CompilerParams(vmem_limit_bytes=8 << 20),
        cost_estimate=small_cost,
        name="second_grads",
    )(kept, came, hidden)


def first_grad_kernel(grad_ref, curve_ref, embed_ref, w1_ref, embed_out, w1_out, b1_out):
    curve = curve_ref[...]
    grad = (grad_ref[...] * (1.0 - curve * curve)).astype(bf16)
    w1_out[...] = dot_tn(embed_ref[...], grad)
    b1_out[...] = jnp.sum(grad.astype(f32), axis=0, keepdims=True)
    embed_out[...] = dot_nt(grad, w1_ref[...])[: embed_out.shape[0]]


def first_grads(grad, curve, embed, w1, prefix_len):
    return pl.pallas_call(
        first_grad_kernel,
        out_shape=[
            jax.ShapeDtypeStruct((prefix_len, embed.shape[1]), f32),
            jax.ShapeDtypeStruct(w1.shape, f32),
            jax.ShapeDtypeStruct((1, w1.shape[1]), f32),
        ],
        in_specs=[whole()] * 4,
        out_specs=[whole()] * 3,
        compiler_params=pltpu.CompilerParams(vmem_limit_bytes=12 << 20),
        cost_estimate=small_cost,
        name="first_grads",
    )(grad, curve, embed, w1)


def place_kernel(spot_ref, low_own, low_other, high_own, high_other, out_ref):
    row = spot_ref[1]

    @pl.when(spot_ref[0] == 0)
    def _():
        out_ref[row] = low_own[...]
        out_ref[1 - row] = low_other[...]

    @pl.when(spot_ref[0] == 1)
    def _():
        out_ref[row] = high_own[...]
        out_ref[1 - row] = high_other[...]


def place_rows(spot, *blocks):
    return pl.pallas_call(
        place_kernel,
        out_shape=jax.ShapeDtypeStruct((2,) + blocks[0].shape, bf16),
        in_specs=[whole(pltpu.SMEM)] + [whole()] * 4,
        out_specs=whole(),
        compiler_params=pltpu.CompilerParams(vmem_limit_bytes=8 << 20),
        cost_estimate=small_cost,
        name="place_rows",
    )(spot, *blocks)


def centered_values(values):
    centered = values - jnp.mean(values, axis=-1, keepdims=True)
    scale = lax.rsqrt(jnp.mean(centered * centered, axis=-1, keepdims=True) + epsilon)
    return (centered * scale, scale)


def layer_norm(values, ln_gain, ln_bias):
    return centered_values(values)[0] * ln_gain + ln_bias


def norm_back(values, ln_gain, grad_normed):
    unit, scale = centered_values(values)
    entry = grad_normed * ln_gain
    return scale * (
        entry
        - jnp.mean(entry, axis=-1, keepdims=True)
        - unit * jnp.mean(entry * unit, axis=-1, keepdims=True)
    )


class Group:
    def __init__(self, tensor_size):
        self.size = tensor_size
        self.count = tensor_size // 2

    def core_swap(self, value):
        return lax.ppermute(value, "section", [(0, 1), (1, 0)])

    def shift(self, value, distance):
        pairs = [
            (half * self.count + place, half * self.count + (place + distance) % self.count)
            for half in range(2)
            for place in range(self.count)
        ]
        return lax.ppermute(value, "tensor", pairs)

    def cross(self, value):
        size, count = self.size, self.count
        pairs = [
            (core * size + place, (1 - core) * size + (place + count) % size)
            for core in range(2)
            for place in range(size)
        ]
        return lax.ppermute(value, ("section", "tensor"), pairs)

    def half_swap(self, value):
        pairs = [(place, (place + self.count) % self.size) for place in range(self.size)]
        return lax.ppermute(value, "tensor", pairs)

    def plane_swap(self, value, distance=1):
        planes = lax.axis_size("dp")
        pairs = [(plane, plane ^ distance) for plane in range(planes)]
        return lax.ppermute(value, "dp", pairs)

    def cross_from(self, value, core):
        size, count = self.size, self.count
        pairs = [
            (core * size + place, (1 - core) * size + (place + count) % size)
            for place in range(size)
        ]
        return lax.ppermute(value, ("section", "tensor"), pairs)

    def sum_planes(self, value):
        planes = lax.axis_size("dp")
        if planes & (planes - 1):
            return lax.psum(value, "dp")
        step = min(planes, 4)
        value = sum([value] + [self.plane_swap(value, distance) for distance in range(1, step)])
        distance = step
        while distance < planes:
            value = value + self.plane_swap(value, distance)
            distance *= 2
        return value

    def tensor_swap(self, value, distance):
        pairs = [(place, place ^ distance) for place in range(self.size)]
        return lax.ppermute(value, "tensor", pairs)

    def sum_shards(self, value):
        if self.size & (self.size - 1):
            return lax.psum(value, ("section", "tensor"))
        value = value + self.core_swap(value)
        step = min(self.size, 4)
        value = sum([value] + [self.tensor_swap(value, distance) for distance in range(1, step)])
        distance = step
        while distance < self.size:
            value = value + self.tensor_swap(value, distance)
            distance *= 2
        return value

    def shifts(self, stages, block):
        return [
            stages.send(functools.partial(self.shift, distance=distance), block)
            for distance in range(1, self.count)
        ]

    def paired(self, blocks):
        return [jnp.concatenate([part, self.core_swap(part)], axis=0) for part in blocks]

    def gather(self, stages, block):
        return self.paired([block] + self.shifts(stages, block))

    def scatter(self, stages, parts):
        rows = parts[0].shape[0] // 2
        total = None
        for distance in list(range(1, self.count)) + [0]:
            own, other = (parts[distance][:rows], parts[distance][rows:])
            if total is not None:
                other = lax.optimization_barrier((other, leaving))[0]
            self.swapped = self.core_swap(other)
            summed = own.astype(f32) + self.swapped.astype(f32)
            if distance:
                back = functools.partial(self.shift, distance=-distance)
                leaving = summed.astype(bf16)
                summed = stages.send(back, leaving).astype(f32)
            total = summed if total is None else total + summed
        return total


class Stages:
    def __init__(self):
        self.before, self.now = ([], [])

    def send(self, transfer, value):
        if self.before:
            value = lax.optimization_barrier((value, *self.before))[0]
        self.now.append(transfer(value))
        return self.now[-1]

    def next(self):
        self.before, self.now = (self.now, [])


def local(
    boundary,
    seg_ids,
    ln1_gain,
    ln1_bias,
    w_qkv,
    b_qkv,
    w_out,
    b_out,
    ln2_gain,
    ln2_bias,
    w_up,
    b_up,
    w_down,
    b_down,
    prefix_embed,
    reparam_w1,
    reparam_b1,
    reparam_w2,
    reparam_b2,
):
    core = lax.axis_index("section")
    place = lax.axis_index("tensor")
    group = Group(lax.axis_size("tensor"))
    count = group.count
    tok_rows, width = boundary.shape[2:]
    heads_local = w_qkv.shape[2]
    head_dim = w_qkv.shape[3] // 3
    head_width = heads_local * head_dim
    prefix_len = prefix_embed.shape[0]
    row = place // count
    low = core == 0

    def tied(value, *others):
        return lax.optimization_barrier((value,) + others)[0]

    stages = Stages()
    steps = range(1, count)

    own_row = lax.dynamic_index_in_dim(boundary[0], row, 0, False)
    other_row = lax.dynamic_index_in_dim(boundary[0], 1 - row, 0, False)
    came_row = stages.send(functools.partial(group.cross_from, core=0), other_row)
    inputs = jnp.where(low, own_row, came_row).astype(f32)
    proj_own = w_out.reshape(head_width, width)

    def layer_pair(own, far):
        return (jnp.where(low, own, far), jnp.where(low, far, own))


    def as_rows(value):
        value = value.reshape(-1, value.shape[-1])
        return jnp.pad(value, ((0, 0), (0, width - value.shape[1])))

    b_qkv_own = b_qkv.reshape(heads_local, 3, head_dim).transpose(1, 0, 2).reshape(1, 3 * head_width)
    small_parts = (ln1_gain, ln1_bias, b_out, ln2_gain, ln2_bias, b_down, b_up, b_up)
    small_own = jnp.concatenate([as_rows(part) for part in small_parts], axis=0)

    def on_chip(value):
        peer = group.core_swap(value)
        return jnp.stack([jnp.where(low, value, peer), jnp.where(low, peer, value)])

    small_chip = on_chip(small_own)

    def vectors_of(layer):
        return small_chip[layer, :8].astype(f32)

    def normed_one(layer, values):
        vectors = vectors_of(layer)
        return layer_norm(values, vectors[0:1], vectors[1:2]).astype(bf16)

    hidden_width = w_up.shape[2]
    rows = hidden_width // 4
    shared = lax.axis_size("dp") % 2 == 0
    parity = lax.axis_index("dp") % 2
    spot = jnp.stack([core, parity]).astype(jnp.int32)
    keep, give = feed_forward_chunks(tied(spot, other_row), w_up[0], w_down[0])
    handed = group.core_swap(give)
    even_0 = jnp.where(low, keep[0], handed[0])
    later_keep, later_handed, _ = lax.optimization_barrier((keep, handed, even_0))
    even = [even_0, jnp.where(low, later_handed[0], later_keep[0])]
    odd = [
        jnp.where(low, later_keep[1], later_handed[1]),
        jnp.where(low, later_handed[1], later_keep[1]),
    ]

    prefix_pre = dot_nn(tied(prefix_embed, even[0]), reparam_w1) + reparam_b1.astype(f32)
    curve = jnp.tanh(prefix_pre)
    hidden_low = curve.astype(bf16)
    w2_own = (
        tied(reparam_w2, even[0])
        .reshape(reparam_w2.shape[0], heads_local, 2, head_dim)
        .transpose(0, 2, 1, 3)
        .reshape(reparam_w2.shape[0], 2 * head_width)
    )
    b2_own = (
        reparam_b2.reshape(heads_local, 2, head_dim).transpose(1, 0, 2).reshape(2 * head_width)
    )
    prefix_own = (dot_nn(hidden_low, w2_own) + b2_own.astype(f32)).astype(bf16)
    pairs_own = jnp.concatenate(
        [
            jnp.pad(value, ((0, prefix_rows - value.shape[0]), (0, width - value.shape[1])))
            for value in (prefix_own[:, :head_width], prefix_own[:, head_width:], b_qkv_own)
        ],
        axis=0,
    )
    qkv_own = (
        tied(w_qkv, even[0])
        .reshape(width, heads_local, 3, head_dim)
        .transpose(0, 2, 1, 3)
        .reshape(width, 3 * head_width)
    )

    def plane_send(value):
        return stages.send(group.plane_swap, value)

    def half_send(value):
        return stages.send(group.half_swap, value)

    def far(value, layer):
        return stages.send(functools.partial(group.cross_from, core=layer), value)

    side_even_0 = [group.shift(even[0], distance) for distance in steps]
    stages.next()
    normed_0 = tied(normed_one(0, inputs), *side_even_0)
    gathered_0 = [normed_0] + group.shifts(stages, normed_0)
    stages.now += side_even_0
    side_bias = small_chip[:, 6, : w_up.shape[2]]
    side_bias = jnp.stack([side_bias] + group.shifts(stages, side_bias), axis=1)
    qkv_far = stages.send(group.cross, qkv_own)
    proj_far_0 = far(proj_own, 0)

    stages.next()
    pairs = layer_pair(pairs_own, stages.send(group.cross, pairs_own))
    half_even_0 = half_send(even[0])
    side_even_1 = group.shifts(stages, even[1])
    if shared:
        side_odd_0 = [plane_send(value) for value in side_even_0]
    else:
        side_odd_0 = group.shifts(stages, odd[0])

    def all_chunks(layer, half, side, corner):
        chunks = [even[layer], odd[layer], *half]
        for at in range(count - 1):
            chunks += [side[0][at], side[1][at], corner[0][at], corner[1][at]]
        return chunks

    seg_row = lax.dynamic_index_in_dim(seg_ids, row, 0, True).astype(f32)
    chip = place % count
    orders = [
        jnp.stack(
            [
                jnp.bitwise_xor(row, jnp.bitwise_xor(core, swapped ^ layer)) * count
                + (chip - distance + count) % count
                for distance in range(count)
                for swapped in range(2)
            ]
        ).astype(jnp.int32)
        for layer in range(2)
    ]

    class Layer:
        def __init__(self, index, qkv):
            self.vectors = vectors_of(index)
            self.ln1_gain, self.ln1_bias, self.b_out = [self.vectors[at : at + 1] for at in range(3)]
            shard = pairs[index]
            self.pairs = shard[: 2 * prefix_rows, :head_width].reshape(2, prefix_rows, head_width)
            self.b_qkv = shard[2 * prefix_rows : 2 * prefix_rows + 1, : 3 * head_width].astype(f32)
            self.order = orders[index]
            self.qkv = tied(qkv, *stages.before)

        def attention(self, inputs, gathered):
            self.inputs = inputs
            gathered = lax.optimization_barrier((*gathered, *stages.before))[:count]
            self.packed = [
                (dot_nn(part, self.qkv) + self.b_qkv).astype(bf16)
                for part in group.paired(gathered)
            ]
            self.context, self.lse = attention_forward(
                self.order, self.packed, self.pairs, seg_row, head_dim, prefix_len
            )

        def project(self):
            context = lax.optimization_barrier((*self.context, *stages.before))[:count]
            own, far_own = lax.optimization_barrier((*self.far_out, *self.context))[:2]
            self.out = jnp.where(low, own, far_own)
            parts = [dot_nn(part, self.out).astype(bf16) for part in context]
            self.middle = self.inputs + (group.scatter(stages, parts) + self.b_out)

        def project_here(self):
            context = lax.optimization_barrier((*self.context, *stages.before))[:count]
            branch = dot_nn(context[0], self.out)
            for distance in steps:
                came = group.shift(context[distance], -distance)
                branch = branch + dot_nn(came, self.out_side[distance - 1])
            rows = branch.shape[0] // 2
            own, peer = (branch[:rows], branch[rows:].astype(bf16))
            self.middle = self.inputs + (self.shared((own, peer)) + self.b_out)

        def norm_two(self, values):
            return layer_norm(values, self.vectors[3:4], self.vectors[4:5]).astype(bf16)

        def shared(self, *pairs):
            return sum([own + group.core_swap(peer).astype(f32) for own, peer in pairs])

        def output(self, middle, *pairs):
            return (middle + (self.shared(*pairs) + self.vectors[5:6])).astype(bf16)

        def middle_back(self, grad_out, *pairs):
            branch = self.shared(*pairs)
            return grad_out.astype(f32) + norm_back(self.middle, self.vectors[3:4], branch)

        def feed_forward(self, normed, grads, with_output):
            return feed_forward(normed, self.bias, self.chunks, grads, with_output, 2)

        def backward(self, grad_middle):
            stages.before = []
            grad_branch = grad_middle.astype(bf16)
            (grad_chip,) = group.paired([grad_branch])
            sides = [dot_nt(grad_chip, side).astype(bf16) for side in self.out_side]
            came = [group.shift(side, at + 1) for at, side in enumerate(sides)]
            grads = [dot_nt(grad_chip, self.out).astype(bf16)] + came
            grad_packed, grad_pairs = attention_backward(
                self.order, self.packed, grads, self.pairs, seg_row, self.lse, head_dim, prefix_len
            )
            parts = [dot_nt(part, self.qkv).astype(bf16) for part in grad_packed]
            grad_normed = group.scatter(stages, parts)
            grad_in = grad_middle + norm_back(self.inputs, self.ln1_gain, grad_normed)
            return (grad_in.astype(bf16), grad_pairs)

    pack_own = jnp.concatenate([tied(proj_own, qkv_far), other_row], axis=0)
    layer_0 = Layer(0, tied(jnp.where(low, qkv_own, qkv_far), pack_own))
    layer_0.far_out = (proj_own, proj_far_0)
    layer_0.attention(inputs, gathered_0)

    stages.next()
    corner_even_0 = group.shifts(stages, half_even_0)
    half_even_1 = half_send(even[1])
    far_pack = far(pack_own, 1)
    if shared:
        side_odd_1 = [plane_send(value) for value in side_even_1]
    else:
        side_odd_1 = group.shifts(stages, odd[1])
    layer_0.project()

    stages.next()
    half_odd_0 = half_send(odd[0])
    if shared:
        corner_odd_0 = [plane_send(value) for value in corner_even_0]
    else:
        corner_odd_0 = group.shifts(stages, half_odd_0)
    corner_even_1 = group.shifts(stages, half_even_1)
    half_bias = half_send(side_bias)
    up_bias = jnp.stack([side_bias, half_bias], axis=2).astype(f32)
    up_bias = up_bias.reshape(2, 2 * count, 2, 2, rows)
    up_bias = jnp.where(low, up_bias[:, :, 0], up_bias[:, :, 1])
    up_bias = jnp.where(parity == 0, up_bias, up_bias[:, :, ::-1])
    up_bias = up_bias.reshape(2, 4 * count, rows)
    layer_0.bias = up_bias[0]
    layer_0.chunks = all_chunks(
        0,
        (half_even_0, half_odd_0),
        (side_even_0, side_odd_0),
        (corner_even_0, corner_odd_0),
    )
    middle_peer = group.core_swap(layer_0.middle)
    normed_pair = (layer_0.norm_two(layer_0.middle), layer_0.norm_two(middle_peer))

    stages.next()
    own_proj, far_pack = lax.optimization_barrier((proj_own, far_pack, layer_0.middle))[:2]
    cotangent = jnp.where(low, far_pack[head_width:], own_row)
    proj_1 = jnp.where(low, far_pack[:head_width], own_proj)
    stages.before += [*normed_pair, proj_1, cotangent]
    half_odd_1 = half_send(odd[1])
    projs = (layer_0.out, proj_1)
    if shared:
        corner_odd_1 = [plane_send(value) for value in corner_even_1]
    else:
        corner_odd_1 = group.shifts(stages, half_odd_1)
    out_sides = [
        [stages.send(functools.partial(group.shift, distance=-distance), proj) for distance in steps]
        for proj in projs
    ]
    normed_swapped = (tied(normed_pair[1], *stages.before), normed_pair[0])
    out_kept, out_sent = layer_0.feed_forward(normed_swapped, None, True)
    first_out = layer_0.output(middle_peer, (out_kept, tied(out_sent, *stages.now)))
    inputs_1 = first_out.astype(f32)
    normed_1 = normed_one(1, inputs_1)
    gathered_1 = [normed_1] + group.shifts(stages, normed_1)
    w2_far = group.cross(tied(w2_own, first_out))
    layer_1 = Layer(1, jnp.where(low, *lax.optimization_barrier((qkv_far, qkv_own, w2_far))[:2]))
    layer_0.out_side, layer_1.out_side = out_sides
    layer_1.out = proj_1
    layer_1.bias = up_bias[1]
    layer_1.attention(inputs_1, gathered_1)
    layer_1.chunks = all_chunks(
        1,
        (half_even_1, half_odd_1),
        (side_even_1, side_odd_1),
        (corner_even_1, corner_odd_1),
    )

    stages.next()
    w2_side = layer_pair(w2_own, w2_far)
    layer_1.project_here()
    normed = layer_1.norm_two(layer_1.middle)
    normed = (normed, group.core_swap(normed))
    cotangents = (cotangent, group.core_swap(cotangent))
    parts = layer_1.feed_forward(normed, cotangents, True)
    last_out = layer_1.output(layer_1.middle, parts[:2])
    grad_middle = layer_1.middle_back(cotangent, parts[2:])
    mid_grad, grad_pairs_one = layer_1.backward(grad_middle)
    high_other = group.cross_from(last_out, 0)
    mid_grad = tied(mid_grad, high_other)
    mid_peer = group.core_swap(mid_grad)
    back_part = layer_0.feed_forward(normed_pair, (mid_peer, mid_grad), False)
    grad_middle = layer_0.middle_back(mid_peer, back_part)
    first_grad, grad_pairs_zero = layer_0.backward(grad_middle)

    low_other = group.cross_from(first_grad, 1)
    spot = jnp.stack([core, row]).astype(jnp.int32)
    boundary_result = place_rows(spot, first_grad, low_other, last_out, high_other)[None]

    def joined(pairs):
        return jnp.concatenate([pairs[0], pairs[1]], axis=1)

    grads = (joined(grad_pairs_zero), joined(grad_pairs_one))
    hidden_part = sum(
        lax.dot_general(
            grad,
            side.astype(f32),
            (((1,), (1,)), ((), ())),
            precision=lax.Precision.HIGHEST,
            preferred_element_type=f32,
        )
        for grad, side in zip(grads, w2_side)
    )
    kept, sent = layer_pair(*grads)
    message = jnp.concatenate([hidden_part, kept, sent], axis=1)
    summed = tied(message, group.swapped)
    summed = group.sum_planes(summed)
    hidden_width = hidden_part.shape[1]
    kept = summed[:, hidden_width : hidden_width + 2 * head_width]
    came = group.cross(summed[:, hidden_width + 2 * head_width :])
    hidden_grad = group.sum_shards(summed[:, :hidden_width])
    pad = ((0, prefix_rows - prefix_len), (0, 0))
    w2_grad, b2_grad = second_grads(kept, came, jnp.pad(hidden_low, pad), heads_local)
    embed_grad, w1_grad, b1_grad = first_grads(
        hidden_grad, jnp.pad(curve, pad), jnp.pad(prefix_embed, pad), reparam_w1, prefix_len
    )
    return (
        boundary_result,
        embed_grad,
        w1_grad,
        b1_grad.reshape(reparam_b1.shape),
        w2_grad.reshape(reparam_w2.shape),
        b2_grad.reshape(reparam_b2.shape),
    )


def solution(mesh):
    return jax.shard_map(
        local,
        mesh=mesh,
        in_specs=(
            P("section", "dp", "tensor", None),
            P("dp", None),
            P("section", None),
            P("section", None),
            P("section", None, "tensor", None),
            P("section", "tensor", None),
            P("section", "tensor", None, None),
            P("section", None),
            P("section", None),
            P("section", None),
            P("section", None, "tensor"),
            P("section", "tensor"),
            P("section", "tensor", None),
            P("section", None),
            P(),
            P(),
            P(),
            P(None, "section", "tensor", None),
            P("section", "tensor", None),
        ),
        out_specs=(
            P("section", "dp", "tensor", None),
            P(),
            P(),
            P(),
            P(None, "section", "tensor", None),
            P("section", "tensor", None),
        ),
        check_vma=False,
    )
```
